128 devices in a mesh: base: 16 (over z, y), freq: 8 (over x, core).
Axes of the slice: x: 4, y: 4, z: 4, core: 2. Of those that a mesh axis runs over, the one named last changes fastest.
Arguments:
- visibilities: bfloat16 [2, 16384, 2048], P(None, 'base', 'freq'), may hold values from -0.01171875 to 0.01171875
- anchor: bfloat16 [2, 16384], P(None, 'base'), may hold values from 4 to 60, as said below
- drift: bfloat16 [2, 16384], P(None, 'base'), may hold values from -0.01953125 to 0.01953125
- target: int32 [16384, 1], P('base'), may hold values from 0 to 127; in each aligned block of 1024 rows (0 to 1023, 1024 to 2047, ...) at most 8 rows name the same one
- subgrid_w: float32 [128], P('base'), may hold values from -1 to 1
- facet_owner: int32 [128, 1], P('base'), may hold values from 0 to 15; in each aligned block of 8 rows (0 to 7, 8 to 15, ...) at most 2 rows name the same one
- row_offset: int32 [128], P('base'), may hold values from 0 to 64
- col_offset: int32 [128], P('base'), may hold values from 0 to 16320
Outputs:
- grid: float32 [2, 2048, 16384], P(None, 'base')
The draws below stay inside these ranges and needn't reach their ends.
Inputs may be any that keep to these rules, and one draw needn't show every extreme that they name: `target`: among the 1024 blocks of one index of base no subgrid is named more than 8 times. `facet_owner`: among the 8 subgrids of one index of base no owner is named more than 2 times. anchor[k,b] + 2048 drift[k,b] lies between 4 and 60, up to the rounding of drift.
All inputs are finite; a program needn't handle non-finite values.
Results may differ from the reference program's by a relative error of at most 0.0038.
Values may be sent and summed in bfloat16 or wider, within the bound.
A program may use at most 128 MiB of HBM per device.

```python
import math
from functools import partial
import jax
import jax.numpy as jnp
import numpy as np
from jax import lax

G = 64
GY = 16384
CAP = 8
FCAP = 2
NB = 1024
SG_DEV = 8
FR = 128
CHANNELS = 2048
BLOCKS = 16384
SUBGRIDS = 128
GX = 2048
SLOT_VIS = 262144
N_BASE = 16


def track_pair(key):
    reach = 5.0 * G / (8.0 * CHANNELS)
    keys = jax.random.split(jax.random.fold_in(key, 7331), 3)
    lowest = 0.7
    sizes = jax.random.uniform(keys[0], (2, BLOCKS), jnp.float32, lowest, 1.0)
    signs = jnp.where(jax.random.bernoulli(keys[1], 0.5, (2, BLOCKS)), 1.0, -1.0).astype(jnp.float32)
    slope = sizes * signs * reach
    span = slope * float(CHANNELS)
    lower = G / 16.0 - jnp.minimum(span, 0.0)
    upper = 15.0 * G / 16.0 - jnp.maximum(span, 0.0)
    spread = jax.random.uniform(keys[2], (2, BLOCKS), jnp.float32, 0.0, 1.0)
    start = lower + spread * (upper - lower)
    return (start, slope)


def draw_anchor(key, part):
    start, slope = track_pair(key)
    return start.astype(jnp.bfloat16)


def draw_drift(key, part):
    start, slope = track_pair(key)
    return slope.astype(jnp.bfloat16)


def place_ends(drawn, own_key, least, largest):
    dims = drawn.shape
    spot = [jax.random.randint(jax.random.fold_in(own_key, axis), (), 0, dims[axis]) for axis in range(len(dims))]
    drawn = drawn.at[tuple(spot)].set(least)
    longest = dims.index(max(dims))
    spot[longest] = (spot[longest] + 1) % dims[longest]
    return drawn.at[tuple(spot)].set(largest)


def block_scale(rng, extent, pieces, least, high):
    def one(dim, parts):
        draws = jax.random.uniform(jax.random.fold_in(jax.random.fold_in(rng, 6), dim), (parts,), jnp.float32, least / len(pieces), high / len(pieces))
        return jnp.repeat(jnp.exp(draws), extent[dim] // parts).reshape((-1,) + (1,) * (len(extent) - dim - 1))

    gain = one(*pieces[0])
    for cut in pieces[1:]:
        gain = gain * one(*cut)
    return gain


def routed_block(stream_key, own, number, rows, amount, top, most, skew):
    sequence = jax.random.permutation(stream_key, amount)
    crowded, common = shares(amount, rows * top, most, skew, True), shares(amount, rows * top, most, skew, False)
    places = jnp.arange(amount)

    def named(lengths, turn):
        used = int((lengths > 0).sum())
        fixed = max(1, used // 4)
        shifted = fixed + (places - fixed + turn * (used - fixed)) % max(1, amount - fixed)
        return jnp.zeros((amount,), jnp.int32).at[sequence[jnp.where(places < fixed, places, shifted)]].set(jnp.asarray(lengths, jnp.int32))

    lengths = jnp.where(number % 4 == 0, named(crowded, number // 4), named(common, number - number // 4 - 1))
    mixed = jax.random.permutation(jax.random.fold_in(own, 3), amount)
    giver, sink = mixed[0:amount // 2 * 2:2], mixed[1:amount // 2 * 2:2]
    margin = jnp.minimum(lengths[giver] - 1, most - lengths[sink]) // 2
    margin = jnp.where((giver == sequence[0]) | (sink == sequence[0]) | (lengths[sink] == 0), 0, jnp.maximum(margin, 0))
    shifted = jax.random.randint(jax.random.fold_in(own, 4), (amount // 2,), 0, 1 << 20) % (margin + 1)
    lengths = lengths.at[giver].add(-shifted).at[sink].add(shifted)
    members = jnp.searchsorted(jnp.cumsum(lengths), jnp.arange(rows * top), side="right").astype(jnp.int32)
    listing = members.reshape(top, rows).T
    listing = listing[jax.random.permutation(jax.random.fold_in(own, 1), rows)]
    turn = jax.random.randint(jax.random.fold_in(own, 2), (rows, 1), 0, top)
    return jnp.take_along_axis(listing, (jnp.arange(top)[None, :] + turn) % top, axis=1)


def shares(amount, total, most, lean, full):
    weights = [(1 << 20) // math.isqrt(standing ** lean) + 1 for standing in range(1, amount + 1)]
    largest = most if full else min(most, max(-(-total // amount), total * weights[0] // sum(weights)))
    least = 1 if total - largest >= amount - 1 else 0
    holding, surplus = [largest] + [least] * (amount - 1), total - largest - least * (amount - 1)
    while surplus > 0:
        movable = [i for i in range(1, amount) if holding[i] < largest] or [i for i in range(1, amount) if holding[i] < most]
        whole, remaining = sum([weights[i] for i in movable]), surplus
        for i in movable:
            addition = min(most - holding[i], max(1, remaining * weights[i] // whole), surplus)
            holding[i] = holding[i] + addition
            surplus = surplus - addition
    return np.array(holding)


def centred(key, shape, scale, most, shards=(), kind=jnp.bfloat16):
    array = jax.random.normal(key, shape, jnp.float32) * scale
    if len(shards) > 0:
        array = block_scale(key, shape, shards, -0.22, 0.18) * array
    return jnp.clip(array, min=-most, max=most).astype(kind)


def setup_inputs(seed: int = 0) -> dict:
    key_list = jax.random.split(jax.random.key(seed), 9)
    visibilities = centred(key_list[0], (2, BLOCKS, CHANNELS), (SLOT_VIS ** -0.5), 0.01171875, ((1, 16), (2, 8)))
    anchor = draw_anchor(jax.random.fold_in(key_list[8], 71), 0)
    drift = draw_drift(jax.random.fold_in(key_list[8], 71), 0)
    target_keys = jax.random.split(jax.random.fold_in(key_list[3], 1), BLOCKS // NB)
    target_turns = jax.random.permutation(jax.random.fold_in(key_list[3], 3), BLOCKS // NB)
    target = jax.vmap(lambda own, number: routed_block(jax.random.fold_in(key_list[3], 2), own, number, NB, SUBGRIDS, 1, CAP, 2))(target_keys, target_turns).reshape((BLOCKS, 1))
    subgrid_w = jnp.clip(jax.random.uniform(key_list[4], (SUBGRIDS,), jnp.float32, -1.0, 1.0) * block_scale(key_list[4], (SUBGRIDS,), ((0, 16),), -0.4, 0.0), -1.0, 1.0)
    facet_owner_keys = jax.random.split(jax.random.fold_in(key_list[5], 1), SUBGRIDS // SG_DEV)
    facet_owner_turns = jax.random.permutation(jax.random.fold_in(key_list[5], 3), SUBGRIDS // SG_DEV)
    facet_owner = jax.vmap(lambda own, number: routed_block(jax.random.fold_in(key_list[5], 2), own, number, SG_DEV, N_BASE, 1, FCAP, 2))(facet_owner_keys, facet_owner_turns).reshape((SUBGRIDS, 1))
    row_offset = place_ends(jax.random.randint(key_list[6], (SUBGRIDS,), 0, FR - G + 1), jax.random.fold_in(key_list[6], 1), 0, FR - G).astype(jnp.int32)
    col_offset = place_ends(jax.random.randint(key_list[7], (SUBGRIDS,), 0, GY - G + 1), jax.random.fold_in(key_list[7], 1), 0, GY - G).astype(jnp.int32)
    return {"visibilities": visibilities, "anchor": anchor, "drift": drift, "target": target, "subgrid_w": subgrid_w, "facet_owner": facet_owner, "row_offset": row_offset, "col_offset": col_offset}


def slot_table(target, groups, depth):
    total = target.shape[0]
    hits = (target[:, None] == jnp.arange(groups, dtype=jnp.int32)[None, :]).astype(jnp.int32)
    before = jnp.cumsum(hits, axis=0) - hits
    ranking = jnp.sum(before * hits, axis=1)
    placed = target * depth + ranking
    match = placed[None, :] == jnp.arange(groups * depth, dtype=jnp.int32)[:, None]
    source = jnp.sum(jnp.where(match, jnp.arange(total, dtype=jnp.int32)[None, :], 0), axis=1).astype(jnp.int32)
    filled = jnp.any(match, axis=1)
    return source, filled


def phase_table(start, slope, first, channels):
    pixels = (jnp.arange(G, dtype=jnp.int32) - G // 2).astype(jnp.float32) * (2.0 * math.pi / G)
    angles = jnp.concatenate([pixels, pixels])
    shifts = jnp.concatenate([jnp.zeros((G,), jnp.float32), jnp.full((G,), -0.5 * math.pi, jnp.float32)])
    coarse = (first + 16 * jnp.arange(channels // 16, dtype=jnp.int32)).astype(jnp.float32)
    fine = jnp.arange(16, dtype=jnp.int32).astype(jnp.float32)
    centre = (start[:, None] + coarse[None, :] * slope[:, None]) - 0.5 * G
    outer = centre[:, :, None] * angles + shifts
    inner = (fine[None, :] * slope[:, None])[:, :, None] * angles
    table = jnp.cos(outer)[:, :, None, :] * jnp.cos(inner)[:, None, :, :] - jnp.sin(outer)[:, :, None, :] * jnp.sin(inner)[:, None, :, :]
    return table.reshape(start.shape[0], channels, 2 * G)


def grid_one(data, where, first):
    bound = data.shape[1]
    channels = data.shape[2]
    values = where.astype(jnp.float32)
    left = phase_table(values[0], values[2], first, channels).astype(jnp.bfloat16).reshape(bound * channels, 2 * G)
    right = phase_table(values[1], values[3], first, channels)
    signs = jnp.concatenate([-jnp.ones((G,), jnp.float32), jnp.ones((G,), jnp.float32)])
    swapped = jnp.roll(right, G, axis=2) * signs
    real_part = data[0].astype(jnp.float32)[:, :, None]
    imag_part = data[1].astype(jnp.float32)[:, :, None]
    weighted = (real_part * right + imag_part * swapped).astype(jnp.bfloat16).reshape(bound * channels, 2 * G)
    product = lax.dot_general(left.astype(jnp.float32), weighted.astype(jnp.float32), (((0,), (0,)), ((), ())),
                              precision=lax.Precision.HIGHEST, preferred_element_type=jnp.float32)
    return jnp.stack([product[:G, :G] - product[G:, G:], product[:G, G:] + product[G:, :G]])


def to_patch(image, weight):
    axis_values = (jnp.arange(G, dtype=jnp.int32) - G // 2).astype(jnp.float32) / (0.5 * G)
    radius = axis_values[:, None] ** 2 + axis_values[None, :] ** 2
    phase = math.pi * weight[:, None, None] * radius
    cosine, sine = jnp.cos(phase), jnp.sin(phase)
    kernel_real = image[:, 0] * cosine - image[:, 1] * sine
    kernel_imag = image[:, 0] * sine + image[:, 1] * cosine
    index = jnp.arange(G, dtype=jnp.int32)
    turns = ((index[:, None] * index[None, :]) % G).astype(jnp.float32) * (2.0 * math.pi / G)
    table_real, table_imag = jnp.cos(turns), -jnp.sin(turns)
    highest = lax.Precision.HIGHEST

    def from_left(matrix, field):
        return jnp.einsum('jl,slm->sjm', matrix, field, precision=highest)

    def from_right(field, matrix):
        return jnp.einsum('sjm,km->sjk', field, matrix, precision=highest)

    turned_real = from_left(table_real, kernel_real) - from_left(table_imag, kernel_imag)
    turned_imag = from_left(table_real, kernel_imag) + from_left(table_imag, kernel_real)
    patch_real = from_right(turned_real, table_real) - from_right(turned_imag, table_imag)
    patch_imag = from_right(turned_real, table_imag) + from_right(turned_imag, table_real)
    return jnp.stack([patch_real, patch_imag], axis=1) * (1.0 / G)


def reference(visibilities, anchor, drift, target, subgrid_w, facet_owner, row_offset, col_offset):
    places = jnp.concatenate([anchor, drift], axis=0)
    source, filled = jax.vmap(partial(slot_table, groups=SUBGRIDS, depth=CAP))(target[:, 0].reshape(N_BASE, NB))
    shifts = NB * jnp.arange(N_BASE, dtype=jnp.int32)
    chosen = (source + shifts[:, None]).reshape(N_BASE, SUBGRIDS, CAP).transpose(1, 0, 2).reshape(SUBGRIDS, N_BASE * CAP)
    usable = filled.reshape(N_BASE, SUBGRIDS, CAP).transpose(1, 0, 2).reshape(SUBGRIDS, N_BASE * CAP)

    def single(item):
        picks, keeps = item
        data = jnp.where(keeps[None, :, None], jnp.take(visibilities, picks, axis=1), jnp.zeros((), visibilities.dtype))
        where = jnp.where(keeps[None, :], jnp.take(places, picks, axis=1), jnp.zeros((), places.dtype))
        return grid_one(data, where, 0)

    images = lax.map(single, (chosen, usable))
    patches = to_patch(images, subgrid_w)
    rows = facet_owner[:, 0] * FR + row_offset

    def deposit(grid, item):
        patch, row, column = item
        start = (jnp.zeros((), jnp.int32), row.astype(jnp.int32), column.astype(jnp.int32))
        region = lax.dynamic_slice(grid, start, (2, G, G))
        return lax.dynamic_update_slice(grid, region + patch, start), None

    grid, _ = lax.scan(deposit, jnp.zeros((2, GX, GY), jnp.float32), (patches, rows, col_offset))
    return grid
```

```python
import functools
import math

import jax
import jax.numpy as jnp
import numpy as np
from jax import lax
from jax.experimental import pallas as pl
from jax.experimental.pallas import tpu as pltpu
from jax.sharding import PartitionSpec as P

G = 64
GY = 16384
CAP = 8
FCAP = 2
FR = 128
NT = (((1,), (1,)), ((), ()))
F32 = jnp.float32
BF16 = jnp.bfloat16
VMEM = pltpu.MemorySpace.VMEM
SMEM = pltpu.MemorySpace.SMEM


def vmem():
    return pl.BlockSpec(memory_space=VMEM)


def smem():
    return pl.BlockSpec(memory_space=SMEM)


def prep_kernel(target_ref, vis_ref, anchor_ref, drift_ref, vr_ref, vi_ref, co_ref):
    blocks = target_ref.shape[1]
    groups = blocks // CAP
    target = target_ref[...]
    hits = (lax.broadcasted_iota(jnp.int32, (groups, blocks), 0) == target).astype(F32)
    earlier = lax.broadcasted_iota(jnp.int32, (blocks, blocks), 0) < lax.broadcasted_iota(
        jnp.int32, (blocks, blocks), 1
    )
    before = jnp.dot(hits.astype(BF16), earlier.astype(F32).astype(BF16), preferred_element_type=F32)
    ranking = jnp.sum(before * hits, axis=0, keepdims=True)
    placed = target * CAP + ranking.astype(jnp.int32)
    step = 128

    def chunk(i, carry):
        start = pl.multiple_of(i * step, step)
        rows = pl.ds(start, step)
        match = lax.broadcasted_iota(jnp.int32, (step, blocks), 0) + start == placed
        pick = match.astype(F32).astype(BF16)
        vr_ref[rows, :] = jnp.dot(pick, vis_ref[0], preferred_element_type=F32)
        vi_ref[rows, :] = jnp.dot(pick, vis_ref[1], preferred_element_type=F32)
        co_ref[rows, 0:2] = lax.dot_general(pick, anchor_ref[...], NT, preferred_element_type=F32)
        co_ref[rows, 2:4] = lax.dot_general(pick, drift_ref[...], NT, preferred_element_type=F32)
        return carry

    lax.fori_loop(0, blocks // step, chunk, 0)


def prep(target, visibilities, anchor, drift):
    _, blocks, channels = visibilities.shape
    return pl.pallas_call(
        prep_kernel,
        out_shape=(
            jax.ShapeDtypeStruct((blocks, channels), F32),
            jax.ShapeDtypeStruct((blocks, channels), F32),
            jax.ShapeDtypeStruct((blocks, 4), F32),
        ),
        in_specs=[vmem()] * 4,
        out_specs=(vmem(), vmem(), vmem()),
        compiler_params=pltpu.CompilerParams(vmem_limit_bytes=48 << 20),
        name="prep",
    )(target.reshape(1, blocks), visibilities, anchor, drift)


def trig(h):
    z = h * h
    s = 1 / 362880 + z * (-1 / 39916800)
    s = h * (1.0 + z * (-1 / 6 + z * (1 / 120 + z * (-1 / 5040 + z * s))))
    c = -1 / 3628800 + z * (1 / 479001600)
    c = 1.0 + z * (-0.5 + z * (1 / 24 + z * (-1 / 720 + z * (1 / 40320 + z * c))))
    return c, s


HALF = 152


def put(tab, row, v):
    tab[row : row + 8, :] = v[:, :128]
    tab[HALF + row : HALF + row + 8, :] = v[:, 128:]


def base_rows(h, tab):
    c0, s0 = trig(h)
    k1 = 4.0 * c0 * c0 - 2.0
    k2 = k1 * k1 - 2.0
    k4 = k2 * k2 - 2.0
    k8 = k4 * k4 - 2.0
    s8 = (2.0 * s0 * c0) * k1 * k2 * k4
    cp, cc = c0, (k1 - 1.0) * c0
    sp, sc = s0, (k1 + 1.0) * s0
    put(tab, 0, c0)
    put(tab, 64, s0)
    for p in range(1, 8):
        put(tab, 8 * p, cc)
        put(tab, 64 + 8 * p, sc)
        cp, cc = cc, k1 * cc - cp
        sp, sc = sc, k1 * sc - sp
    put(tab, 128, k8)
    put(tab, 136, 0.5 * k8)
    put(tab, 144, s8)
    return c0, s0


def expand(tab, s, h):
    o = HALF * h
    k8 = tab[o + 128 + s : o + 129 + s, :]
    c8 = tab[o + 136 + s : o + 137 + s, :]
    s8 = tab[o + 144 + s : o + 145 + s, :]
    a0 = tab[pl.ds(o + s, 8, stride=8), :]
    b0 = tab[pl.ds(o + 64 + s, 8, stride=8), :]
    a1 = c8 * a0 - s8 * b0
    b1 = c8 * b0 + s8 * a0
    a2 = k8 * a1 - a0
    b2 = k8 * b1 - b0
    a3 = k8 * a2 - a1
    b3 = k8 * b2 - b1
    return jnp.concatenate([a0, a1, a2, a3, b0, b1, b2, b3], axis=0)


def one_subgrid(g, chan, vr_ref, vi_ref, co_ref, tx, ty, tv):
    rows = pl.ds(pl.multiple_of(8 * g, 8), 8)
    co = co_ref[rows, :]
    hx = (co[:, 0:1] - 0.5 * G + chan * co[:, 2:3]) * (math.pi / G)
    hy = (co[:, 1:2] - 0.5 * G + chan * co[:, 3:4]) * (math.pi / G)
    cx, sx = base_rows(hx, tx)
    cy, sy = base_rows(hy, ty)
    er = cx * cy - sx * sy
    ei = cx * sy + sx * cy
    vr = vr_ref[rows, :]
    vi = vi_ref[rows, :]
    tv[0:8, :] = vr * er + vi * ei
    tv[8:16, :] = vi * er - vr * ei
    acc = None
    for s in range(8):
        f = jnp.concatenate([expand(tx, s, h).astype(BF16) for h in (0, 1)], axis=1)
        parts = []
        for h in (0, 1):
            g0 = expand(ty, s, h)
            cut = slice(128 * h, 128 * h + 128)
            both = [g0 * tv[s : s + 1, cut], g0 * tv[8 + s : 9 + s, cut]]
            parts.append(jnp.concatenate(both, axis=0).astype(BF16))
        r = jnp.concatenate(parts, axis=1)
        d = lax.dot_general(f, r, NT, preferred_element_type=F32)
        acc = d if acc is None else acc + d
    return acc


def grid_kernel(first_ref, vr_ref, vi_ref, co_ref, out_ref, tx, ty, tv):
    chan = (lax.broadcasted_iota(jnp.int32, (8, 256), 1) + first_ref[0]).astype(F32)

    def body(g, carry):
        out_ref[g] = one_subgrid(g, chan, vr_ref, vi_ref, co_ref, tx, ty, tv)
        return carry

    lax.fori_loop(0, out_ref.shape[0], body, 0)


def grid_all(first, vr, vi, co):
    return pl.pallas_call(
        grid_kernel,
        out_shape=jax.ShapeDtypeStruct((vr.shape[0] // CAP, G, 2 * G), F32),
        in_specs=[smem()] + [vmem()] * 3,
        out_specs=vmem(),
        scratch_shapes=[
            pltpu.VMEM((2 * HALF, 128), F32),
            pltpu.VMEM((2 * HALF, 128), F32),
            pltpu.VMEM((16, 256), F32),
        ],
        compiler_params=pltpu.CompilerParams(vmem_limit_bytes=48 << 20),
        name="gridding",
    )(first, vr, vi, co)


def constants():
    l = np.arange(G) - G // 2 + 0.5
    p = np.arange(G // 2) + 0.5
    same = (np.abs(l)[:, None] == p[None, :]).astype(np.float64)
    a = np.concatenate([same, 0 * same], axis=1)
    b = np.concatenate([0 * same, same * np.sign(l)[:, None]], axis=1)
    turns = 2 * np.pi * ((np.arange(G)[:, None] * np.arange(G)[None, :]) % G) / G
    fr, fi = np.cos(turns), -np.sin(turns)
    left1 = np.concatenate([a, b], axis=0)
    right1 = np.block([[a.T, b.T], [-b.T, a.T]])
    left2 = np.concatenate([fr, fi], axis=0)
    right2 = np.block([[fr, fi], [-fi, fr]]) / G
    return [x.astype(np.float32) for x in (left1, right1, left2, right2)]


def dot32(a, b):
    return jnp.dot(a, b, precision=lax.Precision.HIGHEST, preferred_element_type=F32)


def make_patch(m, w, left1, right1, left2, right2):
    lane = lax.broadcasted_iota(jnp.int32, (G, 2 * G), 1)
    sign = jnp.where(lane < G, -1.0, 1.0).astype(F32)
    row = lax.broadcasted_iota(jnp.int32, (G, 2 * G), 0)
    xl = (row - G // 2).astype(F32) * (2.0 / G)
    xm = (lane % G - G // 2).astype(F32) * (2.0 / G)
    c, s = trig((0.25 * math.pi) * w * (xl * xl + xm * xm))
    for _ in range(2):
        c, s = 2.0 * c * c - 1.0, 2.0 * c * s
    both = dot32(left1, m)
    y = both[:G] + sign * jnp.roll(both[G:], G, axis=1)
    z = dot32(y, right1)
    k = z * c + jnp.roll(z, G, axis=1) * (s * sign)
    both = dot32(left2, k)
    y = both[:G] + sign * jnp.roll(both[G:], G, axis=1)
    return dot32(y, right2)


def deposit_kernel(me_ref, owner_ref, row_ref, col_ref, slot_ref, out_ref, acc, sem):
    me = me_ref[0]
    zeros = jnp.zeros((8, 2048), F32)

    def clear(i, carry):
        q = i // (FR // 8)
        r = pl.ds(pl.multiple_of((i % (FR // 8)) * 8, 8), 8)
        for j in range(GY // 2048):
            acc[q, r, 2048 * j : 2048 * (j + 1)] = zeros
        return carry

    lax.fori_loop(0, 2 * FR // 8, clear, 0)
    for q in range(2):
        for j in range(GY // 2048):
            acc[q, FR : FR + 8, 2048 * j : 2048 * (j + 1)] = zeros
    lane = lax.broadcasted_iota(jnp.int32, (G + 8, 128), 1)

    def place(index, slot):
        row = row_ref[index]
        r = pl.ds(pl.multiple_of(row // 8 * 8, 8), G + 8)
        col = col_ref[index]
        tile = col // 128
        c = col % 128
        first = pl.ds(pl.multiple_of(tile * 128, 128), 128)
        second = pl.ds(pl.multiple_of(jnp.minimum(tile + 1, GY // 128 - 1) * 128, 128), 128)
        patch = jnp.concatenate([slot_ref[slot], jnp.zeros((8, 2 * G), F32)], axis=0)
        patch = pltpu.roll(patch, row % 8, 0)
        for q in range(2):
            part = jnp.where(lane < G, patch if q == 0 else pltpu.roll(patch, G, 1), 0.0)
            moved = pltpu.roll(part, c, 1)
            acc[q, r, first] += jnp.where(lane >= c, moved, 0.0)
            acc[q, r, second] += jnp.where(lane < c, moved, 0.0)

    own = CAP

    def source(b, carry):
        seen = jnp.int32(0)
        for s in range(own):
            index = b * own + s
            mine = owner_ref[index] == me

            @pl.when(mine)
            def _():
                place(index, seen * 16 + b)

            seen = seen + mine.astype(jnp.int32)
        return carry

    lax.fori_loop(0, 16, source, 0)
    copies = []
    for q in range(2):
        for j in range(8):
            r = pl.ds(j * 16, 16)
            copies.append(pltpu.make_async_copy(acc.at[q, r], out_ref.at[q, r], sem.at[q * 8 + j]))
    for copy in copies:
        copy.start()
    for copy in copies:
        copy.wait()


def deposit(me, owners, rows, cols, slots):
    return pl.pallas_call(
        deposit_kernel,
        out_shape=jax.ShapeDtypeStruct((2, FR, GY), F32),
        in_specs=[smem()] * 4 + [vmem()],
        out_specs=pl.BlockSpec(memory_space=pl.ANY),
        scratch_shapes=[pltpu.VMEM((2, FR + 8, GY), F32), pltpu.SemaphoreType.DMA((16,))],
        compiler_params=pltpu.CompilerParams(vmem_limit_bytes=48 << 20),
        name="deposit",
    )(me, owners, rows, cols, slots)


def slot_table(target, groups, depth):
    total = target.shape[0]
    hits = (target[:, None] == jnp.arange(groups, dtype=jnp.int32)[None, :]).astype(jnp.int32)
    before = jnp.cumsum(hits, axis=0) - hits
    ranking = jnp.sum(before * hits, axis=1)
    placed = target * depth + ranking
    match = placed[None, :] == jnp.arange(groups * depth, dtype=jnp.int32)[:, None]
    source = jnp.sum(jnp.where(match, jnp.arange(total, dtype=jnp.int32)[None, :], 0), axis=1)
    return source


def per_device(visibilities, anchor, drift, target, subgrid_w, facet_owner, row_offset, col_offset):
    base_count = lax.axis_size("base")
    own = subgrid_w.shape[0]
    first = (lax.axis_index("freq") * visibilities.shape[2]).astype(jnp.int32).reshape(1)
    me = lax.axis_index("base").astype(jnp.int32).reshape(1)
    vr, vi, co = prep(target, visibilities, anchor, drift)
    table = jnp.stack([facet_owner[:, 0], row_offset, col_offset])
    table = lax.all_gather(table, "base", axis=1, tiled=True)
    images = grid_all(first, vr, vi, co)
    images = lax.psum_scatter(images, "base", scatter_dimension=0, tiled=True)
    images = lax.psum(images, "freq")
    consts = [jnp.asarray(x) for x in constants()]
    patches = jax.vmap(lambda m, w: make_patch(m, w, *consts))(images, subgrid_w)
    chosen = slot_table(facet_owner[:, 0], base_count, FCAP)
    outgoing = jnp.take(patches, chosen, axis=0).reshape(base_count, FCAP, G, 2 * G)
    arrived = lax.all_to_all(outgoing, "base", split_axis=0, concat_axis=0, tiled=True)
    slots = jnp.moveaxis(arrived, 1, 0).reshape(FCAP * base_count, G, 2 * G)
    return deposit(me, table[0], table[1], table[2], slots)


def solution(mesh):
    return jax.shard_map(
        per_device,
        mesh=mesh,
        in_specs=(
            P(None, "base", "freq"),
            P(None, "base"),
            P(None, "base"),
            P("base", None),
            P("base"),
            P("base", None),
            P("base"),
            P("base"),
        ),
        out_specs=P(None, "base", None),
        check_vma=False,
    )
```

```python
import functools
import math

import jax
import jax.numpy as jnp
import numpy as np
from jax import lax
from jax.experimental import pallas as pl
from jax.experimental.pallas import tpu as pltpu
from jax.sharding import PartitionSpec as P

G = 64
GY = 16384
CAP = 8
FCAP = 2
FR = 128
NT = (((1,), (1,)), ((), ()))
F32 = jnp.float32
BF16 = jnp.bfloat16
VMEM = pltpu.MemorySpace.VMEM
SMEM = pltpu.MemorySpace.SMEM


def vmem():
    return pl.BlockSpec(memory_space=VMEM)


def smem():
    return pl.BlockSpec(memory_space=SMEM)


def prep_kernel(target_ref, vis_ref, anchor_ref, drift_ref, vr_ref, vi_ref, co_ref):
    blocks = target_ref.shape[1]
    groups = blocks // CAP
    target = target_ref[...]
    hits = (lax.broadcasted_iota(jnp.int32, (groups, blocks), 0) == target).astype(F32)
    earlier = lax.broadcasted_iota(jnp.int32, (blocks, blocks), 0) < lax.broadcasted_iota(
        jnp.int32, (blocks, blocks), 1
    )
    before = jnp.dot(hits.astype(BF16), earlier.astype(F32).astype(BF16), preferred_element_type=F32)
    ranking = jnp.sum(before * hits, axis=0, keepdims=True)
    placed = target * CAP + ranking.astype(jnp.int32)
    step = 128

    def chunk(i, carry):
        start = pl.multiple_of(i * step, step)
        rows = pl.ds(start, step)
        match = lax.broadcasted_iota(jnp.int32, (step, blocks), 0) + start == placed
        pick = match.astype(F32).astype(BF16)
        vr_ref[rows, :] = jnp.dot(pick, vis_ref[0], preferred_element_type=F32)
        vi_ref[rows, :] = jnp.dot(pick, vis_ref[1], preferred_element_type=F32)
        co_ref[rows, 0:2] = lax.dot_general(pick, anchor_ref[...], NT, preferred_element_type=F32)
        co_ref[rows, 2:4] = lax.dot_general(pick, drift_ref[...], NT, preferred_element_type=F32)
        return carry

    lax.fori_loop(0, blocks // step, chunk, 0)


def prep(target, visibilities, anchor, drift):
    _, blocks, channels = visibilities.shape
    return pl.pallas_call(
        prep_kernel,
        out_shape=(
            jax.ShapeDtypeStruct((blocks, channels), F32),
            jax.ShapeDtypeStruct((blocks, channels), F32),
            jax.ShapeDtypeStruct((blocks, 4), F32),
        ),
        in_specs=[vmem()] * 4,
        out_specs=(vmem(), vmem(), vmem()),
        compiler_params=pltpu.CompilerParams(vmem_limit_bytes=48 << 20),
        name="prep",
    )(target.reshape(1, blocks), visibilities, anchor, drift)


def trig(h):
    z = h * h
    s = 1 / 362880 + z * (-1 / 39916800)
    s = h * (1.0 + z * (-1 / 6 + z * (1 / 120 + z * (-1 / 5040 + z * s))))
    c = -1 / 3628800 + z * (1 / 479001600)
    c = 1.0 + z * (-0.5 + z * (1 / 24 + z * (-1 / 720 + z * (1 / 40320 + z * c))))
    return c, s


HALF = 152


def put(tab, row, v):
    tab[row : row + 8, :] = v[:, :128]
    tab[HALF + row : HALF + row + 8, :] = v[:, 128:]


def base_rows(h, tab):
    c0, s0 = trig(h)
    k1 = 4.0 * c0 * c0 - 2.0
    k2 = k1 * k1 - 2.0
    k4 = k2 * k2 - 2.0
    k8 = k4 * k4 - 2.0
    s8 = (2.0 * s0 * c0) * k1 * k2 * k4
    cp, cc = c0, (k1 - 1.0) * c0
    sp, sc = s0, (k1 + 1.0) * s0
    put(tab, 0, c0)
    put(tab, 64, s0)
    for p in range(1, 8):
        put(tab, 8 * p, cc)
        put(tab, 64 + 8 * p, sc)
        cp, cc = cc, k1 * cc - cp
        sp, sc = sc, k1 * sc - sp
    put(tab, 128, k8)
    put(tab, 136, 0.5 * k8)
    put(tab, 144, s8)
    return c0, s0


def expand(tab, s, h):
    o = HALF * h
    k8 = tab[o + 128 + s : o + 129 + s, :]
    c8 = tab[o + 136 + s : o + 137 + s, :]
    s8 = tab[o + 144 + s : o + 145 + s, :]
    a0 = tab[pl.ds(o + s, 8, stride=8), :]
    b0 = tab[pl.ds(o + 64 + s, 8, stride=8), :]
    a1 = c8 * a0 - s8 * b0
    b1 = c8 * b0 + s8 * a0
    a2 = k8 * a1 - a0
    b2 = k8 * b1 - b0
    a3 = k8 * a2 - a1
    b3 = k8 * b2 - b1
    return jnp.concatenate([a0, a1, a2, a3, b0, b1, b2, b3], axis=0)


def one_subgrid(g, chan, vr_ref, vi_ref, co_ref, tx, ty, tv):
    rows = pl.ds(pl.multiple_of(8 * g, 8), 8)
    co = co_ref[rows, :]
    hx = (co[:, 0:1] - 0.5 * G + chan * co[:, 2:3]) * (math.pi / G)
    hy = (co[:, 1:2] - 0.5 * G + chan * co[:, 3:4]) * (math.pi / G)
    cx, sx = base_rows(hx, tx)
    cy, sy = base_rows(hy, ty)
    er = cx * cy - sx * sy
    ei = cx * sy + sx * cy
    vr = vr_ref[rows, :]
    vi = vi_ref[rows, :]
    tv[0:8, :] = vr * er + vi * ei
    tv[8:16, :] = vi * er - vr * ei
    acc = None
    for s in range(8):
        f = jnp.concatenate([expand(tx, s, h).astype(BF16) for h in (0, 1)], axis=1)
        parts = []
        for h in (0, 1):
            g0 = expand(ty, s, h)
            cut = slice(128 * h, 128 * h + 128)
            both = [g0 * tv[s : s + 1, cut], g0 * tv[8 + s : 9 + s, cut]]
            parts.append(jnp.concatenate(both, axis=0).astype(BF16))
        r = jnp.concatenate(parts, axis=1)
        d = lax.dot_general(f, r, NT, preferred_element_type=F32)
        acc = d if acc is None else acc + d
    return acc


def constants():
    l = np.arange(G) - G // 2 + 0.5
    p = np.arange(G // 2) + 0.5
    same = (np.abs(l)[:, None] == p[None, :]).astype(np.float64)
    a = np.concatenate([same, 0 * same], axis=1)
    b = np.concatenate([0 * same, same * np.sign(l)[:, None]], axis=1)
    turns = 2 * np.pi * ((np.arange(G)[:, None] * np.arange(G)[None, :]) % G) / G
    fr, fi = np.cos(turns), -np.sin(turns)
    left1 = np.concatenate([a, b], axis=0)
    right1 = np.block([[a.T, b.T], [-b.T, a.T]])
    left2 = np.concatenate([fr, fi], axis=0)
    right2 = np.block([[fr, fi], [-fi, fr]]) / G
    return [x.astype(np.float32) for x in (left1, right1, left2, right2)]


def swap(x):
    return pltpu.roll(x, G, 1)


def dot32(a, b):
    return jnp.dot(a, b, precision=lax.Precision.HIGHEST, preferred_element_type=F32)


def make_patch(m, w, left1, right1, left2, right2):
    lane = lax.broadcasted_iota(jnp.int32, (G, 2 * G), 1)
    sign = jnp.where(lane < G, -1.0, 1.0).astype(F32)
    row = lax.broadcasted_iota(jnp.int32, (G, 2 * G), 0)
    xl = (row - G // 2).astype(F32) * (2.0 / G)
    xm = (lane % G - G // 2).astype(F32) * (2.0 / G)
    c, s = trig((0.25 * math.pi) * w * (xl * xl + xm * xm))
    for _ in range(2):
        c, s = 2.0 * c * c - 1.0, 2.0 * c * s
    both = dot32(left1, m)
    y = both[:G] + sign * swap(both[G:])
    z = dot32(y, right1)
    k = z * c + swap(z) * (s * sign)
    both = dot32(left2, k)
    y = both[:G] + sign * swap(both[G:])
    return dot32(y, right2)


MESH = pl.DeviceIdType.MESH


def main_kernel(
    nb,
    nf,
    owner_ref,
    w_ref,
    spot_ref,
    vr_ref,
    vi_ref,
    co_ref,
    left1,
    right1,
    left2,
    right2,
    slots,
    table,
    tx,
    ty,
    tv,
    send,
    recv,
    total,
    fsum,
    gath,
    outb,
    spot_s,
    spot_r,
    base_s,
    base_r,
    freq_s,
    freq_r,
    gath_s,
    gath_r,
    out_s,
    out_r,
    pair_s,
    pair_r,
):
    me_b = lax.axis_index("base")
    me_f = lax.axis_index("freq")
    own = total.shape[0]
    core = me_f % 2

    def base_copy(src, dst, ss, rs, t):
        return pltpu.make_async_remote_copy(
            src_ref=src, dst_ref=dst, send_sem=ss, recv_sem=rs, device_id={"base": (me_b + t) % nb}, device_id_type=MESH
        )

    def freq_copy(src, dst, ss, rs, d):
        return pltpu.make_async_remote_copy(
            src_ref=src, dst_ref=dst, send_sem=ss, recv_sem=rs, device_id={"freq": (me_f + d) % nf}, device_id_type=MESH
        )

    def each(low, high, body):
        def step(i, carry):
            body(i)
            return carry

        lax.fori_loop(low, high, step, 0)

    barrier = pltpu.get_barrier_semaphore()
    each(1, nb, lambda t: pl.semaphore_signal(barrier, inc=1, device_id={"base": (me_b + t) % nb}, device_id_type=MESH))
    each(1, nf, lambda d: pl.semaphore_signal(barrier, inc=1, device_id={"freq": (me_f + d) % nf}, device_id_type=MESH))
    pl.semaphore_wait(barrier, nb + nf - 2)

    def spot_copy(t):
        return base_copy(spot_ref, table.at[pl.ds(me_b, 1)], spot_s.at[t - 1], spot_r.at[t - 1], t)

    each(1, nb, lambda t: spot_copy(t).start())
    table[pl.ds(me_b, 1), :] = spot_ref[...]

    channels = vr_ref.shape[1]
    chan = (lax.broadcasted_iota(jnp.int32, (8, channels), 1) + me_f * channels).astype(F32)

    def share_copy(t):
        return base_copy(send.at[t], recv.at[t], base_s.at[t], base_r.at[t], t + 1)

    def group(t):
        owner = (me_b + 1 + t) % nb

        def one(j):
            g = owner * own + j
            send[t, j] = one_subgrid(g, chan, vr_ref, vi_ref, co_ref, tx, ty, tv).astype(BF16)

        each(0, own, one)

        @pl.when(t < nb - 1)
        def _():
            share_copy(t).start()

    each(0, nb, group)

    def own_share(j):
        total[j] = send[nb - 1, j].astype(F32)

    each(0, own, own_share)

    def add_share(t):
        share_copy(t).wait_recv()

        def add(j):
            total[j] += recv[t, j].astype(F32)

        each(0, own, add)

    each(0, nb - 1, add_share)

    def sum_copy(d):
        return freq_copy(total.at[(me_f + d) % nf], fsum.at[d - 1], freq_s.at[d - 1], freq_r.at[d - 1], d)

    each(1, nf, lambda d: sum_copy(d).start())
    m = total[me_f]
    for d in range(1, nf):
        sum_copy(d).wait_recv()
        m = m + fsum[d - 1]
    gath[me_f] = make_patch(m, w_ref[me_f], left1[...], right1[...], left2[...], right2[...])

    def gath_copy(d):
        return freq_copy(gath.at[me_f], gath.at[me_f], gath_s.at[d - 1], gath_r.at[d - 1], d)

    each(1, nf, lambda d: gath_copy(d).start())
    each(1, nf, lambda d: gath_copy(d).wait_recv())

    def out_copy(t):
        return base_copy(outb.at[(me_b + t) % nb], slots.at[core, me_b], out_s.at[t - 1], out_r.at[t - 1], t)

    def pick(o):
        seen = jnp.int32(0)
        index = jnp.int32(0)
        for s in range(own):
            hit = (owner_ref[s] == o).astype(jnp.int32)
            use = hit * (seen == core).astype(jnp.int32)
            index = index + use * s
            seen = seen + hit
        return gath[index]

    def ship(t):
        o = (me_b + t) % nb
        outb[o] = pick(o)
        out_copy(t).start()

    each(1, nb, ship)
    slots[core, me_b] = pick(me_b)

    def pair_copy(t):
        source = (me_b + nb - t) % nb
        part = slots.at[core, source]
        return pltpu.make_async_remote_copy(
            src_ref=part,
            dst_ref=part,
            send_sem=pair_s.at[t],
            recv_sem=pair_r.at[t],
            device_id={"freq": me_f + 1 - 2 * core},
            device_id_type=MESH,
        )

    pair_copy(0).start()

    def forward(t):
        out_copy(t).wait_recv()
        pair_copy(t).start()

    each(1, nb, forward)
    each(0, nb, lambda t: pair_copy(t).wait())
    each(1, nb, lambda t: out_copy(t).wait_send())
    each(1, nf, lambda d: gath_copy(d).wait_send())
    each(1, nf, lambda d: sum_copy(d).wait_send())
    each(0, nb - 1, lambda t: share_copy(t).wait_send())
    each(1, nb, lambda t: spot_copy(t).wait())


def main(owner, w, spot, vr, vi, co, nb, nf):
    own = w.shape[0]
    unit = (G, 2 * G)
    dma = pltpu.SemaphoreType.DMA
    consts = [jnp.asarray(x) for x in constants()]
    return pl.pallas_call(
        functools.partial(main_kernel, nb, nf),
        out_shape=(
            jax.ShapeDtypeStruct((FCAP, nb) + unit, F32),
            jax.ShapeDtypeStruct((nb, 128), jnp.int32),
        ),
        in_specs=[smem()] * 2 + [vmem()] * 8,
        out_specs=(vmem(), vmem()),
        scratch_shapes=[
            pltpu.VMEM((2 * HALF, 128), F32),
            pltpu.VMEM((2 * HALF, 128), F32),
            pltpu.VMEM((16, 256), F32),
            pltpu.VMEM((nb, own) + unit, BF16),
            pltpu.VMEM((nb - 1, own) + unit, BF16),
            pltpu.VMEM((own,) + unit, F32),
            pltpu.VMEM((nf - 1,) + unit, F32),
            pltpu.VMEM((nf,) + unit, F32),
            pltpu.VMEM((nb,) + unit, F32),
            dma((nb - 1,)),
            dma((nb - 1,)),
            dma((nb - 1,)),
            dma((nb - 1,)),
            dma((nf - 1,)),
            dma((nf - 1,)),
            dma((nf - 1,)),
            dma((nf - 1,)),
            dma((nb - 1,)),
            dma((nb - 1,)),
            dma((nb,)),
            dma((nb,)),
        ],
        compiler_params=pltpu.CompilerParams(
            vmem_limit_bytes=48 << 20, collective_id=0, has_side_effects=True
        ),
        name="main",
    )(owner, w, spot, vr, vi, co, *consts)


def deposit_kernel(me_ref, table_ref, slot_ref, out_ref, acc, sem):
    me = me_ref[0]
    zeros = jnp.zeros((8, 2048), F32)

    def clear(i, carry):
        q = i // (FR // 8)
        r = pl.ds(pl.multiple_of((i % (FR // 8)) * 8, 8), 8)
        for j in range(GY // 2048):
            acc[q, r, 2048 * j : 2048 * (j + 1)] = zeros
        return carry

    lax.fori_loop(0, 2 * FR // 8, clear, 0)
    for q in range(2):
        for j in range(GY // 2048):
            acc[q, FR : FR + 8, 2048 * j : 2048 * (j + 1)] = zeros
    lane = lax.broadcasted_iota(jnp.int32, (G + 8, 128), 1)

    def place(b, s, rank):
        row = table_ref[b, 8 + s]
        r = pl.ds(pl.multiple_of(row // 8 * 8, 8), G + 8)
        col = table_ref[b, 16 + s]
        tile = col // 128
        c = col % 128
        first = pl.ds(pl.multiple_of(tile * 128, 128), 128)
        second = pl.ds(pl.multiple_of(jnp.minimum(tile + 1, GY // 128 - 1) * 128, 128), 128)
        patch = jnp.concatenate([slot_ref[rank, b], jnp.zeros((8, 2 * G), F32)], axis=0)
        patch = pltpu.roll(patch, row % 8, 0)
        for q in range(2):
            part = jnp.where(lane < G, patch if q == 0 else pltpu.roll(patch, G, 1), 0.0)
            moved = pltpu.roll(part, c, 1)
            acc[q, r, first] += jnp.where(lane >= c, moved, 0.0)
            acc[q, r, second] += jnp.where(lane < c, moved, 0.0)

    def source(b, carry):
        seen = jnp.int32(0)
        for s in range(8):
            mine = table_ref[b, s] == me

            @pl.when(mine)
            def _():
                place(b, s, seen)

            seen = seen + mine.astype(jnp.int32)
        return carry

    lax.fori_loop(0, table_ref.shape[0], source, 0)
    copies = []
    for q in range(2):
        for j in range(8):
            r = pl.ds(j * 16, 16)
            copies.append(pltpu.make_async_copy(acc.at[q, r], out_ref.at[q, r], sem.at[q * 8 + j]))
    for copy in copies:
        copy.start()
    for copy in copies:
        copy.wait()


def deposit(me, table, slots):
    return pl.pallas_call(
        deposit_kernel,
        out_shape=jax.ShapeDtypeStruct((2, FR, GY), F32),
        in_specs=[smem()] * 2 + [vmem()],
        out_specs=pl.BlockSpec(memory_space=pl.ANY),
        scratch_shapes=[pltpu.VMEM((2, FR + 8, GY), F32), pltpu.SemaphoreType.DMA((16,))],
        compiler_params=pltpu.CompilerParams(vmem_limit_bytes=48 << 20),
        name="deposit",
    )(me, table, slots)


def per_device(visibilities, anchor, drift, target, subgrid_w, facet_owner, row_offset, col_offset):
    nb, nf = lax.axis_size("base"), lax.axis_size("freq")
    me = lax.axis_index("base").astype(jnp.int32).reshape(1)
    owner = facet_owner[:, 0]
    spot = jnp.concatenate([owner, row_offset, col_offset])
    spot = jnp.pad(spot, (0, 128 - spot.shape[0])).reshape(1, 128)
    vr, vi, co = prep(target, visibilities, anchor, drift)
    slots, table = main(owner, subgrid_w, spot, vr, vi, co, nb, nf)
    return deposit(me, table, slots)


def solution(mesh):
    return jax.shard_map(
        per_device,
        mesh=mesh,
        in_specs=(
            P(None, "base", "freq"),
            P(None, "base"),
            P(None, "base"),
            P("base", None),
            P("base"),
            P("base", None),
            P("base"),
            P("base"),
        ),
        out_specs=P(None, "base", None),
        check_vma=False,
    )
```

```python
import functools
import math

import jax
import jax.numpy as jnp
import numpy as np
from jax import lax
from jax.experimental import pallas as pl
from jax.experimental.pallas import tpu as pltpu
from jax.sharding import PartitionSpec as P

G = 64
GY = 16384
CAP = 8
FCAP = 2
FR = 128
NT = (((1,), (1,)), ((), ()))
F32 = jnp.float32
BF16 = jnp.bfloat16
VMEM = pltpu.MemorySpace.VMEM
SMEM = pltpu.MemorySpace.SMEM


def vmem():
    return pl.BlockSpec(memory_space=VMEM)


def hbm():
    return pl.BlockSpec(memory_space=pltpu.MemorySpace.HBM)


def stay(x):
    return pltpu.with_memory_space_constraint(x, pltpu.MemorySpace.HBM)


def smem():
    return pl.BlockSpec(memory_space=SMEM)


CLEAR = 2048


def prep_kernel(
    target_hbm, vis_hbm, anchor_hbm, drift_hbm, vr_ref, vi_ref, co_ref, grid_ref, target_ref, vis_ref, anchor_ref, drift_ref, zeros, sem, zsem
):
    pairs = [(target_hbm, target_ref), (vis_hbm, vis_ref), (anchor_hbm, anchor_ref), (drift_hbm, drift_ref)]
    loads = [pltpu.make_async_copy(src, dst, sem.at[i]) for i, (src, dst) in enumerate(pairs)]
    for load in loads:
        load.start()
    zeros[...] = jnp.zeros(zeros.shape, F32)
    clears = []
    for q in range(2):
        for j in range(GY // CLEAR):
            part = grid_ref.at[q, :, CLEAR * j : CLEAR * (j + 1)]
            clears.append(pltpu.make_async_copy(zeros, part, zsem.at[len(clears)]))
    loads[0].wait()
    blocks = target_ref.shape[1]
    groups = blocks // CAP
    target = target_ref[...]
    hits = (lax.broadcasted_iota(jnp.int32, (groups, blocks), 0) == target).astype(F32)
    earlier = lax.broadcasted_iota(jnp.int32, (blocks, blocks), 0) < lax.broadcasted_iota(
        jnp.int32, (blocks, blocks), 1
    )
    before = jnp.dot(hits.astype(BF16), earlier.astype(F32).astype(BF16), preferred_element_type=F32)
    ranking = jnp.sum(before * hits, axis=0, keepdims=True)
    placed = target * CAP + ranking.astype(jnp.int32)
    step = 128
    for load in loads[1:]:
        load.wait()
    for clear in clears:
        clear.start()

    def chunk(i, carry):
        start = pl.multiple_of(i * step, step)
        rows = pl.ds(start, step)
        match = lax.broadcasted_iota(jnp.int32, (step, blocks), 0) + start == placed
        pick = match.astype(F32).astype(BF16)
        vr_ref[rows, :] = jnp.dot(pick, vis_ref[0], preferred_element_type=F32)
        vi_ref[rows, :] = jnp.dot(pick, vis_ref[1], preferred_element_type=F32)
        co_ref[rows, 0:2] = lax.dot_general(pick, anchor_ref[...], NT, preferred_element_type=F32)
        co_ref[rows, 2:4] = lax.dot_general(pick, drift_ref[...], NT, preferred_element_type=F32)
        return carry

    lax.fori_loop(0, blocks // step, chunk, 0)
    for clear in clears:
        clear.wait()


def prep(target, visibilities, anchor, drift):
    _, blocks, channels = visibilities.shape
    return pl.pallas_call(
        prep_kernel,
        out_shape=(
            jax.ShapeDtypeStruct((blocks, channels), F32),
            jax.ShapeDtypeStruct((blocks, channels), F32),
            jax.ShapeDtypeStruct((blocks, 4), F32),
            jax.ShapeDtypeStruct((2, FR, GY), F32),
        ),
        in_specs=[hbm()] * 4,
        out_specs=(vmem(), vmem(), vmem(), hbm()),
        scratch_shapes=[
            pltpu.VMEM((1, blocks), jnp.int32),
            pltpu.VMEM(visibilities.shape, BF16),
            pltpu.VMEM(anchor.shape, BF16),
            pltpu.VMEM(drift.shape, BF16),
            pltpu.VMEM((FR, CLEAR), F32),
            pltpu.SemaphoreType.DMA((4,)),
            pltpu.SemaphoreType.DMA((2 * GY // CLEAR,)),
        ],
        compiler_params=pltpu.CompilerParams(vmem_limit_bytes=48 << 20),
        name="prep",
    )(target, visibilities, anchor, drift)


def trig(h):
    z = h * h
    s = 1 / 362880 + z * (-1 / 39916800)
    s = h * (1.0 + z * (-1 / 6 + z * (1 / 120 + z * (-1 / 5040 + z * s))))
    c = -1 / 3628800 + z * (1 / 479001600)
    c = 1.0 + z * (-0.5 + z * (1 / 24 + z * (-1 / 720 + z * (1 / 40320 + z * c))))
    return c, s


HALF = 152


def put(tab, row, v):
    tab[row : row + 8, :] = v[:, :128]
    tab[HALF + row : HALF + row + 8, :] = v[:, 128:]


def base_rows(h, tab):
    c0, s0 = trig(h)
    k1 = 4.0 * c0 * c0 - 2.0
    k2 = k1 * k1 - 2.0
    k4 = k2 * k2 - 2.0
    k8 = k4 * k4 - 2.0
    s8 = (2.0 * s0 * c0) * k1 * k2 * k4
    cp, cc = c0, (k1 - 1.0) * c0
    sp, sc = s0, (k1 + 1.0) * s0
    put(tab, 0, c0)
    put(tab, 64, s0)
    for p in range(1, 8):
        put(tab, 8 * p, cc)
        put(tab, 64 + 8 * p, sc)
        cp, cc = cc, k1 * cc - cp
        sp, sc = sc, k1 * sc - sp
    put(tab, 128, k8)
    put(tab, 136, 0.5 * k8)
    put(tab, 144, s8)
    return c0, s0


def expand(tab, s, h):
    o = HALF * h
    k8 = tab[o + 128 + s : o + 129 + s, :]
    c8 = tab[o + 136 + s : o + 137 + s, :]
    s8 = tab[o + 144 + s : o + 145 + s, :]
    a0 = tab[pl.ds(o + s, 8, stride=8), :]
    b0 = tab[pl.ds(o + 64 + s, 8, stride=8), :]
    a1 = c8 * a0 - s8 * b0
    b1 = c8 * b0 + s8 * a0
    a2 = k8 * a1 - a0
    b2 = k8 * b1 - b0
    a3 = k8 * a2 - a1
    b3 = k8 * b2 - b1
    return jnp.concatenate([a0, a1, a2, a3, b0, b1, b2, b3], axis=0)


def tables(g, chan, vr_ref, vi_ref, co_ref, tx, ty, tv):
    rows = pl.ds(pl.multiple_of(8 * g, 8), 8)
    co = co_ref[rows, :]
    hx = (co[:, 0:1] - 0.5 * G + chan * co[:, 2:3]) * (math.pi / G)
    hy = (co[:, 1:2] - 0.5 * G + chan * co[:, 3:4]) * (math.pi / G)
    cx, sx = base_rows(hx, tx)
    cy, sy = base_rows(hy, ty)
    er = cx * cy - sx * sy
    ei = cx * sy + sx * cy
    vr = vr_ref[rows, :]
    vi = vi_ref[rows, :]
    tv[0:8, :] = vr * er + vi * ei
    tv[8:16, :] = vi * er - vr * ei


def products(tx, ty, tv):
    acc = None
    for s in range(8):
        f = jnp.concatenate([expand(tx, s, h).astype(BF16) for h in (0, 1)], axis=1)
        parts = []
        for h in (0, 1):
            g0 = expand(ty, s, h)
            cut = slice(128 * h, 128 * h + 128)
            both = [g0 * tv[s : s + 1, cut], g0 * tv[8 + s : 9 + s, cut]]
            parts.append(jnp.concatenate(both, axis=0).astype(BF16))
        r = jnp.concatenate(parts, axis=1)
        d = lax.dot_general(f, r, NT, preferred_element_type=F32)
        acc = d if acc is None else acc + d
    return acc


def constants():
    l = np.arange(G) - G // 2 + 0.5
    p = np.arange(G // 2) + 0.5
    same = (np.abs(l)[:, None] == p[None, :]).astype(np.float64)
    a = np.concatenate([same, 0 * same], axis=1)
    b = np.concatenate([0 * same, same * np.sign(l)[:, None]], axis=1)
    turns = 2 * np.pi * ((np.arange(G)[:, None] * np.arange(G)[None, :]) % G) / G
    fr, fi = np.cos(turns), -np.sin(turns)
    left1 = np.concatenate([a, b], axis=0)
    right1 = np.block([[a.T, b.T], [-b.T, a.T]])
    left2 = np.concatenate([fr, fi], axis=0)
    right2 = np.block([[fr, fi], [-fi, fr]]) / G

    def split(x):
        high = x.astype(jnp.bfloat16)
        return high, (x - high.astype(np.float64)).astype(jnp.bfloat16)

    one_l, _ = split(left1)
    one_r, _ = split(right1)
    two_l, two_ll = split(left2)
    two_r, two_rl = split(right2)
    return [
        np.concatenate([one_l, one_l], axis=1),
        np.concatenate([one_r, one_r], axis=0),
        np.concatenate([two_l, two_l, two_ll, 0 * two_l], axis=1),
        np.concatenate([two_r, two_r, two_rl], axis=0),
    ]


def split_rows(x, times, axis):
    high = x.astype(BF16)
    low = (x - high.astype(F32)).astype(BF16)
    return jnp.concatenate(([high, low] + [high] * 2)[:times], axis=axis)


def dot16(a, b):
    return jnp.dot(a, b, preferred_element_type=F32)


def swap(x):
    return pltpu.roll(x, G, 1)


def screen(w):
    row = lax.broadcasted_iota(jnp.int32, (G, 2 * G), 0)
    lane = lax.broadcasted_iota(jnp.int32, (G, 2 * G), 1)
    xl = (row - G // 2).astype(F32) * (2.0 / G)
    xm = (jnp.where(lane < G, lane, lane - G) - G // 2).astype(F32) * (2.0 / G)
    c, s = trig((0.25 * math.pi) * w * (xl * xl + xm * xm))
    for _ in range(2):
        c, s = 2.0 * c * c - 1.0, 2.0 * c * s
    return c, jnp.where(lane < G, -s, s)


def make_patch(m, c, s, left1, right1, left2, right2):
    lane = lax.broadcasted_iota(jnp.int32, (G, 2 * G), 1)
    sign = jnp.where(lane < G, -1.0, 1.0).astype(F32)
    both = dot16(left1, split_rows(m, 2, 0))
    y = both[:G] + sign * swap(both[G:])
    z = dot16(split_rows(y, 2, 1), right1)
    k = z * c + swap(z) * s
    both = dot16(left2, split_rows(k, 4, 0))
    y = both[:G] + sign * swap(both[G:])
    return dot16(split_rows(y, 3, 1), right2)


MESH = pl.DeviceIdType.MESH


def main_kernel(
    nb,
    nf,
    owner_hbm,
    row_hbm,
    col_hbm,
    w_hbm,
    left1_hbm,
    right1_hbm,
    left2_hbm,
    right2_hbm,
    vr_ref,
    vi_ref,
    co_ref,
    slots,
    table,
    owner_ref,
    row_ref,
    col_ref,
    w_ref,
    left1,
    right1,
    left2,
    right2,
    spot_ref,
    tx0,
    ty0,
    tv0,
    tx1,
    ty1,
    tv1,
    cs,
    send,
    recv,
    total,
    fsum,
    gath,
    outb,
    load_sem,
    spot_s,
    spot_r,
    base_s,
    base_r,
    freq_s,
    freq_r,
    gath_s,
    gath_r,
    out_s,
    out_r,
    pair_s,
    pair_r,
):
    me_b = lax.axis_index("base")
    me_f = lax.axis_index("freq")
    own = total.shape[0]
    core = me_f % 2
    even = (tx0, ty0, tv0)
    odd = (tx1, ty1, tv1)

    def base_copy(src, dst, ss, rs, t):
        return pltpu.make_async_remote_copy(
            src_ref=src, dst_ref=dst, send_sem=ss, recv_sem=rs, device_id={"base": (me_b + t) % nb}, device_id_type=MESH
        )

    def freq_copy(src, dst, ss, rs, d):
        return pltpu.make_async_remote_copy(
            src_ref=src, dst_ref=dst, send_sem=ss, recv_sem=rs, device_id={"freq": (me_f + d) % nf}, device_id_type=MESH
        )

    def each(low, high, body):
        def step(i, carry):
            body(i)
            return carry

        lax.fori_loop(low, high, step, 0)

    barrier = pltpu.get_barrier_semaphore()
    each(1, nb, lambda t: pl.semaphore_signal(barrier, inc=1, device_id={"base": (me_b + t) % nb}, device_id_type=MESH))
    each(1, nf, lambda d: pl.semaphore_signal(barrier, inc=1, device_id={"freq": (me_f + d) % nf}, device_id_type=MESH))
    pairs = [
        (owner_hbm, owner_ref),
        (row_hbm, row_ref),
        (col_hbm, col_ref),
        (w_hbm, w_ref),
        (left1_hbm, left1),
        (right1_hbm, right1),
        (left2_hbm, left2),
        (right2_hbm, right2),
    ]
    loads = [pltpu.make_async_copy(src, dst, load_sem.at[i]) for i, (src, dst) in enumerate(pairs)]
    for load in loads:
        load.start()

    channels = vr_ref.shape[1]
    chan = (lax.broadcasted_iota(jnp.int32, (8, channels), 1) + me_f * channels).astype(F32)

    def subgrid(i):
        return (me_b + 1 + i // own) % nb * own + i % own

    def prepare(i, tabs):
        tables(subgrid(i), chan, vr_ref, vi_ref, co_ref, *tabs)

    def spot_copy(t):
        return base_copy(spot_ref, table.at[pl.ds(me_b, 1)], spot_s.at[t - 1], spot_r.at[t - 1], t)

    def share_copy(t):
        return base_copy(send.at[t], recv.at[t], base_s.at[t], base_r.at[t], t + 1)

    prepare(0, even)
    for load in loads:
        load.wait()
    lane = lax.broadcasted_iota(jnp.int32, (1, 128), 1)
    spot = jnp.zeros((1, 128), jnp.int32)
    for n, ref in enumerate((owner_ref, row_ref, col_ref)):
        for i in range(own):
            spot = jnp.where(lane == n * own + i, ref[0, i], spot)
    spot_ref[...] = spot
    table[pl.ds(me_b, 1), :] = spot
    c, s = screen(w_ref[0, me_f])
    cs[0] = c
    cs[1] = s

    def group(t):
        def two(u):
            i = t * own + 2 * u
            prepare(i + 1, odd)
            send[t, 2 * u] = products(*even).astype(BF16)
            prepare(i + 2, even)
            send[t, 2 * u + 1] = products(*odd).astype(BF16)

        each(0, own // 2, two)

        @pl.when(t == 0)
        def _():
            pl.semaphore_wait(barrier, nb + nf - 2)
            each(1, nb, lambda t: spot_copy(t).start())

        @pl.when(t < nb - 1)
        def _():
            share_copy(t).start()

    each(0, nb, group)
    each(0, nb - 1, lambda t: share_copy(t).wait_recv())

    def sum_shares(j):
        m = send[nb - 1, j].astype(F32)
        for t in range(nb - 1):
            m = m + recv[t, j].astype(F32)
        return m

    def sum_copy(d):
        return freq_copy(total.at[(me_f + d) % nf], fsum.at[d - 1], freq_s.at[d - 1], freq_r.at[d - 1], d)

    def reduce(d):
        j = (me_f + d) % nf
        total[j] = sum_shares(j)
        sum_copy(d).start()

    each(1, nf, reduce)
    m = sum_shares(me_f)
    each(1, nf, lambda d: sum_copy(d).wait_recv())
    for d in range(1, nf):
        m = m + fsum[d - 1]
    gath[me_f] = make_patch(m, cs[0], cs[1], left1[...], right1[...], left2[...], right2[...])

    def gath_copy(d):
        return freq_copy(gath.at[me_f], gath.at[me_f], gath_s.at[d - 1], gath_r.at[d - 1], d)

    each(1, nf, lambda d: gath_copy(d).start())
    each(1, nf, lambda d: gath_copy(d).wait_recv())

    def out_copy(t):
        return base_copy(outb.at[(me_b + t) % nb], slots.at[core, me_b], out_s.at[t - 1], out_r.at[t - 1], t)

    def pick(o):
        seen = jnp.int32(0)
        index = jnp.int32(0)
        for s in range(own):
            hit = (owner_ref[0, s] == o).astype(jnp.int32)
            use = hit * (seen == core).astype(jnp.int32)
            index = index + use * s
            seen = seen + hit
        return gath[index]

    def ship(t):
        o = (me_b + t) % nb
        outb[o] = pick(o)
        out_copy(t).start()

    each(1, nb, ship)
    slots[core, me_b] = pick(me_b)

    def pair_copy(t):
        source = (me_b + nb - t) % nb
        part = slots.at[core, source]
        return pltpu.make_async_remote_copy(
            src_ref=part,
            dst_ref=part,
            send_sem=pair_s.at[t],
            recv_sem=pair_r.at[t],
            device_id={"freq": me_f + 1 - 2 * core},
            device_id_type=MESH,
        )

    pair_copy(0).start()

    def forward(t):
        out_copy(t).wait_recv()
        pair_copy(t).start()

    each(1, nb, forward)
    each(0, nb, lambda t: pair_copy(t).wait())
    each(1, nb, lambda t: out_copy(t).wait_send())
    each(1, nf, lambda d: gath_copy(d).wait_send())
    each(1, nf, lambda d: sum_copy(d).wait_send())
    each(0, nb - 1, lambda t: share_copy(t).wait_send())
    each(1, nb, lambda t: spot_copy(t).wait())


def main(owner, row, col, w, vr, vi, co, nb, nf):
    own = w.shape[1]
    unit = (G, 2 * G)
    dma = pltpu.SemaphoreType.DMA
    consts = [stay(jnp.asarray(x)) for x in constants()]
    tabs = [pltpu.VMEM((2 * HALF, 128), F32), pltpu.VMEM((2 * HALF, 128), F32), pltpu.VMEM((16, 256), F32)]
    return pl.pallas_call(
        functools.partial(main_kernel, nb, nf),
        out_shape=(
            jax.ShapeDtypeStruct((FCAP, nb) + unit, F32),
            jax.ShapeDtypeStruct((nb, 128), jnp.int32),
        ),
        in_specs=[hbm()] * 8 + [vmem()] * 3,
        out_specs=(vmem(), vmem()),
        scratch_shapes=[
            pltpu.SMEM((1, own), jnp.int32),
            pltpu.SMEM((1, own), jnp.int32),
            pltpu.SMEM((1, own), jnp.int32),
            pltpu.SMEM((1, own), F32),
        ]
        + [pltpu.VMEM(x.shape, BF16) for x in consts]
        + [pltpu.VMEM((1, 128), jnp.int32)]
        + tabs * 2
        + [
            pltpu.VMEM((2,) + unit, F32),
            pltpu.VMEM((nb, own) + unit, BF16),
            pltpu.VMEM((nb - 1, own) + unit, BF16),
            pltpu.VMEM((own,) + unit, F32),
            pltpu.VMEM((nf - 1,) + unit, F32),
            pltpu.VMEM((nf,) + unit, F32),
            pltpu.VMEM((nb,) + unit, F32),
            dma((8,)),
            dma((nb - 1,)),
            dma((nb - 1,)),
            dma((nb - 1,)),
            dma((nb - 1,)),
            dma((nf - 1,)),
            dma((nf - 1,)),
            dma((nf - 1,)),
            dma((nf - 1,)),
            dma((nb - 1,)),
            dma((nb - 1,)),
            dma((nb,)),
            dma((nb,)),
        ],
        compiler_params=pltpu.CompilerParams(
            vmem_limit_bytes=48 << 20, collective_id=0, has_side_effects=True
        ),
        name="main",
    )(owner, row, col, w, *consts, vr, vi, co)


def deposit_kernel(table_ref, slot_ref, grid_in, grid_ref, blocks, where_ref, tile_ref, count_ref, sem):
    del grid_in
    me = lax.axis_index("base")
    tiles = GY // 128

    def reset(i, carry):
        where_ref[i] = -1
        return carry

    lax.fori_loop(0, tiles, reset, 0)
    count_ref[0] = 0
    lane = lax.broadcasted_iota(jnp.int32, (G + 8, 128), 1)

    def block_of(tile):
        @pl.when(where_ref[tile] < 0)
        def _():
            count = count_ref[0]
            where_ref[tile] = count
            tile_ref[count] = tile
            count_ref[0] = count + 1
            blocks[count] = jnp.zeros(blocks.shape[1:], F32)

        return where_ref[tile]

    def place(b, s, rank):
        row = table_ref[b, 8 + s]
        r = pl.ds(pl.multiple_of(row // 8 * 8, 8), G + 8)
        col = table_ref[b, 16 + s]
        tile = col // 128
        c = col % 128
        patch = jnp.concatenate([slot_ref[rank, b], jnp.zeros((8, 2 * G), F32)], axis=0)
        patch = pltpu.roll(patch, row % 8, 0)
        real = pltpu.roll(jnp.where(lane < G, patch, 0.0), c, 1)
        imag = pltpu.roll(jnp.where(lane < G, 0.0, patch), c + G, 1)
        first = block_of(tile)
        blocks[first, 0, r, :] += jnp.where(lane >= c, real, 0.0)
        blocks[first, 1, r, :] += jnp.where(lane >= c, imag, 0.0)

        @pl.when(c > 128 - G)
        def _():
            second = block_of(tile + 1)
            blocks[second, 0, r, :] += jnp.where(lane < c, real, 0.0)
            blocks[second, 1, r, :] += jnp.where(lane < c, imag, 0.0)

    def source(b, carry):
        seen = jnp.int32(0)
        for s in range(8):
            mine = table_ref[b, s] == me

            @pl.when(mine)
            def _():
                place(b, s, seen)

            seen = seen + mine.astype(jnp.int32)
        return carry

    lax.fori_loop(0, table_ref.shape[0], source, 0)
    count = count_ref[0]

    def copy(i):
        cut = pl.ds(pl.multiple_of(tile_ref[i] * 128, 128), 128)
        return pltpu.make_async_copy(blocks.at[i, :, 0:FR, :], grid_ref.at[:, :, cut], sem.at[i])

    def start(i, carry):
        copy(i).start()
        return carry

    def wait(i, carry):
        copy(i).wait()
        return carry

    lax.fori_loop(0, count, start, 0)
    lax.fori_loop(0, count, wait, 0)


def deposit(table, slots, grid):
    most = 2 * slots.shape[0] * slots.shape[1]
    return pl.pallas_call(
        deposit_kernel,
        out_shape=jax.ShapeDtypeStruct((2, FR, GY), F32),
        in_specs=[smem(), vmem(), hbm()],
        out_specs=hbm(),
        scratch_shapes=[
            pltpu.VMEM((most, 2, FR + 8, 128), F32),
            pltpu.SMEM((GY // 128,), jnp.int32),
            pltpu.SMEM((most,), jnp.int32),
            pltpu.SMEM((1,), jnp.int32),
            pltpu.SemaphoreType.DMA((most,)),
        ],
        input_output_aliases={2: 0},
        compiler_params=pltpu.CompilerParams(vmem_limit_bytes=48 << 20),
        name="deposit",
    )(table, slots, grid)


def per_device(visibilities, anchor, drift, target, subgrid_w, facet_owner, row_offset, col_offset):
    nb, nf = lax.axis_size("base"), lax.axis_size("freq")
    target = target.reshape(1, -1)
    vr, vi, co, grid = prep(*[stay(x) for x in (target, visibilities, anchor, drift)])
    small = [stay(x.reshape(1, -1)) for x in (facet_owner, row_offset, col_offset, subgrid_w)]
    slots, table = main(*small, vr, vi, co, nb, nf)
    return deposit(table, slots, grid)


def solution(mesh):
    return jax.shard_map(
        per_device,
        mesh=mesh,
        in_specs=(
            P(None, "base", "freq"),
            P(None, "base"),
            P(None, "base"),
            P("base", None),
            P("base"),
            P("base", None),
            P("base"),
            P("base"),
        ),
        out_specs=P(None, "base", None),
        check_vma=False,
    )
```

```python
import functools
import math

import jax
import jax.numpy as jnp
import numpy as np
from jax import lax
from jax.experimental import pallas as pl
from jax.experimental.pallas import tpu as pltpu
from jax.sharding import PartitionSpec as P

G = 64
GY = 16384
CAP = 8
FCAP = 2
FR = 128
NT = (((1,), (1,)), ((), ()))
F32 = jnp.float32
BF16 = jnp.bfloat16
VMEM = pltpu.MemorySpace.VMEM
SMEM = pltpu.MemorySpace.SMEM


def vmem():
    return pl.BlockSpec(memory_space=VMEM)


def hbm():
    return pl.BlockSpec(memory_space=pltpu.MemorySpace.HBM)


def stay(x):
    return pltpu.with_memory_space_constraint(x, pltpu.MemorySpace.HBM)


def smem():
    return pl.BlockSpec(memory_space=SMEM)


CLEAR = 2048


def prep_kernel(
    target_hbm, vis_hbm, anchor_hbm, drift_hbm, vr_ref, vi_ref, co_ref, grid_ref, target_ref, vis_ref, anchor_ref, drift_ref, zeros, sem, zsem
):
    pairs = [(target_hbm, target_ref), (vis_hbm, vis_ref), (anchor_hbm, anchor_ref), (drift_hbm, drift_ref)]
    loads = [pltpu.make_async_copy(src, dst, sem.at[i]) for i, (src, dst) in enumerate(pairs)]
    for load in loads:
        load.start()
    zeros[...] = jnp.zeros(zeros.shape, F32)
    clears = []
    for q in range(2):
        for j in range(GY // CLEAR):
            part = grid_ref.at[q, :, CLEAR * j : CLEAR * (j + 1)]
            clears.append(pltpu.make_async_copy(zeros, part, zsem.at[len(clears)]))
    for clear in clears:
        clear.start()
    loads[0].wait()
    blocks = target_ref.shape[1]
    groups = blocks // CAP
    target = target_ref[...]
    hits = (lax.broadcasted_iota(jnp.int32, (groups, blocks), 0) == target).astype(F32)
    earlier = lax.broadcasted_iota(jnp.int32, (blocks, blocks), 0) < lax.broadcasted_iota(
        jnp.int32, (blocks, blocks), 1
    )
    before = jnp.dot(hits.astype(BF16), earlier.astype(F32).astype(BF16), preferred_element_type=F32)
    ranking = jnp.sum(before * hits, axis=0, keepdims=True)
    placed = target * CAP + ranking.astype(jnp.int32)
    step = 128
    for load in loads[1:]:
        load.wait()

    def chunk(i, carry):
        start = pl.multiple_of(i * step, step)
        rows = pl.ds(start, step)
        match = lax.broadcasted_iota(jnp.int32, (step, blocks), 0) + start == placed
        pick = match.astype(F32).astype(BF16)
        vr_ref[rows, :] = jnp.dot(pick, vis_ref[0], preferred_element_type=F32)
        vi_ref[rows, :] = jnp.dot(pick, vis_ref[1], preferred_element_type=F32)
        co_ref[rows, 0:2] = lax.dot_general(pick, anchor_ref[...], NT, preferred_element_type=F32)
        co_ref[rows, 2:4] = lax.dot_general(pick, drift_ref[...], NT, preferred_element_type=F32)
        return carry

    lax.fori_loop(0, blocks // step, chunk, 0)
    for clear in clears:
        clear.wait()


def prep(target, visibilities, anchor, drift):
    _, blocks, channels = visibilities.shape
    return pl.pallas_call(
        prep_kernel,
        out_shape=(
            jax.ShapeDtypeStruct((blocks, channels), F32),
            jax.ShapeDtypeStruct((blocks, channels), F32),
            jax.ShapeDtypeStruct((blocks, 4), F32),
            jax.ShapeDtypeStruct((2, FR, GY), F32),
        ),
        in_specs=[hbm()] * 4,
        out_specs=(vmem(), vmem(), vmem(), hbm()),
        scratch_shapes=[
            pltpu.VMEM((1, blocks), jnp.int32),
            pltpu.VMEM(visibilities.shape, BF16),
            pltpu.VMEM(anchor.shape, BF16),
            pltpu.VMEM(drift.shape, BF16),
            pltpu.VMEM((FR, CLEAR), F32),
            pltpu.SemaphoreType.DMA((4,)),
            pltpu.SemaphoreType.DMA((2 * GY // CLEAR,)),
        ],
        compiler_params=pltpu.CompilerParams(vmem_limit_bytes=48 << 20),
        name="prep",
    )(target, visibilities, anchor, drift)


def trig(h):
    z = h * h
    s = 1 / 362880 + z * (-1 / 39916800)
    s = h * (1.0 + z * (-1 / 6 + z * (1 / 120 + z * (-1 / 5040 + z * s))))
    c = -1 / 3628800 + z * (1 / 479001600)
    c = 1.0 + z * (-0.5 + z * (1 / 24 + z * (-1 / 720 + z * (1 / 40320 + z * c))))
    return c, s


HALF = 152


def put(tab, row, v):
    tab[row : row + 8, :] = v[:, :128]
    tab[HALF + row : HALF + row + 8, :] = v[:, 128:]


def base_rows(h, tab):
    c0, s0 = trig(h)
    k1 = 4.0 * c0 * c0 - 2.0
    k2 = k1 * k1 - 2.0
    k4 = k2 * k2 - 2.0
    k8 = k4 * k4 - 2.0
    s8 = (2.0 * s0 * c0) * k1 * k2 * k4
    cp, cc = c0, (k1 - 1.0) * c0
    sp, sc = s0, (k1 + 1.0) * s0
    put(tab, 0, c0)
    put(tab, 64, s0)
    for p in range(1, 8):
        put(tab, 8 * p, cc)
        put(tab, 64 + 8 * p, sc)
        cp, cc = cc, k1 * cc - cp
        sp, sc = sc, k1 * sc - sp
    put(tab, 128, k8)
    put(tab, 136, 0.5 * k8)
    put(tab, 144, s8)
    return c0, s0


def expand(tab, s, h):
    o = HALF * h
    k8 = tab[o + 128 + s : o + 129 + s, :]
    c8 = tab[o + 136 + s : o + 137 + s, :]
    s8 = tab[o + 144 + s : o + 145 + s, :]
    a0 = tab[pl.ds(o + s, 8, stride=8), :]
    b0 = tab[pl.ds(o + 64 + s, 8, stride=8), :]
    a1 = c8 * a0 - s8 * b0
    b1 = c8 * b0 + s8 * a0
    a2 = k8 * a1 - a0
    b2 = k8 * b1 - b0
    a3 = k8 * a2 - a1
    b3 = k8 * b2 - b1
    return jnp.concatenate([a0, a1, a2, a3, b0, b1, b2, b3], axis=0)


def tables(g, chan, vr_ref, vi_ref, co_ref, tx, ty, tv):
    rows = pl.ds(pl.multiple_of(8 * g, 8), 8)
    co = co_ref[rows, :]
    hx = (co[:, 0:1] - 0.5 * G + chan * co[:, 2:3]) * (math.pi / G)
    hy = (co[:, 1:2] - 0.5 * G + chan * co[:, 3:4]) * (math.pi / G)
    cx, sx = base_rows(hx, tx)
    cy, sy = base_rows(hy, ty)
    er = cx * cy - sx * sy
    ei = cx * sy + sx * cy
    vr = vr_ref[rows, :]
    vi = vi_ref[rows, :]
    tv[0:8, :] = vr * er + vi * ei
    tv[8:16, :] = vi * er - vr * ei


def products(tx, ty, tv):
    acc = None
    for s in range(8):
        f = jnp.concatenate([expand(tx, s, h).astype(BF16) for h in (0, 1)], axis=1)
        parts = []
        for h in (0, 1):
            g0 = expand(ty, s, h)
            cut = slice(128 * h, 128 * h + 128)
            both = [g0 * tv[s : s + 1, cut], g0 * tv[8 + s : 9 + s, cut]]
            parts.append(jnp.concatenate(both, axis=0).astype(BF16))
        r = jnp.concatenate(parts, axis=1)
        d = lax.dot_general(f, r, NT, preferred_element_type=F32)
        acc = d if acc is None else acc + d
    return acc


def constants():
    l = np.arange(G) - G // 2 + 0.5
    p = np.arange(G // 2) + 0.5
    same = (np.abs(l)[:, None] == p[None, :]).astype(np.float64)
    a = np.concatenate([same, 0 * same], axis=1)
    b = np.concatenate([0 * same, same * np.sign(l)[:, None]], axis=1)
    turns = 2 * np.pi * ((np.arange(G)[:, None] * np.arange(G)[None, :]) % G) / G
    fr, fi = np.cos(turns), -np.sin(turns)
    left1 = np.concatenate([a, b], axis=0)
    right1 = np.block([[a.T, b.T], [-b.T, a.T]])
    left2 = np.concatenate([fr, fi], axis=0)
    right2 = np.block([[fr, fi], [-fi, fr]]) / G

    def split(x):
        high = x.astype(jnp.bfloat16)
        return high, (x - high.astype(np.float64)).astype(jnp.bfloat16)

    one_l, _ = split(left1)
    one_r, _ = split(right1)
    two_l, two_ll = split(left2)
    two_r, two_rl = split(right2)
    return [
        np.concatenate([one_l, one_l], axis=1),
        np.concatenate([one_r, one_r], axis=0),
        np.concatenate([two_l, two_l, two_ll, 0 * two_l], axis=1),
        np.concatenate([two_r, two_r, two_rl], axis=0),
    ]


def split_rows(x, times, axis):
    high = x.astype(BF16)
    low = (x - high.astype(F32)).astype(BF16)
    return jnp.concatenate(([high, low] + [high] * 2)[:times], axis=axis)


def dot16(a, b):
    return jnp.dot(a, b, preferred_element_type=F32)


def swap(x):
    return pltpu.roll(x, G, 1)


def screen(w):
    row = lax.broadcasted_iota(jnp.int32, (G, 2 * G), 0)
    lane = lax.broadcasted_iota(jnp.int32, (G, 2 * G), 1)
    xl = (row - G // 2).astype(F32) * (2.0 / G)
    xm = (jnp.where(lane < G, lane, lane - G) - G // 2).astype(F32) * (2.0 / G)
    c, s = trig((0.25 * math.pi) * w * (xl * xl + xm * xm))
    for _ in range(2):
        c, s = 2.0 * c * c - 1.0, 2.0 * c * s
    return c, jnp.where(lane < G, -s, s)


def make_patch(m, c, s, left1, right1, left2, right2):
    lane = lax.broadcasted_iota(jnp.int32, (G, 2 * G), 1)
    sign = jnp.where(lane < G, -1.0, 1.0).astype(F32)
    both = dot16(left1, split_rows(m, 2, 0))
    y = both[:G] + sign * swap(both[G:])
    z = dot16(split_rows(y, 2, 1), right1)
    k = z * c + swap(z) * s
    both = dot16(left2, split_rows(k, 4, 0))
    y = both[:G] + sign * swap(both[G:])
    return dot16(split_rows(y, 3, 1), right2)


MESH = pl.DeviceIdType.MESH
CHUNKS = 2


def main_kernel(
    nb,
    nf,
    owner_hbm,
    row_hbm,
    col_hbm,
    w_hbm,
    left1_hbm,
    right1_hbm,
    left2_hbm,
    right2_hbm,
    vr_ref,
    vi_ref,
    co_ref,
    slots,
    table,
    owner_ref,
    row_ref,
    col_ref,
    w_ref,
    left1,
    right1,
    left2,
    right2,
    spot_ref,
    tx0,
    ty0,
    tv0,
    tx1,
    ty1,
    tv1,
    cs,
    part,
    got,
    send,
    recv,
    total,
    fsum,
    gath0,
    gath1,
    outb,
    choice,
    load_sem,
    core_s,
    core_r,
    spot_s,
    spot_r,
    base_s,
    base_r,
    freq_s,
    freq_r,
    gath_s,
    gath_r,
    out_s,
    out_r,
    pair_s,
    pair_r,
):
    me_b = lax.axis_index("base")
    me_f = lax.axis_index("freq")
    own = w_ref.shape[1]
    core = me_f % 2
    place = me_f // 2
    half = own // 2
    even = (tx0, ty0, tv0)
    odd = (tx1, ty1, tv1)

    def base_copy(src, dst, ss, rs, t):
        return pltpu.make_async_remote_copy(
            src_ref=src, dst_ref=dst, send_sem=ss, recv_sem=rs, device_id={"base": (me_b + t) % nb}, device_id_type=MESH
        )

    def freq_copy(src, dst, ss, rs, d):
        return pltpu.make_async_remote_copy(
            src_ref=src, dst_ref=dst, send_sem=ss, recv_sem=rs, device_id={"freq": (me_f + d) % nf}, device_id_type=MESH
        )

    def each(low, high, body):
        def step(i, carry):
            body(i)
            return carry

        lax.fori_loop(low, high, step, 0)

    barrier = pltpu.get_barrier_semaphore()
    each(1, nb, lambda t: pl.semaphore_signal(barrier, inc=1, device_id={"base": (me_b + t) % nb}, device_id_type=MESH))
    each(1, nf, lambda d: pl.semaphore_signal(barrier, inc=1, device_id={"freq": (me_f + d) % nf}, device_id_type=MESH))
    pairs = [
        (owner_hbm, owner_ref),
        (row_hbm, row_ref),
        (col_hbm, col_ref),
        (w_hbm, w_ref),
        (left1_hbm, left1),
        (right1_hbm, right1),
        (left2_hbm, left2),
        (right2_hbm, right2),
    ]
    loads = [pltpu.make_async_copy(src, dst, load_sem.at[i]) for i, (src, dst) in enumerate(pairs)]
    for load in loads:
        load.start()

    channels = vr_ref.shape[1]
    chan = (lax.broadcasted_iota(jnp.int32, (8, channels), 1) + me_f * channels).astype(F32)

    def subgrid(i):
        return (me_b + 1 + i // own) % nb * own + i % own

    def prepare(i, tabs):
        tables(subgrid(i), chan, vr_ref, vi_ref, co_ref, *tabs)

    def spot_copy(t):
        return base_copy(spot_ref, table.at[pl.ds(me_b, 1)], spot_s.at[t - 1], spot_r.at[t - 1], t)

    def core_copy(t):
        return freq_copy(part.at[t, 1 - core], got.at[t], core_s.at[t], core_r.at[t], 1 - 2 * core + nf)

    def share_copy(t):
        return base_copy(send.at[t], recv.at[t], base_s.at[t], base_r.at[t], t + 1)

    prepare(0, even)
    for load in loads:
        load.wait()
    lane = lax.broadcasted_iota(jnp.int32, (1, 128), 1)
    spot = jnp.zeros((1, 128), jnp.int32)
    for n, ref in enumerate((owner_ref, row_ref, col_ref)):
        for i in range(own):
            spot = jnp.where(lane == n * own + i, ref[0, i], spot)
    spot_ref[...] = spot
    table[pl.ds(me_b, 1), :] = spot
    c, s = screen(w_ref[0, me_f])
    cs[0] = c
    cs[1] = s

    def choose(o):
        seen = jnp.int32(0)
        index = jnp.int32(0)
        for s in range(own):
            hit = (owner_ref[0, s] == o).astype(jnp.int32)
            index = index + hit * (seen == core).astype(jnp.int32) * s
            seen = seen + hit
        choice[o] = index

    each(0, nb, choose)

    def send_share(t):
        core_copy(t).wait_recv()
        for i in range(half):
            send[t, i] = (part[t, core, i] + got[t, i]).astype(BF16)
        share_copy(t).start()

    def group(t):
        def two(u):
            i = t * own + 2 * u
            prepare(i + 1, odd)
            part[t, 0, u] = products(*even)
            prepare(i + 2, even)
            part[t, 1, u] = products(*odd)

        each(0, 1, two)

        @pl.when(t == 0)
        def _():
            pl.semaphore_wait(barrier, nb + nf - 2)
            each(1, nb, lambda t: spot_copy(t).start())

        @pl.when(t > 0)
        def _():
            send_share(t - 1)

        each(1, half, two)

        core_copy(t).start()

    each(0, nb, group)
    each(0, nb - 1, lambda t: share_copy(t).wait_recv())
    core_copy(nb - 1).wait_recv()

    def sum_shares(i):
        m = part[nb - 1, core, i] + got[nb - 1, i]
        for t in range(nb - 1):
            m = m + recv[t, i].astype(F32)
        return m

    chips = nf // 2

    def sum_copy(d):
        return freq_copy(total.at[(place + d) % chips], fsum.at[d - 1], freq_s.at[d - 1], freq_r.at[d - 1], 2 * d)

    def reduce(d):
        i = (place + d) % chips
        total[i] = sum_shares(i)
        sum_copy(d).start()

    each(1, chips, reduce)
    m = sum_shares(place)
    each(1, chips, lambda d: sum_copy(d).wait_recv())
    for d in range(1, chips):
        m = m + fsum[d - 1]
    patch = make_patch(m, cs[0], cs[1], left1[...], right1[...], left2[...], right2[...])
    gath = (gath0, gath1)
    for chunk in range(CHUNKS):
        gath[chunk][me_f] = patch[chunk * (G // CHUNKS) : (chunk + 1) * (G // CHUNKS)]

    def rows_of(chunk):
        return pl.ds(chunk * (G // CHUNKS), G // CHUNKS)

    def gath_copy(chunk, d):
        piece = gath[chunk].at[me_f]
        return freq_copy(piece, piece, gath_s.at[chunk, d - 1], gath_r.at[chunk, d - 1], d)

    def out_copy(chunk, t):
        return base_copy(
            outb.at[(me_b + t) % nb, rows_of(chunk)],
            slots.at[core, me_b, rows_of(chunk)],
            out_s.at[chunk, t - 1],
            out_r.at[chunk, t - 1],
            t,
        )

    def pair_copy(chunk, t):
        piece = slots.at[core, (me_b + nb - t) % nb, rows_of(chunk)]
        return freq_copy(piece, piece, pair_s.at[chunk, t], pair_r.at[chunk, t], 1 - 2 * core + nf)

    for chunk in range(CHUNKS):
        each(1, nf, lambda d: gath_copy(chunk, d).start())
    for chunk in range(CHUNKS):
        each(1, nf, lambda d: gath_copy(chunk, d).wait_recv())
        rows = rows_of(chunk)

        def ship(t):
            o = (me_b + t) % nb
            outb[o, rows] = gath[chunk][choice[o]]
            out_copy(chunk, t).start()

        each(1, nb, ship)
        slots[core, me_b, rows] = gath[chunk][choice[me_b]]
        pair_copy(chunk, 0).start()
    for chunk in range(CHUNKS):

        def forward(t):
            out_copy(chunk, t).wait_recv()
            pair_copy(chunk, t).start()

        each(1, nb, forward)
    for chunk in range(CHUNKS):
        each(0, nb, lambda t: pair_copy(chunk, t).wait())
        each(1, nb, lambda t: out_copy(chunk, t).wait_send())
        each(1, nf, lambda d: gath_copy(chunk, d).wait_send())
    each(1, chips, lambda d: sum_copy(d).wait_send())
    each(0, nb - 1, lambda t: share_copy(t).wait_send())
    each(0, nb, lambda t: core_copy(t).wait_send())
    each(1, nb, lambda t: spot_copy(t).wait())


def main(owner, row, col, w, vr, vi, co, nb, nf):
    own = w.shape[1]
    unit = (G, 2 * G)
    dma = pltpu.SemaphoreType.DMA
    consts = [stay(jnp.asarray(x)) for x in constants()]
    tabs = [pltpu.VMEM((2 * HALF, 128), F32), pltpu.VMEM((2 * HALF, 128), F32), pltpu.VMEM((16, 256), F32)]
    return pl.pallas_call(
        functools.partial(main_kernel, nb, nf),
        out_shape=(
            jax.ShapeDtypeStruct((FCAP, nb) + unit, F32),
            jax.ShapeDtypeStruct((nb, 128), jnp.int32),
        ),
        in_specs=[hbm()] * 8 + [vmem()] * 3,
        out_specs=(vmem(), vmem()),
        scratch_shapes=[
            pltpu.SMEM((1, own), jnp.int32),
            pltpu.SMEM((1, own), jnp.int32),
            pltpu.SMEM((1, own), jnp.int32),
            pltpu.SMEM((1, own), F32),
        ]
        + [pltpu.VMEM(x.shape, BF16) for x in consts]
        + [pltpu.VMEM((1, 128), jnp.int32)]
        + tabs * 2
        + [
            pltpu.VMEM((2,) + unit, F32),
            pltpu.VMEM((nb, 2, own // 2) + unit, F32),
            pltpu.VMEM((nb, own // 2) + unit, F32),
            pltpu.VMEM((nb - 1, own // 2) + unit, BF16),
            pltpu.VMEM((nb - 1, own // 2) + unit, BF16),
            pltpu.VMEM((own // 2,) + unit, F32),
            pltpu.VMEM((nf // 2 - 1,) + unit, F32),
            pltpu.VMEM((nf, G // CHUNKS, 2 * G), F32),
            pltpu.VMEM((nf, G // CHUNKS, 2 * G), F32),
            pltpu.VMEM((nb,) + unit, F32),
            pltpu.SMEM((nb,), jnp.int32),
            dma((8,)),
            dma((nb,)),
            dma((nb,)),
            dma((nb - 1,)),
            dma((nb - 1,)),
            dma((nb - 1,)),
            dma((nb - 1,)),
            dma((nf // 2 - 1,)),
            dma((nf // 2 - 1,)),
            dma((CHUNKS, nf - 1)),
            dma((CHUNKS, nf - 1)),
            dma((CHUNKS, nb - 1)),
            dma((CHUNKS, nb - 1)),
            dma((CHUNKS, nb)),
            dma((CHUNKS, nb)),
        ],
        compiler_params=pltpu.CompilerParams(
            vmem_limit_bytes=48 << 20, collective_id=0, has_side_effects=True
        ),
        name="main",
    )(owner, row, col, w, *consts, vr, vi, co)


def deposit_kernel(table_ref, slot_ref, grid_in, grid_ref, blocks, where_ref, tile_ref, count_ref, sem):
    del grid_in
    me = lax.axis_index("base")
    tiles = GY // 128

    def reset(i, carry):
        where_ref[i] = -1
        return carry

    lax.fori_loop(0, tiles, reset, 0)
    count_ref[0] = 0
    lane = lax.broadcasted_iota(jnp.int32, (G + 8, 128), 1)

    def block_of(tile):
        @pl.when(where_ref[tile] < 0)
        def _():
            count = count_ref[0]
            where_ref[tile] = count
            tile_ref[count] = tile
            count_ref[0] = count + 1
            blocks[count] = jnp.zeros(blocks.shape[1:], F32)

        return where_ref[tile]

    def place(b, s, rank):
        row = table_ref[b, 8 + s]
        r = pl.ds(pl.multiple_of(row // 8 * 8, 8), G + 8)
        col = table_ref[b, 16 + s]
        tile = col // 128
        c = col % 128
        patch = jnp.concatenate([slot_ref[rank, b], jnp.zeros((8, 2 * G), F32)], axis=0)
        patch = pltpu.roll(patch, row % 8, 0)
        real = pltpu.roll(jnp.where(lane < G, patch, 0.0), c, 1)
        imag = pltpu.roll(jnp.where(lane < G, 0.0, patch), c + G, 1)
        first = block_of(tile)
        blocks[first, 0, r, :] += jnp.where(lane >= c, real, 0.0)
        blocks[first, 1, r, :] += jnp.where(lane >= c, imag, 0.0)

        @pl.when(c > 128 - G)
        def _():
            second = block_of(tile + 1)
            blocks[second, 0, r, :] += jnp.where(lane < c, real, 0.0)
            blocks[second, 1, r, :] += jnp.where(lane < c, imag, 0.0)

    def source(b, carry):
        seen = jnp.int32(0)
        for s in range(8):
            mine = table_ref[b, s] == me

            @pl.when(mine)
            def _():
                place(b, s, seen)

            seen = seen + mine.astype(jnp.int32)
        return carry

    lax.fori_loop(0, table_ref.shape[0], source, 0)
    count = count_ref[0]

    def copy(i):
        cut = pl.ds(pl.multiple_of(tile_ref[i] * 128, 128), 128)
        return pltpu.make_async_copy(blocks.at[i, :, 0:FR, :], grid_ref.at[:, :, cut], sem.at[i])

    def start(i, carry):
        copy(i).start()
        return carry

    def wait(i, carry):
        copy(i).wait()
        return carry

    lax.fori_loop(0, count, start, 0)
    lax.fori_loop(0, count, wait, 0)


def deposit(table, slots, grid):
    most = 2 * slots.shape[0] * slots.shape[1]
    return pl.pallas_call(
        deposit_kernel,
        out_shape=jax.ShapeDtypeStruct((2, FR, GY), F32),
        in_specs=[smem(), vmem(), hbm()],
        out_specs=hbm(),
        scratch_shapes=[
            pltpu.VMEM((most, 2, FR + 8, 128), F32),
            pltpu.SMEM((GY // 128,), jnp.int32),
            pltpu.SMEM((most,), jnp.int32),
            pltpu.SMEM((1,), jnp.int32),
            pltpu.SemaphoreType.DMA((most,)),
        ],
        input_output_aliases={2: 0},
        compiler_params=pltpu.CompilerParams(vmem_limit_bytes=48 << 20),
        name="deposit",
    )(table, slots, grid)


def per_device(visibilities, anchor, drift, target, subgrid_w, facet_owner, row_offset, col_offset):
    nb, nf = lax.axis_size("base"), lax.axis_size("freq")
    target = target.reshape(1, -1)
    vr, vi, co, grid = prep(*[stay(x) for x in (target, visibilities, anchor, drift)])
    small = [stay(x.reshape(1, -1)) for x in (facet_owner, row_offset, col_offset, subgrid_w)]
    slots, table = main(*small, vr, vi, co, nb, nf)
    return deposit(table, slots, grid)


def solution(mesh):
    return jax.shard_map(
        per_device,
        mesh=mesh,
        in_specs=(
            P(None, "base", "freq"),
            P(None, "base"),
            P(None, "base"),
            P("base", None),
            P("base"),
            P("base", None),
            P("base"),
            P("base"),
        ),
        out_specs=P(None, "base", None),
        check_vma=False,
    )
```

```python
import functools
import math

import jax
import jax.numpy as jnp
import numpy as np
from jax import lax
from jax.experimental import pallas as pl
from jax.experimental.pallas import tpu as pltpu
from jax.sharding import PartitionSpec as P

G = 64
GY = 16384
CAP = 8
FCAP = 2
FR = 128
NT = (((1,), (1,)), ((), ()))
F32 = jnp.float32
BF16 = jnp.bfloat16
VMEM = pltpu.MemorySpace.VMEM
SMEM = pltpu.MemorySpace.SMEM


def vmem():
    return pl.BlockSpec(memory_space=VMEM)


def hbm():
    return pl.BlockSpec(memory_space=pltpu.MemorySpace.HBM)


def stay(x):
    return pltpu.with_memory_space_constraint(x, pltpu.MemorySpace.HBM)


def smem():
    return pl.BlockSpec(memory_space=SMEM)


CLEAR = 2048


def prep_kernel(
    target_hbm, vis_hbm, anchor_hbm, drift_hbm, vr_ref, vi_ref, co_ref, grid_ref, target_ref, vis_ref, anchor_ref, drift_ref, zeros, sem, zsem
):
    pairs = [(target_hbm, target_ref), (vis_hbm, vis_ref), (anchor_hbm, anchor_ref), (drift_hbm, drift_ref)]
    loads = [pltpu.make_async_copy(src, dst, sem.at[i]) for i, (src, dst) in enumerate(pairs)]
    for load in loads:
        load.start()
    zeros[...] = jnp.zeros(zeros.shape, F32)
    clears = []
    for q in range(2):
        for j in range(GY // CLEAR):
            part = grid_ref.at[q, :, CLEAR * j : CLEAR * (j + 1)]
            clears.append(pltpu.make_async_copy(zeros, part, zsem.at[len(clears)]))
    for clear in clears:
        clear.start()
    loads[0].wait()
    blocks = target_ref.shape[1]
    groups = blocks // CAP
    target = target_ref[...]
    hits = (lax.broadcasted_iota(jnp.int32, (groups, blocks), 0) == target).astype(F32)
    earlier = lax.broadcasted_iota(jnp.int32, (blocks, blocks), 0) < lax.broadcasted_iota(
        jnp.int32, (blocks, blocks), 1
    )
    before = jnp.dot(hits.astype(BF16), earlier.astype(F32).astype(BF16), preferred_element_type=F32)
    ranking = jnp.sum(before * hits, axis=0, keepdims=True)
    placed = target * CAP + ranking.astype(jnp.int32)
    step = 128
    for load in loads[1:]:
        load.wait()

    def chunk(i, carry):
        start = pl.multiple_of(i * step, step)
        rows = pl.ds(start, step)
        match = lax.broadcasted_iota(jnp.int32, (step, blocks), 0) + start == placed
        pick = match.astype(F32).astype(BF16)
        vr_ref[rows, :] = jnp.dot(pick, vis_ref[0], preferred_element_type=F32)
        vi_ref[rows, :] = jnp.dot(pick, vis_ref[1], preferred_element_type=F32)
        co_ref[rows, 0:2] = lax.dot_general(pick, anchor_ref[...], NT, preferred_element_type=F32)
        co_ref[rows, 2:4] = lax.dot_general(pick, drift_ref[...], NT, preferred_element_type=F32)
        return carry

    lax.fori_loop(0, blocks // step, chunk, 0)
    for clear in clears:
        clear.wait()


def prep(target, visibilities, anchor, drift):
    _, blocks, channels = visibilities.shape
    return pl.pallas_call(
        prep_kernel,
        out_shape=(
            jax.ShapeDtypeStruct((blocks, channels), F32),
            jax.ShapeDtypeStruct((blocks, channels), F32),
            jax.ShapeDtypeStruct((blocks, 4), F32),
            jax.ShapeDtypeStruct((2, FR, GY), F32),
        ),
        in_specs=[hbm()] * 4,
        out_specs=(vmem(), vmem(), vmem(), hbm()),
        scratch_shapes=[
            pltpu.VMEM((1, blocks), jnp.int32),
            pltpu.VMEM(visibilities.shape, BF16),
            pltpu.VMEM(anchor.shape, BF16),
            pltpu.VMEM(drift.shape, BF16),
            pltpu.VMEM((FR, CLEAR), F32),
            pltpu.SemaphoreType.DMA((4,)),
            pltpu.SemaphoreType.DMA((2 * GY // CLEAR,)),
        ],
        compiler_params=pltpu.CompilerParams(vmem_limit_bytes=48 << 20),
        name="prep",
    )(target, visibilities, anchor, drift)


def trig(h):
    z = h * h
    s = 1 / 362880 + z * (-1 / 39916800)
    s = h * (1.0 + z * (-1 / 6 + z * (1 / 120 + z * (-1 / 5040 + z * s))))
    c = -1 / 3628800 + z * (1 / 479001600)
    c = 1.0 + z * (-0.5 + z * (1 / 24 + z * (-1 / 720 + z * (1 / 40320 + z * c))))
    return c, s


HALF = 152


def put(tab, row, v):
    tab[row : row + 8, :] = v[:, :128]
    tab[HALF + row : HALF + row + 8, :] = v[:, 128:]


def base_rows(h, tab):
    c0, s0 = trig(h)
    k1 = 4.0 * c0 * c0 - 2.0
    k2 = k1 * k1 - 2.0
    k4 = k2 * k2 - 2.0
    k8 = k4 * k4 - 2.0
    s8 = (2.0 * s0 * c0) * k1 * k2 * k4
    cp, cc = c0, (k1 - 1.0) * c0
    sp, sc = s0, (k1 + 1.0) * s0
    put(tab, 0, c0)
    put(tab, 64, s0)
    for p in range(1, 8):
        put(tab, 8 * p, cc)
        put(tab, 64 + 8 * p, sc)
        cp, cc = cc, k1 * cc - cp
        sp, sc = sc, k1 * sc - sp
    put(tab, 128, k8)
    put(tab, 136, 0.5 * k8)
    put(tab, 144, s8)
    return c0, s0


def expand(tab, s, h):
    o = HALF * h
    k8 = tab[o + 128 + s : o + 129 + s, :]
    c8 = tab[o + 136 + s : o + 137 + s, :]
    s8 = tab[o + 144 + s : o + 145 + s, :]
    a0 = tab[pl.ds(o + s, 8, stride=8), :]
    b0 = tab[pl.ds(o + 64 + s, 8, stride=8), :]
    a1 = c8 * a0 - s8 * b0
    b1 = c8 * b0 + s8 * a0
    a2 = k8 * a1 - a0
    b2 = k8 * b1 - b0
    a3 = k8 * a2 - a1
    b3 = k8 * b2 - b1
    return jnp.concatenate([a0, a1, a2, a3, b0, b1, b2, b3], axis=0)


def tables(g, chan, vr_ref, vi_ref, co_ref, tx, ty, tv):
    rows = pl.ds(pl.multiple_of(8 * g, 8), 8)
    co = co_ref[rows, :]
    hx = (co[:, 0:1] - 0.5 * G + chan * co[:, 2:3]) * (math.pi / G)
    hy = (co[:, 1:2] - 0.5 * G + chan * co[:, 3:4]) * (math.pi / G)
    cx, sx = base_rows(hx, tx)
    cy, sy = base_rows(hy, ty)
    er = cx * cy - sx * sy
    ei = cx * sy + sx * cy
    vr = vr_ref[rows, :]
    vi = vi_ref[rows, :]
    tv[0:8, :] = vr * er + vi * ei
    tv[8:16, :] = vi * er - vr * ei


def products(tx, ty, tv):
    acc = None
    for s in range(8):
        f = jnp.concatenate([expand(tx, s, h).astype(BF16) for h in (0, 1)], axis=1)
        parts = []
        for h in (0, 1):
            g0 = expand(ty, s, h)
            cut = slice(128 * h, 128 * h + 128)
            both = [g0 * tv[s : s + 1, cut], g0 * tv[8 + s : 9 + s, cut]]
            parts.append(jnp.concatenate(both, axis=0).astype(BF16))
        r = jnp.concatenate(parts, axis=1)
        d = lax.dot_general(f, r, NT, preferred_element_type=F32)
        acc = d if acc is None else acc + d
    return acc


def constants():
    l = np.arange(G) - G // 2 + 0.5
    p = np.arange(G // 2) + 0.5
    same = (np.abs(l)[:, None] == p[None, :]).astype(np.float64)
    a = np.concatenate([same, 0 * same], axis=1)
    b = np.concatenate([0 * same, same * np.sign(l)[:, None]], axis=1)
    turns = 2 * np.pi * ((np.arange(G)[:, None] * np.arange(G)[None, :]) % G) / G
    fr, fi = np.cos(turns), -np.sin(turns)
    left1 = np.concatenate([a, b], axis=0)
    right1 = np.block([[a.T, b.T], [-b.T, a.T]])
    left2 = np.concatenate([fr, fi], axis=0)
    right2 = np.block([[fr, fi], [-fi, fr]]) / G

    def split(x):
        high = x.astype(jnp.bfloat16)
        return high, (x - high.astype(np.float64)).astype(jnp.bfloat16)

    one_l, _ = split(left1)
    one_r, _ = split(right1)
    two_l, two_ll = split(left2)
    two_r, two_rl = split(right2)
    return [
        np.concatenate([one_l, one_l], axis=1),
        np.concatenate([one_r, one_r], axis=0),
        np.concatenate([two_l, two_l, two_ll, 0 * two_l], axis=1),
        np.concatenate([two_r, two_r, two_rl], axis=0),
    ]


def split_rows(x, times, axis):
    high = x.astype(BF16)
    low = (x - high.astype(F32)).astype(BF16)
    return jnp.concatenate(([high, low] + [high] * 2)[:times], axis=axis)


def dot16(a, b):
    return jnp.dot(a, b, preferred_element_type=F32)


def swap(x):
    return pltpu.roll(x, G, 1)


def screen(w):
    row = lax.broadcasted_iota(jnp.int32, (G, 2 * G), 0)
    lane = lax.broadcasted_iota(jnp.int32, (G, 2 * G), 1)
    xl = (row - G // 2).astype(F32) * (2.0 / G)
    xm = (jnp.where(lane < G, lane, lane - G) - G // 2).astype(F32) * (2.0 / G)
    c, s = trig((0.25 * math.pi) * w * (xl * xl + xm * xm))
    for _ in range(2):
        c, s = 2.0 * c * c - 1.0, 2.0 * c * s
    return c, jnp.where(lane < G, -s, s)


def make_patch(m, c, s, left1, right1, left2, right2):
    lane = lax.broadcasted_iota(jnp.int32, (G, 2 * G), 1)
    sign = jnp.where(lane < G, -1.0, 1.0).astype(F32)
    both = dot16(left1, split_rows(m, 2, 0))
    y = both[:G] + sign * swap(both[G:])
    z = dot16(split_rows(y, 2, 1), right1)
    k = z * c + swap(z) * s
    both = dot16(left2, split_rows(k, 4, 0))
    y = both[:G] + sign * swap(both[G:])
    return dot16(split_rows(y, 3, 1), right2)


MESH = pl.DeviceIdType.MESH


def main_kernel(
    nb,
    nf,
    owner_hbm,
    row_hbm,
    col_hbm,
    w_hbm,
    left1_hbm,
    right1_hbm,
    left2_hbm,
    right2_hbm,
    vr_ref,
    vi_ref,
    co_ref,
    slots,
    table,
    owner_ref,
    row_ref,
    col_ref,
    w_ref,
    left1,
    right1,
    left2,
    right2,
    spot_ref,
    tx0,
    ty0,
    tv0,
    tx1,
    ty1,
    tv1,
    cs,
    send,
    recv,
    total,
    fsum,
    gath,
    outb,
    choice,
    load_sem,
    spot_s,
    spot_r,
    base_s,
    base_r,
    freq_s,
    freq_r,
    gath_s,
    gath_r,
    out_s,
    out_r,
    pair_s,
    pair_r,
):
    me_b = lax.axis_index("base")
    me_f = lax.axis_index("freq")
    own = total.shape[0]
    core = me_f % 2
    even = (tx0, ty0, tv0)
    odd = (tx1, ty1, tv1)

    side = math.isqrt(nb)

    def peer(t, sign):
        z = (me_b // side + side + sign * (t % side)) % side
        y = (me_b % side + side + sign * ((t // side + t) % side)) % side
        return z * side + y

    def base_copy(src, dst, ss, rs, t):
        return pltpu.make_async_remote_copy(
            src_ref=src, dst_ref=dst, send_sem=ss, recv_sem=rs, device_id={"base": peer(t, 1)}, device_id_type=MESH
        )

    def freq_copy(src, dst, ss, rs, d):
        return pltpu.make_async_remote_copy(
            src_ref=src, dst_ref=dst, send_sem=ss, recv_sem=rs, device_id={"freq": (me_f + d) % nf}, device_id_type=MESH
        )

    def each(low, high, body):
        def step(i, carry):
            body(i)
            return carry

        lax.fori_loop(low, high, step, 0)

    barrier = pltpu.get_barrier_semaphore()
    each(1, nb, lambda t: pl.semaphore_signal(barrier, inc=1, device_id={"base": (me_b + t) % nb}, device_id_type=MESH))
    each(1, nf, lambda d: pl.semaphore_signal(barrier, inc=1, device_id={"freq": (me_f + d) % nf}, device_id_type=MESH))
    pairs = [
        (owner_hbm, owner_ref),
        (row_hbm, row_ref),
        (col_hbm, col_ref),
        (w_hbm, w_ref),
        (left1_hbm, left1),
        (right1_hbm, right1),
        (left2_hbm, left2),
        (right2_hbm, right2),
    ]
    loads = [pltpu.make_async_copy(src, dst, load_sem.at[i]) for i, (src, dst) in enumerate(pairs)]
    for load in loads:
        load.start()

    channels = vr_ref.shape[1]
    chan = (lax.broadcasted_iota(jnp.int32, (8, channels), 1) + me_f * channels).astype(F32)

    def subgrid(i):
        return peer(i // own + 1, 1) * own + i % own

    def prepare(i, tabs):
        tables(subgrid(i), chan, vr_ref, vi_ref, co_ref, *tabs)

    def spot_copy(t):
        return base_copy(spot_ref, table.at[pl.ds(me_b, 1)], spot_s.at[t - 1], spot_r.at[t - 1], t)

    def share_copy(t):
        return base_copy(send.at[t], recv.at[t], base_s.at[t], base_r.at[t], t + 1)

    prepare(0, even)
    for load in loads:
        load.wait()
    lane = lax.broadcasted_iota(jnp.int32, (1, 128), 1)
    spot = jnp.zeros((1, 128), jnp.int32)
    for n, ref in enumerate((owner_ref, row_ref, col_ref)):
        for i in range(own):
            spot = jnp.where(lane == n * own + i, ref[0, i], spot)
    spot_ref[...] = spot
    table[pl.ds(me_b, 1), :] = spot
    c, s = screen(w_ref[0, me_f])
    cs[0] = c
    cs[1] = s

    def choose(o):
        seen = jnp.int32(0)
        index = jnp.int32(0)
        for s in range(own):
            hit = (owner_ref[0, s] == o).astype(jnp.int32)
            index = index + hit * (seen == core).astype(jnp.int32) * s
            seen = seen + hit
        choice[o] = index

    each(0, nb, choose)

    def group(t):
        def two(u):
            i = t * own + 2 * u
            prepare(i + 1, odd)
            send[t, 2 * u] = products(*even).astype(BF16)
            prepare(i + 2, even)
            send[t, 2 * u + 1] = products(*odd).astype(BF16)

        each(0, own // 2, two)

        @pl.when(t == 0)
        def _():
            pl.semaphore_wait(barrier, nb + nf - 2)
            each(1, nb, lambda t: spot_copy(t).start())

        @pl.when(t < nb - 1)
        def _():
            share_copy(t).start()

    each(0, nb, group)
    each(0, nb - 1, lambda t: share_copy(t).wait_recv())

    def sum_shares(j):
        m = send[nb - 1, j].astype(F32)
        for t in range(nb - 1):
            m = m + recv[t, j].astype(F32)
        return m

    def sum_copy(d):
        return freq_copy(total.at[(me_f + d) % nf], fsum.at[d - 1], freq_s.at[d - 1], freq_r.at[d - 1], d)

    def reduce(d):
        j = (me_f + d) % nf
        total[j] = sum_shares(j)
        sum_copy(d).start()

    each(1, nf, reduce)
    m = sum_shares(me_f)
    each(1, nf, lambda d: sum_copy(d).wait_recv())
    for d in range(1, nf):
        m = m + fsum[d - 1]
    gath[me_f] = make_patch(m, cs[0], cs[1], left1[...], right1[...], left2[...], right2[...])

    def gath_copy(d):
        return freq_copy(gath.at[me_f], gath.at[me_f], gath_s.at[d - 1], gath_r.at[d - 1], d)

    each(1, nf, lambda d: gath_copy(d).start())
    each(1, nf, lambda d: gath_copy(d).wait_recv())

    def out_copy(t):
        return base_copy(outb.at[peer(t, 1)], slots.at[core, me_b], out_s.at[t - 1], out_r.at[t - 1], t)

    def pick(o):
        return gath[choice[o]]

    def ship(t):
        o = peer(t, 1)
        outb[o] = pick(o)
        out_copy(t).start()

    each(1, nb, ship)
    slots[core, me_b] = pick(me_b)

    def pair_copy(t):
        source = peer(t, -1)
        part = slots.at[core, source]
        return pltpu.make_async_remote_copy(
            src_ref=part,
            dst_ref=part,
            send_sem=pair_s.at[t],
            recv_sem=pair_r.at[t],
            device_id={"freq": me_f + 1 - 2 * core},
            device_id_type=MESH,
        )

    pair_copy(0).start()

    def forward(t):
        out_copy(t).wait_recv()
        pair_copy(t).start()

    each(1, nb, forward)
    each(0, nb, lambda t: pair_copy(t).wait())
    each(1, nb, lambda t: out_copy(t).wait_send())
    each(1, nf, lambda d: gath_copy(d).wait_send())
    each(1, nf, lambda d: sum_copy(d).wait_send())
    each(0, nb - 1, lambda t: share_copy(t).wait_send())
    each(1, nb, lambda t: spot_copy(t).wait())


def main(owner, row, col, w, vr, vi, co, nb, nf):
    own = w.shape[1]
    unit = (G, 2 * G)
    dma = pltpu.SemaphoreType.DMA
    consts = [stay(jnp.asarray(x)) for x in constants()]
    tabs = [pltpu.VMEM((2 * HALF, 128), F32), pltpu.VMEM((2 * HALF, 128), F32), pltpu.VMEM((16, 256), F32)]
    return pl.pallas_call(
        functools.partial(main_kernel, nb, nf),
        out_shape=(
            jax.ShapeDtypeStruct((FCAP, nb) + unit, F32),
            jax.ShapeDtypeStruct((nb, 128), jnp.int32),
        ),
        in_specs=[hbm()] * 8 + [vmem()] * 3,
        out_specs=(vmem(), vmem()),
        scratch_shapes=[
            pltpu.SMEM((1, own), jnp.int32),
            pltpu.SMEM((1, own), jnp.int32),
            pltpu.SMEM((1, own), jnp.int32),
            pltpu.SMEM((1, own), F32),
        ]
        + [pltpu.VMEM(x.shape, BF16) for x in consts]
        + [pltpu.VMEM((1, 128), jnp.int32)]
        + tabs * 2
        + [
            pltpu.VMEM((2,) + unit, F32),
            pltpu.VMEM((nb, own) + unit, BF16),
            pltpu.VMEM((nb - 1, own) + unit, BF16),
            pltpu.VMEM((own,) + unit, F32),
            pltpu.VMEM((nf - 1,) + unit, F32),
            pltpu.VMEM((nf,) + unit, F32),
            pltpu.VMEM((nb,) + unit, F32),
            pltpu.SMEM((nb,), jnp.int32),
            dma((8,)),
            dma((nb - 1,)),
            dma((nb - 1,)),
            dma((nb - 1,)),
            dma((nb - 1,)),
            dma((nf - 1,)),
            dma((nf - 1,)),
            dma((nf - 1,)),
            dma((nf - 1,)),
            dma((nb - 1,)),
            dma((nb - 1,)),
            dma((nb,)),
            dma((nb,)),
        ],
        compiler_params=pltpu.CompilerParams(
            vmem_limit_bytes=48 << 20, collective_id=0, has_side_effects=True
        ),
        name="main",
    )(owner, row, col, w, *consts, vr, vi, co)


def deposit_kernel(table_ref, slot_ref, grid_in, grid_ref, blocks, where_ref, tile_ref, count_ref, sem):
    del grid_in
    me = lax.axis_index("base")
    tiles = GY // 128

    def reset(i, carry):
        where_ref[i] = -1
        return carry

    lax.fori_loop(0, tiles, reset, 0)
    count_ref[0] = 0
    lane = lax.broadcasted_iota(jnp.int32, (G + 8, 128), 1)

    def block_of(tile):
        @pl.when(where_ref[tile] < 0)
        def _():
            count = count_ref[0]
            where_ref[tile] = count
            tile_ref[count] = tile
            count_ref[0] = count + 1
            blocks[count] = jnp.zeros(blocks.shape[1:], F32)

        return where_ref[tile]

    def place(b, s, rank):
        row = table_ref[b, 8 + s]
        r = pl.ds(pl.multiple_of(row // 8 * 8, 8), G + 8)
        col = table_ref[b, 16 + s]
        tile = col // 128
        c = col % 128
        patch = jnp.concatenate([slot_ref[rank, b], jnp.zeros((8, 2 * G), F32)], axis=0)
        patch = pltpu.roll(patch, row % 8, 0)
        real = pltpu.roll(jnp.where(lane < G, patch, 0.0), c, 1)
        imag = pltpu.roll(jnp.where(lane < G, 0.0, patch), c + G, 1)
        first = block_of(tile)
        blocks[first, 0, r, :] += jnp.where(lane >= c, real, 0.0)
        blocks[first, 1, r, :] += jnp.where(lane >= c, imag, 0.0)

        @pl.when(c > 128 - G)
        def _():
            second = block_of(tile + 1)
            blocks[second, 0, r, :] += jnp.where(lane < c, real, 0.0)
            blocks[second, 1, r, :] += jnp.where(lane < c, imag, 0.0)

    def source(b, carry):
        seen = jnp.int32(0)
        for s in range(8):
            mine = table_ref[b, s] == me

            @pl.when(mine)
            def _():
                place(b, s, seen)

            seen = seen + mine.astype(jnp.int32)
        return carry

    lax.fori_loop(0, table_ref.shape[0], source, 0)
    count = count_ref[0]

    def copy(i):
        cut = pl.ds(pl.multiple_of(tile_ref[i] * 128, 128), 128)
        return pltpu.make_async_copy(blocks.at[i, :, 0:FR, :], grid_ref.at[:, :, cut], sem.at[i])

    def start(i, carry):
        copy(i).start()
        return carry

    def wait(i, carry):
        copy(i).wait()
        return carry

    lax.fori_loop(0, count, start, 0)
    lax.fori_loop(0, count, wait, 0)


def deposit(table, slots, grid):
    most = 2 * slots.shape[0] * slots.shape[1]
    return pl.pallas_call(
        deposit_kernel,
        out_shape=jax.ShapeDtypeStruct((2, FR, GY), F32),
        in_specs=[smem(), vmem(), hbm()],
        out_specs=hbm(),
        scratch_shapes=[
            pltpu.VMEM((most, 2, FR + 8, 128), F32),
            pltpu.SMEM((GY // 128,), jnp.int32),
            pltpu.SMEM((most,), jnp.int32),
            pltpu.SMEM((1,), jnp.int32),
            pltpu.SemaphoreType.DMA((most,)),
        ],
        input_output_aliases={2: 0},
        compiler_params=pltpu.CompilerParams(vmem_limit_bytes=48 << 20),
        name="deposit",
    )(table, slots, grid)


def per_device(visibilities, anchor, drift, target, subgrid_w, facet_owner, row_offset, col_offset):
    nb, nf = lax.axis_size("base"), lax.axis_size("freq")
    target = target.reshape(1, -1)
    vr, vi, co, grid = prep(*[stay(x) for x in (target, visibilities, anchor, drift)])
    small = [stay(x.reshape(1, -1)) for x in (facet_owner, row_offset, col_offset, subgrid_w)]
    slots, table = main(*small, vr, vi, co, nb, nf)
    return deposit(table, slots, grid)


def solution(mesh):
    return jax.shard_map(
        per_device,
        mesh=mesh,
        in_specs=(
            P(None, "base", "freq"),
            P(None, "base"),
            P(None, "base"),
            P("base", None),
            P("base"),
            P("base", None),
            P("base"),
            P("base"),
        ),
        out_specs=P(None, "base", None),
        check_vma=False,
    )
```

```python
import functools
import math

import jax
import jax.numpy as jnp
import numpy as np
from jax import lax
from jax.experimental import pallas as pl
from jax.experimental.pallas import tpu as pltpu
from jax.sharding import PartitionSpec as P

G = 64
GY = 16384
CAP = 8
FCAP = 2
FR = 128
NT = (((1,), (1,)), ((), ()))
F32 = jnp.float32
BF16 = jnp.bfloat16
VMEM = pltpu.MemorySpace.VMEM
SMEM = pltpu.MemorySpace.SMEM


def vmem():
    return pl.BlockSpec(memory_space=VMEM)


def hbm():
    return pl.BlockSpec(memory_space=pltpu.MemorySpace.HBM)


def stay(x):
    return pltpu.with_memory_space_constraint(x, pltpu.MemorySpace.HBM)


def smem():
    return pl.BlockSpec(memory_space=SMEM)


CLEAR = 2048
PIECES = 2 * GY // CLEAR
EARLY = PIECES - 4


def clear_copy(zeros, grid_ref, sem, i, first):
    j = i % (GY // CLEAR)
    part = grid_ref.at[i // (GY // CLEAR), :, CLEAR * j : CLEAR * (j + 1)]
    return pltpu.make_async_copy(zeros, part, sem.at[i - first])


def prep_kernel(
    target_hbm, vis_hbm, anchor_hbm, drift_hbm, vr_ref, vi_ref, co_ref, grid_ref, target_ref, vis_ref, anchor_ref, drift_ref, zeros, sem, zsem
):
    pairs = [(target_hbm, target_ref), (vis_hbm, vis_ref), (anchor_hbm, anchor_ref), (drift_hbm, drift_ref)]
    loads = [pltpu.make_async_copy(src, dst, sem.at[i]) for i, (src, dst) in enumerate(pairs)]
    for load in loads:
        load.start()
    zeros[...] = jnp.zeros(zeros.shape, F32)
    clears = [clear_copy(zeros, grid_ref, zsem, i, 0) for i in range(EARLY)]
    for clear in clears:
        clear.start()
    loads[0].wait()
    blocks = target_ref.shape[1]
    groups = blocks // CAP
    target = target_ref[...]
    hits = (lax.broadcasted_iota(jnp.int32, (groups, blocks), 0) == target).astype(F32)
    earlier = lax.broadcasted_iota(jnp.int32, (blocks, blocks), 0) < lax.broadcasted_iota(
        jnp.int32, (blocks, blocks), 1
    )
    before = jnp.dot(hits.astype(BF16), earlier.astype(F32).astype(BF16), preferred_element_type=F32)
    ranking = jnp.sum(before * hits, axis=0, keepdims=True)
    placed = target * CAP + ranking.astype(jnp.int32)
    step = 128
    for load in loads[1:]:
        load.wait()

    def chunk(i, carry):
        start = pl.multiple_of(i * step, step)
        rows = pl.ds(start, step)
        match = lax.broadcasted_iota(jnp.int32, (step, blocks), 0) + start == placed
        pick = match.astype(F32).astype(BF16)
        vr_ref[rows, :] = jnp.dot(pick, vis_ref[0], preferred_element_type=F32)
        vi_ref[rows, :] = jnp.dot(pick, vis_ref[1], preferred_element_type=F32)
        co_ref[rows, 0:2] = lax.dot_general(pick, anchor_ref[...], NT, preferred_element_type=F32)
        co_ref[rows, 2:4] = lax.dot_general(pick, drift_ref[...], NT, preferred_element_type=F32)
        return carry

    lax.fori_loop(0, blocks // step, chunk, 0)
    for clear in clears:
        clear.wait()


def prep(target, visibilities, anchor, drift):
    _, blocks, channels = visibilities.shape
    return pl.pallas_call(
        prep_kernel,
        out_shape=(
            jax.ShapeDtypeStruct((blocks, channels), F32),
            jax.ShapeDtypeStruct((blocks, channels), F32),
            jax.ShapeDtypeStruct((blocks, 4), F32),
            jax.ShapeDtypeStruct((2, FR, GY), F32),
        ),
        in_specs=[hbm()] * 4,
        out_specs=(vmem(), vmem(), vmem(), hbm()),
        scratch_shapes=[
            pltpu.VMEM((1, blocks), jnp.int32),
            pltpu.VMEM(visibilities.shape, BF16),
            pltpu.VMEM(anchor.shape, BF16),
            pltpu.VMEM(drift.shape, BF16),
            pltpu.VMEM((FR, CLEAR), F32),
            pltpu.SemaphoreType.DMA((4,)),
            pltpu.SemaphoreType.DMA((EARLY,)),
        ],
        compiler_params=pltpu.CompilerParams(vmem_limit_bytes=48 << 20),
        name="prep",
    )(target, visibilities, anchor, drift)


def trig(h):
    z = h * h
    s = 1 / 362880 + z * (-1 / 39916800)
    s = h * (1.0 + z * (-1 / 6 + z * (1 / 120 + z * (-1 / 5040 + z * s))))
    c = -1 / 3628800 + z * (1 / 479001600)
    c = 1.0 + z * (-0.5 + z * (1 / 24 + z * (-1 / 720 + z * (1 / 40320 + z * c))))
    return c, s


HALF = 152


def put(tab, row, v):
    tab[row : row + 8, :] = v[:, :128]
    tab[HALF + row : HALF + row + 8, :] = v[:, 128:]


def base_rows(h, tab):
    c0, s0 = trig(h)
    k1 = 4.0 * c0 * c0 - 2.0
    k2 = k1 * k1 - 2.0
    k4 = k2 * k2 - 2.0
    k8 = k4 * k4 - 2.0
    s8 = (2.0 * s0 * c0) * k1 * k2 * k4
    cp, cc = c0, (k1 - 1.0) * c0
    sp, sc = s0, (k1 + 1.0) * s0
    put(tab, 0, c0)
    put(tab, 64, s0)
    for p in range(1, 8):
        put(tab, 8 * p, cc)
        put(tab, 64 + 8 * p, sc)
        cp, cc = cc, k1 * cc - cp
        sp, sc = sc, k1 * sc - sp
    put(tab, 128, k8)
    put(tab, 136, 0.5 * k8)
    put(tab, 144, s8)
    return c0, s0


def expand(tab, s, h):
    o = HALF * h
    k8 = tab[o + 128 + s : o + 129 + s, :]
    c8 = tab[o + 136 + s : o + 137 + s, :]
    s8 = tab[o + 144 + s : o + 145 + s, :]
    a0 = tab[pl.ds(o + s, 8, stride=8), :]
    b0 = tab[pl.ds(o + 64 + s, 8, stride=8), :]
    a1 = c8 * a0 - s8 * b0
    b1 = c8 * b0 + s8 * a0
    a2 = k8 * a1 - a0
    b2 = k8 * b1 - b0
    a3 = k8 * a2 - a1
    b3 = k8 * b2 - b1
    return jnp.concatenate([a0, a1, a2, a3, b0, b1, b2, b3], axis=0)


def tables(g, chan, vr_ref, vi_ref, co_ref, tx, ty, tv):
    rows = pl.ds(pl.multiple_of(8 * g, 8), 8)
    co = co_ref[rows, :]
    hx = (co[:, 0:1] - 0.5 * G + chan * co[:, 2:3]) * (math.pi / G)
    hy = (co[:, 1:2] - 0.5 * G + chan * co[:, 3:4]) * (math.pi / G)
    cx, sx = base_rows(hx, tx)
    cy, sy = base_rows(hy, ty)
    er = cx * cy - sx * sy
    ei = cx * sy + sx * cy
    vr = vr_ref[rows, :]
    vi = vi_ref[rows, :]
    tv[0:8, :] = vr * er + vi * ei
    tv[8:16, :] = vi * er - vr * ei


def products(tx, ty, tv):
    acc = None
    for s in range(8):
        f = jnp.concatenate([expand(tx, s, h).astype(BF16) for h in (0, 1)], axis=1)
        parts = []
        for h in (0, 1):
            g0 = expand(ty, s, h)
            cut = slice(128 * h, 128 * h + 128)
            both = [g0 * tv[s : s + 1, cut], g0 * tv[8 + s : 9 + s, cut]]
            parts.append(jnp.concatenate(both, axis=0).astype(BF16))
        r = jnp.concatenate(parts, axis=1)
        d = lax.dot_general(f, r, NT, preferred_element_type=F32)
        acc = d if acc is None else acc + d
    return acc


def constants():
    l = np.arange(G) - G // 2 + 0.5
    p = np.arange(G // 2) + 0.5
    same = (np.abs(l)[:, None] == p[None, :]).astype(np.float64)
    a = np.concatenate([same, 0 * same], axis=1)
    b = np.concatenate([0 * same, same * np.sign(l)[:, None]], axis=1)
    turns = 2 * np.pi * ((np.arange(G)[:, None] * np.arange(G)[None, :]) % G) / G
    fr, fi = np.cos(turns), -np.sin(turns)
    left1 = np.concatenate([a, b], axis=0)
    right1 = np.block([[a.T, b.T], [-b.T, a.T]])
    left2 = np.concatenate([fr, fi], axis=0)
    right2 = np.block([[fr, fi], [-fi, fr]]) / G

    def split(x):
        high = x.astype(jnp.bfloat16)
        return high, (x - high.astype(np.float64)).astype(jnp.bfloat16)

    one_l, _ = split(left1)
    one_r, _ = split(right1)
    two_l, two_ll = split(left2)
    two_r, two_rl = split(right2)
    return [
        np.concatenate([one_l, one_l], axis=1),
        np.concatenate([one_r, one_r], axis=0),
        np.concatenate([two_l, two_l, two_ll, 0 * two_l], axis=1),
        np.concatenate([two_r, two_r, two_rl], axis=0),
    ]


def split_rows(x, times, axis):
    high = x.astype(BF16)
    low = (x - high.astype(F32)).astype(BF16)
    return jnp.concatenate(([high, low] + [high] * 2)[:times], axis=axis)


def dot16(a, b):
    return jnp.dot(a, b, preferred_element_type=F32)


def swap(x):
    return pltpu.roll(x, G, 1)


def screen(w):
    row = lax.broadcasted_iota(jnp.int32, (G, 2 * G), 0)
    lane = lax.broadcasted_iota(jnp.int32, (G, 2 * G), 1)
    xl = (row - G // 2).astype(F32) * (2.0 / G)
    xm = (jnp.where(lane < G, lane, lane - G) - G // 2).astype(F32) * (2.0 / G)
    c, s = trig((0.25 * math.pi) * w * (xl * xl + xm * xm))
    for _ in range(2):
        c, s = 2.0 * c * c - 1.0, 2.0 * c * s
    return c, jnp.where(lane < G, -s, s)


def make_patch(m, c, s, left1, right1, left2, right2):
    lane = lax.broadcasted_iota(jnp.int32, (G, 2 * G), 1)
    sign = jnp.where(lane < G, -1.0, 1.0).astype(F32)
    both = dot16(left1, split_rows(m, 2, 0))
    y = both[:G] + sign * swap(both[G:])
    z = dot16(split_rows(y, 2, 1), right1)
    k = z * c + swap(z) * s
    both = dot16(left2, split_rows(k, 4, 0))
    y = both[:G] + sign * swap(both[G:])
    return dot16(split_rows(y, 3, 1), right2)


MESH = pl.DeviceIdType.MESH


def main_kernel(
    nb,
    nf,
    owner_hbm,
    row_hbm,
    col_hbm,
    w_hbm,
    left1_hbm,
    right1_hbm,
    left2_hbm,
    right2_hbm,
    vr_ref,
    vi_ref,
    co_ref,
    slots,
    table,
    owner_ref,
    row_ref,
    col_ref,
    w_ref,
    left1,
    right1,
    left2,
    right2,
    spot_ref,
    tx0,
    ty0,
    tv0,
    tx1,
    ty1,
    tv1,
    cs,
    send,
    recv,
    total,
    fsum,
    gath,
    outb,
    choice,
    load_sem,
    spot_s,
    spot_r,
    base_s,
    base_r,
    freq_s,
    freq_r,
    gath_s,
    gath_r,
    out_s,
    out_r,
    pair_s,
    pair_r,
):
    me_b = lax.axis_index("base")
    me_f = lax.axis_index("freq")
    own = total.shape[0]
    core = me_f % 2
    even = (tx0, ty0, tv0)
    odd = (tx1, ty1, tv1)

    side = math.isqrt(nb)

    def peer(t, sign):
        z = (me_b // side + side + sign * (t % side)) % side
        y = (me_b % side + side + sign * ((t // side + t) % side)) % side
        return z * side + y

    def base_copy(src, dst, ss, rs, t):
        return pltpu.make_async_remote_copy(
            src_ref=src, dst_ref=dst, send_sem=ss, recv_sem=rs, device_id={"base": peer(t, 1)}, device_id_type=MESH
        )

    def freq_copy(src, dst, ss, rs, d):
        return pltpu.make_async_remote_copy(
            src_ref=src, dst_ref=dst, send_sem=ss, recv_sem=rs, device_id={"freq": (me_f + d) % nf}, device_id_type=MESH
        )

    def each(low, high, body):
        def step(i, carry):
            body(i)
            return carry

        lax.fori_loop(low, high, step, 0)

    barrier = pltpu.get_barrier_semaphore()
    each(1, nb, lambda t: pl.semaphore_signal(barrier, inc=1, device_id={"base": (me_b + t) % nb}, device_id_type=MESH))
    each(1, nf, lambda d: pl.semaphore_signal(barrier, inc=1, device_id={"freq": (me_f + d) % nf}, device_id_type=MESH))
    pairs = [
        (owner_hbm, owner_ref),
        (row_hbm, row_ref),
        (col_hbm, col_ref),
        (w_hbm, w_ref),
        (left1_hbm, left1),
        (right1_hbm, right1),
        (left2_hbm, left2),
        (right2_hbm, right2),
    ]
    loads = [pltpu.make_async_copy(src, dst, load_sem.at[i]) for i, (src, dst) in enumerate(pairs)]
    for load in loads:
        load.start()

    channels = vr_ref.shape[1]
    chan = (lax.broadcasted_iota(jnp.int32, (8, channels), 1) + me_f * channels).astype(F32)

    def subgrid(i):
        return peer(i // own + 1, 1) * own + i % own

    def prepare(i, tabs):
        tables(subgrid(i), chan, vr_ref, vi_ref, co_ref, *tabs)

    def spot_copy(t):
        return base_copy(spot_ref.at[pl.ds(peer(t, 1), 1)], table.at[pl.ds(me_b, 1)], spot_s.at[t - 1], spot_r.at[t - 1], t)

    def share_copy(t):
        return base_copy(send.at[t], recv.at[t], base_s.at[t], base_r.at[t], t + 1)

    prepare(0, even)
    lane = lax.broadcasted_iota(jnp.int32, (1, 128), 1)

    def choose(o):
        seen = jnp.int32(0)
        index = [jnp.int32(0)] * FCAP
        for s in range(own):
            hit = (owner_ref[0, s] == o).astype(jnp.int32)
            index = [index[r] + hit * (seen == r).astype(jnp.int32) * s for r in range(FCAP)]
            seen = seen + hit
        choice[o] = index[0] * (1 - core) + index[1] * core
        spot = jnp.zeros((1, 128), jnp.int32)
        for r in range(FCAP):
            fields = ((seen > r).astype(jnp.int32), row_ref[0, index[r]], col_ref[0, index[r]])
            for n, value in enumerate(fields):
                spot = jnp.where(lane == 3 * r + n, value, spot)
        spot_ref[pl.ds(o, 1), :] = spot

    def small_work():
        for load in loads:
            load.wait()
        c, s = screen(w_ref[0, me_f])
        cs[0] = c
        cs[1] = s
        each(0, nb, choose)
        table[pl.ds(me_b, 1), :] = spot_ref[pl.ds(me_b, 1), :]

    def group(t):
        def two(u):
            i = t * own + 2 * u
            prepare(i + 1, odd)
            send[t, 2 * u] = products(*even).astype(BF16)
            prepare(i + 2, even)
            send[t, 2 * u + 1] = products(*odd).astype(BF16)

        each(0, own // 2, two)

        @pl.when(t == 0)
        def _():
            pl.semaphore_wait(barrier, nb + nf - 2)

        @pl.when(t < nb - 1)
        def _():
            share_copy(t).start()

        @pl.when(t == 0)
        def _():
            small_work()
            each(1, nb, lambda t: spot_copy(t).start())

    each(0, nb, group)
    each(0, nb - 1, lambda t: share_copy(t).wait_recv())

    def sum_shares(j):
        m = send[nb - 1, j].astype(F32)
        for t in range(nb - 1):
            m = m + recv[t, j].astype(F32)
        return m

    def sum_copy(d):
        return freq_copy(total.at[(me_f + d) % nf], fsum.at[d - 1], freq_s.at[d - 1], freq_r.at[d - 1], d)

    def reduce(d):
        j = (me_f + d) % nf
        total[j] = sum_shares(j)
        sum_copy(d).start()

    each(1, nf, reduce)
    m = sum_shares(me_f)
    each(1, nf, lambda d: sum_copy(d).wait_recv())
    for d in range(1, nf):
        m = m + fsum[d - 1]
    gath[me_f] = make_patch(m, cs[0], cs[1], left1[...], right1[...], left2[...], right2[...])

    def gath_copy(d):
        return freq_copy(gath.at[me_f], gath.at[me_f], gath_s.at[d - 1], gath_r.at[d - 1], d)

    each(1, nf, lambda d: gath_copy(d).start())
    each(1, nf, lambda d: gath_copy(d).wait_recv())

    def out_copy(t):
        return base_copy(outb.at[peer(t, 1)], slots.at[core, me_b], out_s.at[t - 1], out_r.at[t - 1], t)

    def pick(o):
        return gath[choice[o]]

    def ship(t):
        o = peer(t, 1)
        outb[o] = pick(o)
        out_copy(t).start()

    each(1, nb, ship)
    slots[core, me_b] = pick(me_b)

    def pair_copy(t):
        source = peer(t, -1)
        part = slots.at[core, source]
        return pltpu.make_async_remote_copy(
            src_ref=part,
            dst_ref=part,
            send_sem=pair_s.at[t],
            recv_sem=pair_r.at[t],
            device_id={"freq": me_f + 1 - 2 * core},
            device_id_type=MESH,
        )

    pair_copy(0).start()

    def forward(t):
        out_copy(t).wait_recv()
        pair_copy(t).start()

    each(1, nb, forward)
    each(0, nb, lambda t: pair_copy(t).wait())
    each(1, nb, lambda t: out_copy(t).wait_send())
    each(1, nf, lambda d: gath_copy(d).wait_send())
    each(1, nf, lambda d: sum_copy(d).wait_send())
    each(0, nb - 1, lambda t: share_copy(t).wait_send())
    each(1, nb, lambda t: spot_copy(t).wait())


def main(owner, row, col, w, vr, vi, co, nb, nf):
    own = w.shape[1]
    unit = (G, 2 * G)
    dma = pltpu.SemaphoreType.DMA
    consts = [stay(jnp.asarray(x)) for x in constants()]
    tabs = [pltpu.VMEM((2 * HALF, 128), F32), pltpu.VMEM((2 * HALF, 128), F32), pltpu.VMEM((16, 256), F32)]
    return pl.pallas_call(
        functools.partial(main_kernel, nb, nf),
        out_shape=(
            jax.ShapeDtypeStruct((FCAP, nb) + unit, F32),
            jax.ShapeDtypeStruct((nb, 128), jnp.int32),
        ),
        in_specs=[hbm()] * 8 + [vmem()] * 3,
        out_specs=(vmem(), vmem()),
        scratch_shapes=[
            pltpu.SMEM((1, own), jnp.int32),
            pltpu.SMEM((1, own), jnp.int32),
            pltpu.SMEM((1, own), jnp.int32),
            pltpu.SMEM((1, own), F32),
        ]
        + [pltpu.VMEM(x.shape, BF16) for x in consts]
        + [pltpu.VMEM((nb, 128), jnp.int32)]
        + tabs * 2
        + [
            pltpu.VMEM((2,) + unit, F32),
            pltpu.VMEM((nb, own) + unit, BF16),
            pltpu.VMEM((nb - 1, own) + unit, BF16),
            pltpu.VMEM((own,) + unit, F32),
            pltpu.VMEM((nf - 1,) + unit, F32),
            pltpu.VMEM((nf,) + unit, F32),
            pltpu.VMEM((nb,) + unit, F32),
            pltpu.SMEM((nb,), jnp.int32),
            dma((8,)),
            dma((nb - 1,)),
            dma((nb - 1,)),
            dma((nb - 1,)),
            dma((nb - 1,)),
            dma((nf - 1,)),
            dma((nf - 1,)),
            dma((nf - 1,)),
            dma((nf - 1,)),
            dma((nb - 1,)),
            dma((nb - 1,)),
            dma((nb,)),
            dma((nb,)),
        ],
        compiler_params=pltpu.CompilerParams(
            vmem_limit_bytes=48 << 20, collective_id=0, has_side_effects=True
        ),
        name="main",
    )(owner, row, col, w, *consts, vr, vi, co)


def deposit_kernel(table_ref, slot_ref, grid_in, grid_ref, zeros, blocks, where_ref, tile_ref, count_ref, sem, zsem):
    del grid_in
    zeros[...] = jnp.zeros(zeros.shape, F32)
    clears = [clear_copy(zeros, grid_ref, zsem, i, EARLY) for i in range(EARLY, PIECES)]
    for clear in clears:
        clear.start()
    tiles = GY // 128

    def reset(i, carry):
        where_ref[i] = -1
        return carry

    lax.fori_loop(0, tiles, reset, 0)
    count_ref[0] = 0
    lane = lax.broadcasted_iota(jnp.int32, (G + 8, 128), 1)

    def block_of(tile):
        @pl.when(where_ref[tile] < 0)
        def _():
            count = count_ref[0]
            where_ref[tile] = count
            tile_ref[count] = tile
            count_ref[0] = count + 1
            blocks[count] = jnp.zeros(blocks.shape[1:], F32)

        return where_ref[tile]

    def place(b, rank):
        row = table_ref[b, 3 * rank + 1]
        r = pl.ds(pl.multiple_of(row // 8 * 8, 8), G + 8)
        col = table_ref[b, 3 * rank + 2]
        tile = col // 128
        c = col % 128
        patch = jnp.concatenate([slot_ref[rank, b], jnp.zeros((8, 2 * G), F32)], axis=0)
        patch = pltpu.roll(patch, row % 8, 0)
        real = pltpu.roll(jnp.where(lane < G, patch, 0.0), c, 1)
        imag = pltpu.roll(jnp.where(lane < G, 0.0, patch), c + G, 1)
        first = block_of(tile)
        blocks[first, 0, r, :] += jnp.where(lane >= c, real, 0.0)
        blocks[first, 1, r, :] += jnp.where(lane >= c, imag, 0.0)

        @pl.when(c > 128 - G)
        def _():
            second = block_of(tile + 1)
            blocks[second, 0, r, :] += jnp.where(lane < c, real, 0.0)
            blocks[second, 1, r, :] += jnp.where(lane < c, imag, 0.0)

    def source(b, carry):
        for rank in range(FCAP):

            @pl.when(table_ref[b, 3 * rank] > 0)
            def _():
                place(b, rank)

        return carry

    lax.fori_loop(0, table_ref.shape[0], source, 0)
    count = count_ref[0]

    def copy(i):
        cut = pl.ds(pl.multiple_of(tile_ref[i] * 128, 128), 128)
        return pltpu.make_async_copy(blocks.at[i, :, 0:FR, :], grid_ref.at[:, :, cut], sem.at[i])

    def start(i, carry):
        copy(i).start()
        return carry

    def wait(i, carry):
        copy(i).wait()
        return carry

    for clear in clears:
        clear.wait()
    lax.fori_loop(0, count, start, 0)
    lax.fori_loop(0, count, wait, 0)


def deposit(table, slots, grid):
    most = 2 * slots.shape[0] * slots.shape[1]
    return pl.pallas_call(
        deposit_kernel,
        out_shape=jax.ShapeDtypeStruct((2, FR, GY), F32),
        in_specs=[smem(), vmem(), hbm()],
        out_specs=hbm(),
        scratch_shapes=[
            pltpu.VMEM((FR, CLEAR), F32),
            pltpu.VMEM((most, 2, FR + 8, 128), F32),
            pltpu.SMEM((GY // 128,), jnp.int32),
            pltpu.SMEM((most,), jnp.int32),
            pltpu.SMEM((1,), jnp.int32),
            pltpu.SemaphoreType.DMA((most,)),
            pltpu.SemaphoreType.DMA((PIECES - EARLY,)),
        ],
        input_output_aliases={2: 0},
        compiler_params=pltpu.CompilerParams(vmem_limit_bytes=48 << 20),
        name="deposit",
    )(table, slots, grid)


def per_device(visibilities, anchor, drift, target, subgrid_w, facet_owner, row_offset, col_offset):
    nb, nf = lax.axis_size("base"), lax.axis_size("freq")
    target = target.reshape(1, -1)
    vr, vi, co, grid = prep(*[stay(x) for x in (target, visibilities, anchor, drift)])
    small = [stay(x.reshape(1, -1)) for x in (facet_owner, row_offset, col_offset, subgrid_w)]
    slots, table = main(*small, vr, vi, co, nb, nf)
    return deposit(table, slots, grid)


def solution(mesh):
    return jax.shard_map(
        per_device,
        mesh=mesh,
        in_specs=(
            P(None, "base", "freq"),
            P(None, "base"),
            P(None, "base"),
            P("base", None),
            P("base"),
            P("base", None),
            P("base"),
            P("base"),
        ),
        out_specs=P(None, "base", None),
        check_vma=False,
    )
```

```python
import functools
import math

import jax
import jax.numpy as jnp
import numpy as np
from jax import lax
from jax.experimental import pallas as pl
from jax.experimental.pallas import tpu as pltpu
from jax.sharding import PartitionSpec as P

G = 64
GY = 16384
CAP = 8
FCAP = 2
FR = 128
NT = (((1,), (1,)), ((), ()))
F32 = jnp.float32
BF16 = jnp.bfloat16
VMEM = pltpu.MemorySpace.VMEM
SMEM = pltpu.MemorySpace.SMEM


def vmem():
    return pl.BlockSpec(memory_space=VMEM)


def hbm():
    return pl.BlockSpec(memory_space=pltpu.MemorySpace.HBM)


def stay(x):
    return pltpu.with_memory_space_constraint(x, pltpu.MemorySpace.HBM)


def smem():
    return pl.BlockSpec(memory_space=SMEM)


CLEAR = 2048
PIECES = 2 * GY // CLEAR
EARLY = PIECES - 4


def clear_copy(zeros, grid_ref, sem, i, first):
    j = i % (GY // CLEAR)
    part = grid_ref.at[i // (GY // CLEAR), :, CLEAR * j : CLEAR * (j + 1)]
    return pltpu.make_async_copy(zeros, part, sem.at[i - first])


def prep_kernel(
    target_hbm, vis_hbm, anchor_hbm, drift_hbm, vr_ref, vi_ref, co_ref, grid_ref, target_ref, vis_ref, anchor_ref, drift_ref, pick_ref, zeros, sem, zsem
):
    pairs = [(target_hbm, target_ref), (vis_hbm, vis_ref), (anchor_hbm, anchor_ref), (drift_hbm, drift_ref)]
    loads = [pltpu.make_async_copy(src, dst, sem.at[i]) for i, (src, dst) in enumerate(pairs)]
    for load in loads:
        load.start()
    zeros[...] = jnp.zeros(zeros.shape, F32)
    clears = [clear_copy(zeros, grid_ref, zsem, i, 0) for i in range(EARLY)]
    for clear in clears:
        clear.start()
    loads[0].wait()
    blocks = target_ref.shape[1]
    groups = blocks // CAP
    width = 128
    rows = lax.broadcasted_iota(jnp.int32, (width, width), 0)
    lanes = lax.broadcasted_iota(jnp.int32, (width, width), 1)
    count = jnp.concatenate([(rows < lanes).astype(F32), jnp.ones((width, width), F32)], axis=1)
    ids = lax.broadcasted_iota(jnp.int32, (groups, width), 0)
    pieces = range(blocks // width)
    targets = [target_ref[:, width * i : width * (i + 1)] for i in pieces]
    hits = [(ids == target).astype(F32) for target in targets]
    counts = jnp.dot(
        jnp.concatenate(hits, axis=0).astype(BF16), count.astype(BF16), preferred_element_type=F32
    )
    seen = jnp.zeros((groups, width), F32)
    placed = []
    for i in pieces:
        inside = counts[groups * i : groups * (i + 1)]
        ranking = jnp.sum((inside[:, :width] + seen) * hits[i], axis=0, keepdims=True)
        placed.append(targets[i] * CAP + ranking.astype(jnp.int32))
        seen = seen + inside[:, width:]
    placed = jnp.concatenate(placed, axis=1)
    step = 128

    def choose(i, carry):
        start = pl.multiple_of(i * step, step)
        match = lax.broadcasted_iota(jnp.int32, (step, blocks), 0) + start == placed
        pick_ref[pl.ds(start, step), :] = match.astype(F32).astype(BF16)
        return carry

    lax.fori_loop(0, blocks // step, choose, 0)
    for load in loads[1:]:
        load.wait()
    pick = pick_ref[...]
    places = jnp.concatenate([anchor_ref[...].astype(F32), drift_ref[...].astype(F32)], axis=0).astype(BF16)
    co_ref[...] = lax.dot_general(pick, places, NT, preferred_element_type=F32)
    vr_ref[...] = jnp.dot(pick, vis_ref[0], preferred_element_type=F32)
    vi_ref[...] = jnp.dot(pick, vis_ref[1], preferred_element_type=F32)
    for clear in clears:
        clear.wait()


def prep(target, visibilities, anchor, drift):
    _, blocks, channels = visibilities.shape
    return pl.pallas_call(
        prep_kernel,
        out_shape=(
            jax.ShapeDtypeStruct((blocks, channels), F32),
            jax.ShapeDtypeStruct((blocks, channels), F32),
            jax.ShapeDtypeStruct((blocks, 4), F32),
            jax.ShapeDtypeStruct((2, FR, GY), F32),
        ),
        in_specs=[hbm()] * 4,
        out_specs=(vmem(), vmem(), vmem(), hbm()),
        scratch_shapes=[
            pltpu.VMEM((1, blocks), jnp.int32),
            pltpu.VMEM(visibilities.shape, BF16),
            pltpu.VMEM(anchor.shape, BF16),
            pltpu.VMEM(drift.shape, BF16),
            pltpu.VMEM((blocks, blocks), BF16),
            pltpu.VMEM((FR, CLEAR), F32),
            pltpu.SemaphoreType.DMA((4,)),
            pltpu.SemaphoreType.DMA((EARLY,)),
        ],
        compiler_params=pltpu.CompilerParams(vmem_limit_bytes=48 << 20),
        name="prep",
    )(target, visibilities, anchor, drift)


def trig(h):
    z = h * h
    s = 1 / 362880 + z * (-1 / 39916800)
    s = h * (1.0 + z * (-1 / 6 + z * (1 / 120 + z * (-1 / 5040 + z * s))))
    c = -1 / 3628800 + z * (1 / 479001600)
    c = 1.0 + z * (-0.5 + z * (1 / 24 + z * (-1 / 720 + z * (1 / 40320 + z * c))))
    return c, s


HALF = 152


def put(tab, row, v):
    tab[row : row + 8, :] = v[:, :128]
    tab[HALF + row : HALF + row + 8, :] = v[:, 128:]


def base_rows(h, tab):
    c0, s0 = trig(h)
    k1 = 4.0 * c0 * c0 - 2.0
    k2 = k1 * k1 - 2.0
    k4 = k2 * k2 - 2.0
    k8 = k4 * k4 - 2.0
    s8 = (2.0 * s0 * c0) * k1 * k2 * k4
    cp, cc = c0, (k1 - 1.0) * c0
    sp, sc = s0, (k1 + 1.0) * s0
    put(tab, 0, c0)
    put(tab, 64, s0)
    for p in range(1, 8):
        put(tab, 8 * p, cc)
        put(tab, 64 + 8 * p, sc)
        cp, cc = cc, k1 * cc - cp
        sp, sc = sc, k1 * sc - sp
    put(tab, 128, k8)
    put(tab, 136, 0.5 * k8)
    put(tab, 144, s8)
    return c0, s0


def expand(tab, s, h):
    o = HALF * h
    k8 = tab[o + 128 + s : o + 129 + s, :]
    c8 = tab[o + 136 + s : o + 137 + s, :]
    s8 = tab[o + 144 + s : o + 145 + s, :]
    a0 = tab[pl.ds(o + s, 8, stride=8), :]
    b0 = tab[pl.ds(o + 64 + s, 8, stride=8), :]
    a1 = c8 * a0 - s8 * b0
    b1 = c8 * b0 + s8 * a0
    a2 = k8 * a1 - a0
    b2 = k8 * b1 - b0
    a3 = k8 * a2 - a1
    b3 = k8 * b2 - b1
    return jnp.concatenate([a0, a1, a2, a3, b0, b1, b2, b3], axis=0)


def tables(g, chan, vr_ref, vi_ref, co_ref, tx, ty, tv):
    rows = pl.ds(pl.multiple_of(8 * g, 8), 8)
    co = co_ref[rows, :]
    hx = (co[:, 0:1] - 0.5 * G + chan * co[:, 2:3]) * (math.pi / G)
    hy = (co[:, 1:2] - 0.5 * G + chan * co[:, 3:4]) * (math.pi / G)
    cx, sx = base_rows(hx, tx)
    cy, sy = base_rows(hy, ty)
    er = cx * cy - sx * sy
    ei = cx * sy + sx * cy
    vr = vr_ref[rows, :]
    vi = vi_ref[rows, :]
    tv[0:8, :] = vr * er + vi * ei
    tv[8:16, :] = vi * er - vr * ei


def products(tx, ty, tv):
    acc = None
    for s in range(8):
        f = jnp.concatenate([expand(tx, s, h).astype(BF16) for h in (0, 1)], axis=1)
        parts = []
        for h in (0, 1):
            g0 = expand(ty, s, h)
            cut = slice(128 * h, 128 * h + 128)
            both = [g0 * tv[s : s + 1, cut], g0 * tv[8 + s : 9 + s, cut]]
            parts.append(jnp.concatenate(both, axis=0).astype(BF16))
        r = jnp.concatenate(parts, axis=1)
        d = lax.dot_general(f, r, NT, preferred_element_type=F32)
        acc = d if acc is None else acc + d
    return acc


def constants():
    l = np.arange(G) - G // 2 + 0.5
    p = np.arange(G // 2) + 0.5
    same = (np.abs(l)[:, None] == p[None, :]).astype(np.float64)
    a = np.concatenate([same, 0 * same], axis=1)
    b = np.concatenate([0 * same, same * np.sign(l)[:, None]], axis=1)
    turns = 2 * np.pi * ((np.arange(G)[:, None] * np.arange(G)[None, :]) % G) / G
    fr, fi = np.cos(turns), -np.sin(turns)
    left1 = np.concatenate([a, b], axis=0)
    right1 = np.block([[a.T, b.T], [-b.T, a.T]])
    left2 = np.concatenate([fr, fi], axis=0)
    right2 = np.block([[fr, fi], [-fi, fr]]) / G

    def split(x):
        high = x.astype(jnp.bfloat16)
        return high, (x - high.astype(np.float64)).astype(jnp.bfloat16)

    one_l, _ = split(left1)
    one_r, _ = split(right1)
    two_l, two_ll = split(left2)
    two_r, two_rl = split(right2)
    return [
        np.concatenate([one_l, one_l], axis=1),
        np.concatenate([one_r, one_r], axis=0),
        np.concatenate([two_l, two_l, two_ll, 0 * two_l], axis=1),
        np.concatenate([two_r, two_r, two_rl], axis=0),
    ]


def split_rows(x, times, axis):
    high = x.astype(BF16)
    low = (x - high.astype(F32)).astype(BF16)
    return jnp.concatenate(([high, low] + [high] * 2)[:times], axis=axis)


def dot16(a, b):
    return jnp.dot(a, b, preferred_element_type=F32)


def swap(x):
    return pltpu.roll(x, G, 1)


def screen(w):
    row = lax.broadcasted_iota(jnp.int32, (G, 2 * G), 0)
    lane = lax.broadcasted_iota(jnp.int32, (G, 2 * G), 1)
    xl = (row - G // 2).astype(F32) * (2.0 / G)
    xm = (jnp.where(lane < G, lane, lane - G) - G // 2).astype(F32) * (2.0 / G)
    c, s = trig((0.25 * math.pi) * w * (xl * xl + xm * xm))
    for _ in range(2):
        c, s = 2.0 * c * c - 1.0, 2.0 * c * s
    return c, jnp.where(lane < G, -s, s)


def make_patch(m, c, s, left1, right1, left2, right2):
    lane = lax.broadcasted_iota(jnp.int32, (G, 2 * G), 1)
    sign = jnp.where(lane < G, -1.0, 1.0).astype(F32)
    both = dot16(left1, split_rows(m, 2, 0))
    y = both[:G] + sign * swap(both[G:])
    z = dot16(split_rows(y, 2, 1), right1)
    k = z * c + swap(z) * s
    both = dot16(left2, split_rows(k, 4, 0))
    y = both[:G] + sign * swap(both[G:])
    return dot16(split_rows(y, 3, 1), right2)


MESH = pl.DeviceIdType.MESH


def main_kernel(
    nb,
    nf,
    owner_hbm,
    row_hbm,
    col_hbm,
    w_hbm,
    left1_hbm,
    right1_hbm,
    left2_hbm,
    right2_hbm,
    vr_ref,
    vi_ref,
    co_ref,
    slots,
    table,
    owner_ref,
    row_ref,
    col_ref,
    w_ref,
    left1,
    right1,
    left2,
    right2,
    spot_ref,
    tx0,
    ty0,
    tv0,
    tx1,
    ty1,
    tv1,
    cs,
    send,
    recv,
    total,
    fsum,
    gath,
    outb,
    choice,
    load_sem,
    spot_s,
    spot_r,
    base_s,
    base_r,
    freq_s,
    freq_r,
    gath_s,
    gath_r,
    out_s,
    out_r,
    pair_s,
    pair_r,
):
    me_b = lax.axis_index("base")
    me_f = lax.axis_index("freq")
    own = total.shape[0]
    core = me_f % 2
    even = (tx0, ty0, tv0)
    odd = (tx1, ty1, tv1)

    side = math.isqrt(nb)

    def peer(t, sign):
        z = (me_b // side + side + sign * (t % side)) % side
        y = (me_b % side + side + sign * ((t // side + t) % side)) % side
        return z * side + y

    def base_copy(src, dst, ss, rs, t):
        return pltpu.make_async_remote_copy(
            src_ref=src, dst_ref=dst, send_sem=ss, recv_sem=rs, device_id={"base": peer(t, 1)}, device_id_type=MESH
        )

    def freq_copy(src, dst, ss, rs, d):
        return pltpu.make_async_remote_copy(
            src_ref=src, dst_ref=dst, send_sem=ss, recv_sem=rs, device_id={"freq": (me_f + d) % nf}, device_id_type=MESH
        )

    def each(low, high, body):
        def step(i, carry):
            body(i)
            return carry

        lax.fori_loop(low, high, step, 0)

    barrier = pltpu.get_barrier_semaphore()
    each(1, nb, lambda t: pl.semaphore_signal(barrier, inc=1, device_id={"base": (me_b + t) % nb}, device_id_type=MESH))
    each(1, nf, lambda d: pl.semaphore_signal(barrier, inc=1, device_id={"freq": (me_f + d) % nf}, device_id_type=MESH))
    pairs = [
        (owner_hbm, owner_ref),
        (row_hbm, row_ref),
        (col_hbm, col_ref),
        (w_hbm, w_ref),
        (left1_hbm, left1),
        (right1_hbm, right1),
        (left2_hbm, left2),
        (right2_hbm, right2),
    ]
    loads = [pltpu.make_async_copy(src, dst, load_sem.at[i]) for i, (src, dst) in enumerate(pairs)]
    for load in loads:
        load.start()

    channels = vr_ref.shape[1]
    chan = (lax.broadcasted_iota(jnp.int32, (8, channels), 1) + me_f * channels).astype(F32)

    def subgrid(i):
        return peer(i // own + 1, 1) * own + i % own

    def prepare(i, tabs):
        tables(subgrid(i), chan, vr_ref, vi_ref, co_ref, *tabs)

    def spot_copy(t):
        return base_copy(spot_ref.at[pl.ds(peer(t, 1), 1)], table.at[pl.ds(me_b, 1)], spot_s.at[t - 1], spot_r.at[t - 1], t)

    def share_copy(t):
        return base_copy(send.at[t], recv.at[t], base_s.at[t], base_r.at[t], t + 1)

    prepare(0, even)
    lane = lax.broadcasted_iota(jnp.int32, (1, 128), 1)

    def choose(o):
        seen = jnp.int32(0)
        index = [jnp.int32(0)] * FCAP
        for s in range(own):
            hit = (owner_ref[0, s] == o).astype(jnp.int32)
            index = [index[r] + hit * (seen == r).astype(jnp.int32) * s for r in range(FCAP)]
            seen = seen + hit
        choice[o] = index[0] * (1 - core) + index[1] * core
        spot = jnp.zeros((1, 128), jnp.int32)
        for r in range(FCAP):
            fields = ((seen > r).astype(jnp.int32), row_ref[0, index[r]], col_ref[0, index[r]])
            for n, value in enumerate(fields):
                spot = jnp.where(lane == 3 * r + n, value, spot)
        spot_ref[pl.ds(o, 1), :] = spot

    def small_work():
        for load in loads:
            load.wait()
        c, s = screen(w_ref[0, me_f])
        cs[0] = c
        cs[1] = s
        each(0, nb, choose)
        table[pl.ds(me_b, 1), :] = spot_ref[pl.ds(me_b, 1), :]

    def group(t):
        def two(u):
            i = t * own + 2 * u
            prepare(i + 1, odd)
            send[t, 2 * u] = products(*even).astype(BF16)
            prepare(i + 2, even)
            send[t, 2 * u + 1] = products(*odd).astype(BF16)

        each(0, own // 2, two)

        @pl.when(t == 0)
        def _():
            pl.semaphore_wait(barrier, nb + nf - 2)

        @pl.when(t < nb - 1)
        def _():
            share_copy(t).start()

        @pl.when(t == 0)
        def _():
            small_work()
            each(1, nb, lambda t: spot_copy(t).start())

    each(0, nb, group)
    each(0, nb - 1, lambda t: share_copy(t).wait_recv())

    def sum_shares(j):
        m = send[nb - 1, j].astype(F32)
        for t in range(nb - 1):
            m = m + recv[t, j].astype(F32)
        return m

    def sum_copy(d):
        return freq_copy(total.at[(me_f + d) % nf], fsum.at[d - 1], freq_s.at[d - 1], freq_r.at[d - 1], d)

    def reduce(d):
        j = (me_f + d) % nf
        total[j] = sum_shares(j)
        sum_copy(d).start()

    each(1, nf, reduce)
    m = sum_shares(me_f)
    each(1, nf, lambda d: sum_copy(d).wait_recv())
    for d in range(1, nf):
        m = m + fsum[d - 1]
    gath[me_f] = make_patch(m, cs[0], cs[1], left1[...], right1[...], left2[...], right2[...])

    def gath_copy(d):
        return freq_copy(gath.at[me_f], gath.at[me_f], gath_s.at[d - 1], gath_r.at[d - 1], d)

    each(1, nf, lambda d: gath_copy(d).start())
    each(1, nf, lambda d: gath_copy(d).wait_recv())

    def out_copy(t):
        return base_copy(outb.at[peer(t, 1)], slots.at[core, me_b], out_s.at[t - 1], out_r.at[t - 1], t)

    def pick(o):
        return gath[choice[o]]

    def ship(t):
        o = peer(t, 1)
        outb[o] = pick(o)
        out_copy(t).start()

    each(1, nb, ship)
    slots[core, me_b] = pick(me_b)

    def pair_copy(t):
        source = peer(t, -1)
        part = slots.at[core, source]
        return pltpu.make_async_remote_copy(
            src_ref=part,
            dst_ref=part,
            send_sem=pair_s.at[t],
            recv_sem=pair_r.at[t],
            device_id={"freq": me_f + 1 - 2 * core},
            device_id_type=MESH,
        )

    pair_copy(0).start()

    def forward(t):
        out_copy(t).wait_recv()
        pair_copy(t).start()

    each(1, nb, forward)
    each(0, nb, lambda t: pair_copy(t).wait())
    each(1, nb, lambda t: out_copy(t).wait_send())
    each(1, nf, lambda d: gath_copy(d).wait_send())
    each(1, nf, lambda d: sum_copy(d).wait_send())
    each(0, nb - 1, lambda t: share_copy(t).wait_send())
    each(1, nb, lambda t: spot_copy(t).wait())


def main(owner, row, col, w, vr, vi, co, nb, nf):
    own = w.shape[1]
    unit = (G, 2 * G)
    dma = pltpu.SemaphoreType.DMA
    consts = [stay(jnp.asarray(x)) for x in constants()]
    tabs = [pltpu.VMEM((2 * HALF, 128), F32), pltpu.VMEM((2 * HALF, 128), F32), pltpu.VMEM((16, 256), F32)]
    return pl.pallas_call(
        functools.partial(main_kernel, nb, nf),
        out_shape=(
            jax.ShapeDtypeStruct((FCAP, nb) + unit, F32),
            jax.ShapeDtypeStruct((nb, 128), jnp.int32),
        ),
        in_specs=[hbm()] * 8 + [vmem()] * 3,
        out_specs=(vmem(), vmem()),
        scratch_shapes=[
            pltpu.SMEM((1, own), jnp.int32),
            pltpu.SMEM((1, own), jnp.int32),
            pltpu.SMEM((1, own), jnp.int32),
            pltpu.SMEM((1, own), F32),
        ]
        + [pltpu.VMEM(x.shape, BF16) for x in consts]
        + [pltpu.VMEM((nb, 128), jnp.int32)]
        + tabs * 2
        + [
            pltpu.VMEM((2,) + unit, F32),
            pltpu.VMEM((nb, own) + unit, BF16),
            pltpu.VMEM((nb - 1, own) + unit, BF16),
            pltpu.VMEM((own,) + unit, F32),
            pltpu.VMEM((nf - 1,) + unit, F32),
            pltpu.VMEM((nf,) + unit, F32),
            pltpu.VMEM((nb,) + unit, F32),
            pltpu.SMEM((nb,), jnp.int32),
            dma((8,)),
            dma((nb - 1,)),
            dma((nb - 1,)),
            dma((nb - 1,)),
            dma((nb - 1,)),
            dma((nf - 1,)),
            dma((nf - 1,)),
            dma((nf - 1,)),
            dma((nf - 1,)),
            dma((nb - 1,)),
            dma((nb - 1,)),
            dma((nb,)),
            dma((nb,)),
        ],
        compiler_params=pltpu.CompilerParams(
            vmem_limit_bytes=48 << 20, collective_id=0, has_side_effects=True
        ),
        name="main",
    )(owner, row, col, w, *consts, vr, vi, co)


def deposit_kernel(table_ref, slot_ref, grid_in, grid_ref, zeros, blocks, where_ref, tile_ref, count_ref, sem, zsem):
    del grid_in
    zeros[...] = jnp.zeros(zeros.shape, F32)
    clears = [clear_copy(zeros, grid_ref, zsem, i, EARLY) for i in range(EARLY, PIECES)]
    for clear in clears:
        clear.start()
    tiles = GY // 128

    def reset(i, carry):
        where_ref[i] = -1
        return carry

    lax.fori_loop(0, tiles, reset, 0)
    count_ref[0] = 0
    lane = lax.broadcasted_iota(jnp.int32, (G + 8, 128), 1)

    def block_of(tile):
        @pl.when(where_ref[tile] < 0)
        def _():
            count = count_ref[0]
            where_ref[tile] = count
            tile_ref[count] = tile
            count_ref[0] = count + 1
            blocks[count] = jnp.zeros(blocks.shape[1:], F32)

        return where_ref[tile]

    def place(b, rank):
        row = table_ref[b, 3 * rank + 1]
        r = pl.ds(pl.multiple_of(row // 8 * 8, 8), G + 8)
        col = table_ref[b, 3 * rank + 2]
        tile = col // 128
        c = col % 128
        patch = jnp.concatenate([slot_ref[rank, b], jnp.zeros((8, 2 * G), F32)], axis=0)
        patch = pltpu.roll(patch, row % 8, 0)
        real = pltpu.roll(jnp.where(lane < G, patch, 0.0), c, 1)
        imag = pltpu.roll(jnp.where(lane < G, 0.0, patch), c + G, 1)
        first = block_of(tile)
        blocks[first, 0, r, :] += jnp.where(lane >= c, real, 0.0)
        blocks[first, 1, r, :] += jnp.where(lane >= c, imag, 0.0)

        @pl.when(c > 128 - G)
        def _():
            second = block_of(tile + 1)
            blocks[second, 0, r, :] += jnp.where(lane < c, real, 0.0)
            blocks[second, 1, r, :] += jnp.where(lane < c, imag, 0.0)

    def source(b, carry):
        for rank in range(FCAP):

            @pl.when(table_ref[b, 3 * rank] > 0)
            def _():
                place(b, rank)

        return carry

    lax.fori_loop(0, table_ref.shape[0], source, 0)
    count = count_ref[0]

    def copy(i):
        cut = pl.ds(pl.multiple_of(tile_ref[i] * 128, 128), 128)
        return pltpu.make_async_copy(blocks.at[i, :, 0:FR, :], grid_ref.at[:, :, cut], sem.at[i])

    def start(i, carry):
        copy(i).start()
        return carry

    def wait(i, carry):
        copy(i).wait()
        return carry

    for clear in clears:
        clear.wait()
    lax.fori_loop(0, count, start, 0)
    lax.fori_loop(0, count, wait, 0)


def deposit(table, slots, grid):
    most = 2 * slots.shape[0] * slots.shape[1]
    return pl.pallas_call(
        deposit_kernel,
        out_shape=jax.ShapeDtypeStruct((2, FR, GY), F32),
        in_specs=[smem(), vmem(), hbm()],
        out_specs=hbm(),
        scratch_shapes=[
            pltpu.VMEM((FR, CLEAR), F32),
            pltpu.VMEM((most, 2, FR + 8, 128), F32),
            pltpu.SMEM((GY // 128,), jnp.int32),
            pltpu.SMEM((most,), jnp.int32),
            pltpu.SMEM((1,), jnp.int32),
            pltpu.SemaphoreType.DMA((most,)),
            pltpu.SemaphoreType.DMA((PIECES - EARLY,)),
        ],
        input_output_aliases={2: 0},
        compiler_params=pltpu.CompilerParams(vmem_limit_bytes=48 << 20),
        name="deposit",
    )(table, slots, grid)


def per_device(visibilities, anchor, drift, target, subgrid_w, facet_owner, row_offset, col_offset):
    nb, nf = lax.axis_size("base"), lax.axis_size("freq")
    target = target.reshape(1, -1)
    vr, vi, co, grid = prep(*[stay(x) for x in (target, visibilities, anchor, drift)])
    small = [stay(x.reshape(1, -1)) for x in (facet_owner, row_offset, col_offset, subgrid_w)]
    slots, table = main(*small, vr, vi, co, nb, nf)
    return deposit(table, slots, grid)


def solution(mesh):
    return jax.shard_map(
        per_device,
        mesh=mesh,
        in_specs=(
            P(None, "base", "freq"),
            P(None, "base"),
            P(None, "base"),
            P("base", None),
            P("base"),
            P("base", None),
            P("base"),
            P("base"),
        ),
        out_specs=P(None, "base", None),
        check_vma=False,
    )
```

```python
import functools
import math

import jax
import jax.numpy as jnp
import numpy as np
from jax import lax
from jax.experimental import pallas as pl
from jax.experimental.pallas import tpu as pltpu
from jax.sharding import PartitionSpec as P

G = 64
GY = 16384
CAP = 8
FCAP = 2
FR = 128
NT = (((1,), (1,)), ((), ()))
F32 = jnp.float32
BF16 = jnp.bfloat16
VMEM = pltpu.MemorySpace.VMEM
SMEM = pltpu.MemorySpace.SMEM


def vmem():
    return pl.BlockSpec(memory_space=VMEM)


def hbm():
    return pl.BlockSpec(memory_space=pltpu.MemorySpace.HBM)


def stay(x):
    return pltpu.with_memory_space_constraint(x, pltpu.MemorySpace.HBM)


def smem():
    return pl.BlockSpec(memory_space=SMEM)


CLEAR = 2048
PIECES = 2 * GY // CLEAR
EARLY = PIECES - 5


def clear_copy(zeros, grid_ref, sem, i, first):
    j = i % (GY // CLEAR)
    part = grid_ref.at[i // (GY // CLEAR), :, CLEAR * j : CLEAR * (j + 1)]
    return pltpu.make_async_copy(zeros, part, sem.at[i - first])


def prep_kernel(
    target_hbm, vis_hbm, anchor_hbm, drift_hbm, vr_ref, vi_ref, co_ref, grid_ref, target_ref, vis_ref, anchor_ref, drift_ref, pick_ref, zeros, sem, zsem
):
    pairs = [(target_hbm, target_ref), (vis_hbm, vis_ref), (anchor_hbm, anchor_ref), (drift_hbm, drift_ref)]
    loads = [pltpu.make_async_copy(src, dst, sem.at[i]) for i, (src, dst) in enumerate(pairs)]
    for load in loads:
        load.start()
    zeros[...] = jnp.zeros(zeros.shape, F32)
    clears = [clear_copy(zeros, grid_ref, zsem, i, 0) for i in range(EARLY)]
    for clear in clears:
        clear.start()
    loads[0].wait()
    blocks = target_ref.shape[1]
    groups = blocks // CAP
    width = 128
    rows = lax.broadcasted_iota(jnp.int32, (width, width), 0)
    lanes = lax.broadcasted_iota(jnp.int32, (width, width), 1)
    count = jnp.concatenate([(rows < lanes).astype(F32), jnp.ones((width, width), F32)], axis=1)
    ids = lax.broadcasted_iota(jnp.int32, (groups, width), 0)
    pieces = range(blocks // width)
    targets = [target_ref[:, width * i : width * (i + 1)] for i in pieces]
    hits = [(ids == target).astype(F32) for target in targets]
    counts = jnp.dot(
        jnp.concatenate(hits, axis=0).astype(BF16), count.astype(BF16), preferred_element_type=F32
    )
    seen = jnp.zeros((groups, width), F32)
    placed = []
    for i in pieces:
        inside = counts[groups * i : groups * (i + 1)]
        ranking = jnp.sum((inside[:, :width] + seen) * hits[i], axis=0, keepdims=True)
        placed.append(targets[i] * CAP + ranking.astype(jnp.int32))
        seen = seen + inside[:, width:]
    placed = jnp.concatenate(placed, axis=1)
    step = 128

    def choose(i, carry):
        start = pl.multiple_of(i * step, step)
        match = lax.broadcasted_iota(jnp.int32, (step, blocks), 0) + start == placed
        pick_ref[pl.ds(start, step), :] = match.astype(F32).astype(BF16)
        return carry

    lax.fori_loop(0, blocks // step, choose, 0)
    for load in loads[1:]:
        load.wait()
    pick = pick_ref[...]
    places = jnp.concatenate([anchor_ref[...].astype(F32), drift_ref[...].astype(F32)], axis=0).astype(BF16)
    co_ref[...] = lax.dot_general(pick, places, NT, preferred_element_type=F32)
    vr_ref[...] = jnp.dot(pick, vis_ref[0], preferred_element_type=F32)
    vi_ref[...] = jnp.dot(pick, vis_ref[1], preferred_element_type=F32)
    for clear in clears:
        clear.wait()


def prep(target, visibilities, anchor, drift):
    _, blocks, channels = visibilities.shape
    return pl.pallas_call(
        prep_kernel,
        out_shape=(
            jax.ShapeDtypeStruct((blocks, channels), F32),
            jax.ShapeDtypeStruct((blocks, channels), F32),
            jax.ShapeDtypeStruct((blocks, 4), F32),
            jax.ShapeDtypeStruct((2, FR, GY), F32),
        ),
        in_specs=[hbm()] * 4,
        out_specs=(vmem(), vmem(), vmem(), hbm()),
        scratch_shapes=[
            pltpu.VMEM((1, blocks), jnp.int32),
            pltpu.VMEM(visibilities.shape, BF16),
            pltpu.VMEM(anchor.shape, BF16),
            pltpu.VMEM(drift.shape, BF16),
            pltpu.VMEM((blocks, blocks), BF16),
            pltpu.VMEM((FR, CLEAR), F32),
            pltpu.SemaphoreType.DMA((4,)),
            pltpu.SemaphoreType.DMA((EARLY,)),
        ],
        compiler_params=pltpu.CompilerParams(vmem_limit_bytes=48 << 20),
        name="prep",
    )(target, visibilities, anchor, drift)


def trig(h):
    z = h * h
    s = 1 / 362880 + z * (-1 / 39916800)
    s = h * (1.0 + z * (-1 / 6 + z * (1 / 120 + z * (-1 / 5040 + z * s))))
    c = -1 / 3628800 + z * (1 / 479001600)
    c = 1.0 + z * (-0.5 + z * (1 / 24 + z * (-1 / 720 + z * (1 / 40320 + z * c))))
    return c, s


HALF = 152


def put(tab, row, v):
    tab[row : row + 8, :] = v[:, :128]
    tab[HALF + row : HALF + row + 8, :] = v[:, 128:]


def base_rows(h, tab):
    c0, s0 = trig(h)
    k1 = 4.0 * c0 * c0 - 2.0
    k2 = k1 * k1 - 2.0
    k4 = k2 * k2 - 2.0
    k8 = k4 * k4 - 2.0
    s8 = (2.0 * s0 * c0) * k1 * k2 * k4
    cp, cc = c0, (k1 - 1.0) * c0
    sp, sc = s0, (k1 + 1.0) * s0
    put(tab, 0, c0)
    put(tab, 64, s0)
    for p in range(1, 8):
        put(tab, 8 * p, cc)
        put(tab, 64 + 8 * p, sc)
        cp, cc = cc, k1 * cc - cp
        sp, sc = sc, k1 * sc - sp
    put(tab, 128, k8)
    put(tab, 136, 0.5 * k8)
    put(tab, 144, s8)
    return c0, s0


def expand(tab, s, h):
    o = HALF * h
    k8 = tab[o + 128 + s : o + 129 + s, :]
    c8 = tab[o + 136 + s : o + 137 + s, :]
    s8 = tab[o + 144 + s : o + 145 + s, :]
    a0 = tab[pl.ds(o + s, 8, stride=8), :]
    b0 = tab[pl.ds(o + 64 + s, 8, stride=8), :]
    a1 = c8 * a0 - s8 * b0
    b1 = c8 * b0 + s8 * a0
    a2 = k8 * a1 - a0
    b2 = k8 * b1 - b0
    a3 = k8 * a2 - a1
    b3 = k8 * b2 - b1
    return jnp.concatenate([a0, a1, a2, a3, b0, b1, b2, b3], axis=0)


def tables(g, chan, vr_ref, vi_ref, co_ref, tx, ty, tv):
    rows = pl.ds(pl.multiple_of(8 * g, 8), 8)
    co = co_ref[rows, :]
    hx = (co[:, 0:1] - 0.5 * G + chan * co[:, 2:3]) * (math.pi / G)
    hy = (co[:, 1:2] - 0.5 * G + chan * co[:, 3:4]) * (math.pi / G)
    cx, sx = base_rows(hx, tx)
    cy, sy = base_rows(hy, ty)
    er = cx * cy - sx * sy
    ei = cx * sy + sx * cy
    vr = vr_ref[rows, :]
    vi = vi_ref[rows, :]
    tv[0:8, :] = vr * er + vi * ei
    tv[8:16, :] = vi * er - vr * ei


def products(tx, ty, tv):
    acc = None
    for s in range(8):
        f = jnp.concatenate([expand(tx, s, h).astype(BF16) for h in (0, 1)], axis=1)
        parts = []
        for h in (0, 1):
            g0 = expand(ty, s, h)
            cut = slice(128 * h, 128 * h + 128)
            both = [g0 * tv[s : s + 1, cut], g0 * tv[8 + s : 9 + s, cut]]
            parts.append(jnp.concatenate(both, axis=0).astype(BF16))
        r = jnp.concatenate(parts, axis=1)
        d = lax.dot_general(f, r, NT, preferred_element_type=F32)
        acc = d if acc is None else acc + d
    return acc


def constants():
    l = np.arange(G) - G // 2 + 0.5
    p = np.arange(G // 2) + 0.5
    same = (np.abs(l)[:, None] == p[None, :]).astype(np.float64)
    a = np.concatenate([same, 0 * same], axis=1)
    b = np.concatenate([0 * same, same * np.sign(l)[:, None]], axis=1)
    turns = 2 * np.pi * ((np.arange(G)[:, None] * np.arange(G)[None, :]) % G) / G
    fr, fi = np.cos(turns), -np.sin(turns)
    left1 = np.concatenate([a, b], axis=0)
    right1 = np.block([[a.T, b.T], [-b.T, a.T]])
    left2 = np.concatenate([fr, fi], axis=0)
    right2 = np.block([[fr, fi], [-fi, fr]]) / G

    def split(x):
        high = x.astype(jnp.bfloat16)
        return high, (x - high.astype(np.float64)).astype(jnp.bfloat16)

    one_l, _ = split(left1)
    one_r, _ = split(right1)
    two_l, two_ll = split(left2)
    two_r, two_rl = split(right2)
    return [
        np.concatenate([one_l, one_l], axis=1),
        np.concatenate([one_r, one_r], axis=0),
        np.concatenate([two_l, two_l, two_ll, 0 * two_l], axis=1),
        np.concatenate([two_r, two_r, two_rl], axis=0),
    ]


def split_rows(x, times, axis):
    high = x.astype(BF16)
    low = (x - high.astype(F32)).astype(BF16)
    return jnp.concatenate(([high, low] + [high] * 2)[:times], axis=axis)


def dot16(a, b):
    return jnp.dot(a, b, preferred_element_type=F32)


def swap(x):
    return pltpu.roll(x, G, 1)


def screen(w):
    row = lax.broadcasted_iota(jnp.int32, (G, 2 * G), 0)
    lane = lax.broadcasted_iota(jnp.int32, (G, 2 * G), 1)
    xl = (row - G // 2).astype(F32) * (2.0 / G)
    xm = (jnp.where(lane < G, lane, lane - G) - G // 2).astype(F32) * (2.0 / G)
    c, s = trig((0.25 * math.pi) * w * (xl * xl + xm * xm))
    for _ in range(2):
        c, s = 2.0 * c * c - 1.0, 2.0 * c * s
    return c, jnp.where(lane < G, -s, s)


def make_patch(m, c, s, left1, right1, left2, right2):
    lane = lax.broadcasted_iota(jnp.int32, (G, 2 * G), 1)
    sign = jnp.where(lane < G, -1.0, 1.0).astype(F32)
    both = dot16(left1, split_rows(m, 2, 0))
    y = both[:G] + sign * swap(both[G:])
    z = dot16(split_rows(y, 2, 1), right1)
    k = z * c + swap(z) * s
    both = dot16(left2, split_rows(k, 4, 0))
    y = both[:G] + sign * swap(both[G:])
    return dot16(split_rows(y, 3, 1), right2)


MESH = pl.DeviceIdType.MESH


def main_kernel(
    nb,
    nf,
    owner_hbm,
    row_hbm,
    col_hbm,
    w_hbm,
    left1_hbm,
    right1_hbm,
    left2_hbm,
    right2_hbm,
    vr_ref,
    vi_ref,
    co_ref,
    slots,
    table,
    owner_ref,
    row_ref,
    col_ref,
    w_ref,
    left1,
    right1,
    left2,
    right2,
    spot_ref,
    tx0,
    ty0,
    tv0,
    tx1,
    ty1,
    tv1,
    cs,
    send,
    recv,
    total,
    fsum,
    gath,
    outb,
    choice,
    load_sem,
    spot_s,
    spot_r,
    base_s,
    base_r,
    freq_s,
    freq_r,
    gath_s,
    gath_r,
    hand_s,
    hand_r,
    out_s,
    out_r,
    pair_s,
    pair_r,
):
    me_b = lax.axis_index("base")
    me_f = lax.axis_index("freq")
    own = total.shape[0]
    core = me_f % 2
    even = (tx0, ty0, tv0)
    odd = (tx1, ty1, tv1)

    side = math.isqrt(nb)

    def peer(t, sign):
        z = (me_b // side + side + sign * (t % side)) % side
        y = (me_b % side + side + sign * ((t // side + t) % side)) % side
        return z * side + y

    def base_copy(src, dst, ss, rs, t):
        return pltpu.make_async_remote_copy(
            src_ref=src, dst_ref=dst, send_sem=ss, recv_sem=rs, device_id={"base": peer(t, 1)}, device_id_type=MESH
        )

    def freq_copy(src, dst, ss, rs, d):
        return pltpu.make_async_remote_copy(
            src_ref=src, dst_ref=dst, send_sem=ss, recv_sem=rs, device_id={"freq": (me_f + d) % nf}, device_id_type=MESH
        )

    def each(low, high, body):
        def step(i, carry):
            body(i)
            return carry

        lax.fori_loop(low, high, step, 0)

    barrier = pltpu.get_barrier_semaphore()
    each(1, nb, lambda t: pl.semaphore_signal(barrier, inc=1, device_id={"base": (me_b + t) % nb}, device_id_type=MESH))
    each(1, nf, lambda d: pl.semaphore_signal(barrier, inc=1, device_id={"freq": (me_f + d) % nf}, device_id_type=MESH))
    pairs = [
        (owner_hbm, owner_ref),
        (row_hbm, row_ref),
        (col_hbm, col_ref),
        (w_hbm, w_ref),
        (left1_hbm, left1),
        (right1_hbm, right1),
        (left2_hbm, left2),
        (right2_hbm, right2),
    ]
    loads = [pltpu.make_async_copy(src, dst, load_sem.at[i]) for i, (src, dst) in enumerate(pairs)]
    for load in loads:
        load.start()

    channels = vr_ref.shape[1]
    chan = (lax.broadcasted_iota(jnp.int32, (8, channels), 1) + me_f * channels).astype(F32)

    def subgrid(i):
        return peer(i // own + 1, 1) * own + i % own

    def prepare(i, tabs):
        tables(subgrid(i), chan, vr_ref, vi_ref, co_ref, *tabs)

    def spot_copy(t):
        return base_copy(spot_ref.at[pl.ds(peer(t, 1), 1)], table.at[pl.ds(me_b, 1)], spot_s.at[t - 1], spot_r.at[t - 1], t)

    def share_copy(t):
        return base_copy(send.at[t], recv.at[t], base_s.at[t], base_r.at[t], t + 1)

    prepare(0, even)
    lane = lax.broadcasted_iota(jnp.int32, (1, 128), 1)

    def choose(o):
        seen = jnp.int32(0)
        index = [jnp.int32(0)] * FCAP
        for s in range(own):
            hit = (owner_ref[0, s] == o).astype(jnp.int32)
            index = [index[r] + hit * (seen == r).astype(jnp.int32) * s for r in range(FCAP)]
            seen = seen + hit
        choice[o] = index[0] * (1 - core) + index[1] * core
        spot = jnp.zeros((1, 128), jnp.int32)
        for r in range(FCAP):
            fields = ((seen > r).astype(jnp.int32), row_ref[0, index[r]], col_ref[0, index[r]])
            for n, value in enumerate(fields):
                spot = jnp.where(lane == 3 * r + n, value, spot)
        spot_ref[pl.ds(o, 1), :] = spot

    def small_work():
        for load in loads:
            load.wait()
        c, s = screen(w_ref[0, me_f])
        cs[0] = c
        cs[1] = s
        each(0, nb, choose)
        table[pl.ds(me_b, 1), :] = spot_ref[pl.ds(me_b, 1), :]

    def group(t):
        def two(u):
            i = t * own + 2 * u
            prepare(i + 1, odd)
            send[t, 2 * u] = products(*even).astype(BF16)
            prepare(i + 2, even)
            send[t, 2 * u + 1] = products(*odd).astype(BF16)

        each(0, own // 2, two)

        @pl.when(t == 0)
        def _():
            pl.semaphore_wait(barrier, nb + nf - 2)

        @pl.when(t < nb - 1)
        def _():
            share_copy(t).start()

        @pl.when(t == 0)
        def _():
            small_work()
            each(1, nb, lambda t: spot_copy(t).start())

    each(0, nb, group)
    each(0, nb - 1, lambda t: share_copy(t).wait_recv())

    def sum_shares(j):
        m = send[nb - 1, j].astype(F32)
        for t in range(nb - 1):
            m = m + recv[t, j].astype(F32)
        return m

    def sum_copy(d):
        return freq_copy(total.at[(me_f + d) % nf], fsum.at[d - 1], freq_s.at[d - 1], freq_r.at[d - 1], d)

    def reduce(d):
        j = (me_f + d) % nf
        total[j] = sum_shares(j)
        sum_copy(d).start()

    each(1, nf, reduce)
    m = sum_shares(me_f)
    each(1, nf, lambda d: sum_copy(d).wait_recv())
    for d in range(1, nf):
        m = m + fsum[d - 1]
    gath[me_f] = make_patch(m, cs[0], cs[1], left1[...], right1[...], left2[...], right2[...])

    chips = nf // 2
    turn = 1 - 2 * core + nf

    def gath_copy(d):
        return freq_copy(gath.at[me_f], gath.at[me_f], gath_s.at[d - 1], gath_r.at[d - 1], 2 * d)

    def hand_copy(d):
        piece = gath.at[(me_f + nf - 2 * d) % nf]
        return freq_copy(piece, piece, hand_s.at[d], hand_r.at[d], turn)

    def hand_on(d):
        gath_copy(d).wait_recv()
        hand_copy(d).start()

    each(1, chips, lambda d: gath_copy(d).start())
    hand_copy(0).start()
    each(1, chips, hand_on)
    each(0, chips, lambda d: hand_copy(d).wait_recv())

    def out_copy(t):
        return base_copy(outb.at[peer(t, 1)], slots.at[core, me_b], out_s.at[t - 1], out_r.at[t - 1], t)

    def pick(o):
        return gath[choice[o]]

    def ship(t):
        o = peer(t, 1)
        outb[o] = pick(o)
        out_copy(t).start()

    each(1, nb, ship)
    slots[core, me_b] = pick(me_b)

    def pair_copy(t):
        source = peer(t, -1)
        part = slots.at[core, source]
        return pltpu.make_async_remote_copy(
            src_ref=part,
            dst_ref=part,
            send_sem=pair_s.at[t],
            recv_sem=pair_r.at[t],
            device_id={"freq": me_f + 1 - 2 * core},
            device_id_type=MESH,
        )

    pair_copy(0).start()

    def forward(t):
        out_copy(t).wait_recv()
        pair_copy(t).start()

    each(1, nb, forward)
    each(0, nb, lambda t: pair_copy(t).wait())
    each(1, nb, lambda t: out_copy(t).wait_send())
    each(1, chips, lambda d: gath_copy(d).wait_send())
    each(0, chips, lambda d: hand_copy(d).wait_send())
    each(1, nf, lambda d: sum_copy(d).wait_send())
    each(0, nb - 1, lambda t: share_copy(t).wait_send())
    each(1, nb, lambda t: spot_copy(t).wait())


def main(owner, row, col, w, vr, vi, co, nb, nf):
    own = w.shape[1]
    unit = (G, 2 * G)
    dma = pltpu.SemaphoreType.DMA
    consts = [stay(jnp.asarray(x)) for x in constants()]
    tabs = [pltpu.VMEM((2 * HALF, 128), F32), pltpu.VMEM((2 * HALF, 128), F32), pltpu.VMEM((16, 256), F32)]
    return pl.pallas_call(
        functools.partial(main_kernel, nb, nf),
        out_shape=(
            jax.ShapeDtypeStruct((FCAP, nb) + unit, F32),
            jax.ShapeDtypeStruct((nb, 128), jnp.int32),
        ),
        in_specs=[hbm()] * 8 + [vmem()] * 3,
        out_specs=(vmem(), vmem()),
        scratch_shapes=[
            pltpu.SMEM((1, own), jnp.int32),
            pltpu.SMEM((1, own), jnp.int32),
            pltpu.SMEM((1, own), jnp.int32),
            pltpu.SMEM((1, own), F32),
        ]
        + [pltpu.VMEM(x.shape, BF16) for x in consts]
        + [pltpu.VMEM((nb, 128), jnp.int32)]
        + tabs * 2
        + [
            pltpu.VMEM((2,) + unit, F32),
            pltpu.VMEM((nb, own) + unit, BF16),
            pltpu.VMEM((nb - 1, own) + unit, BF16),
            pltpu.VMEM((own,) + unit, F32),
            pltpu.VMEM((nf - 1,) + unit, F32),
            pltpu.VMEM((nf,) + unit, F32),
            pltpu.VMEM((nb,) + unit, F32),
            pltpu.SMEM((nb,), jnp.int32),
            dma((8,)),
            dma((nb - 1,)),
            dma((nb - 1,)),
            dma((nb - 1,)),
            dma((nb - 1,)),
            dma((nf - 1,)),
            dma((nf - 1,)),
            dma((nf // 2 - 1,)),
            dma((nf // 2 - 1,)),
            dma((nf // 2,)),
            dma((nf // 2,)),
            dma((nb - 1,)),
            dma((nb - 1,)),
            dma((nb,)),
            dma((nb,)),
        ],
        compiler_params=pltpu.CompilerParams(
            vmem_limit_bytes=48 << 20, collective_id=0, has_side_effects=True
        ),
        name="main",
    )(owner, row, col, w, *consts, vr, vi, co)


def deposit_kernel(table_ref, slot_ref, grid_in, grid_ref, zeros, blocks, where_ref, tile_ref, count_ref, sem, zsem):
    del grid_in
    zeros[...] = jnp.zeros(zeros.shape, F32)
    clears = [clear_copy(zeros, grid_ref, zsem, i, EARLY) for i in range(EARLY, PIECES)]
    for clear in clears:
        clear.start()
    tiles = GY // 128

    def reset(i, carry):
        where_ref[i] = -1
        return carry

    lax.fori_loop(0, tiles, reset, 0)
    count_ref[0] = 0
    lane = lax.broadcasted_iota(jnp.int32, (G + 8, 128), 1)

    def block_of(tile):
        @pl.when(where_ref[tile] < 0)
        def _():
            count = count_ref[0]
            where_ref[tile] = count
            tile_ref[count] = tile
            count_ref[0] = count + 1
            blocks[count] = jnp.zeros(blocks.shape[1:], F32)

        return where_ref[tile]

    def place(b, rank):
        row = table_ref[b, 3 * rank + 1]
        r = pl.ds(pl.multiple_of(row // 8 * 8, 8), G + 8)
        col = table_ref[b, 3 * rank + 2]
        tile = col // 128
        c = col % 128
        patch = jnp.concatenate([slot_ref[rank, b], jnp.zeros((8, 2 * G), F32)], axis=0)
        patch = pltpu.roll(patch, row % 8, 0)
        real = pltpu.roll(jnp.where(lane < G, patch, 0.0), c, 1)
        imag = pltpu.roll(jnp.where(lane < G, 0.0, patch), c + G, 1)
        first = block_of(tile)
        blocks[first, 0, r, :] += jnp.where(lane >= c, real, 0.0)
        blocks[first, 1, r, :] += jnp.where(lane >= c, imag, 0.0)

        @pl.when(c > 128 - G)
        def _():
            second = block_of(tile + 1)
            blocks[second, 0, r, :] += jnp.where(lane < c, real, 0.0)
            blocks[second, 1, r, :] += jnp.where(lane < c, imag, 0.0)

    def source(b, carry):
        for rank in range(FCAP):

            @pl.when(table_ref[b, 3 * rank] > 0)
            def _():
                place(b, rank)

        return carry

    lax.fori_loop(0, table_ref.shape[0], source, 0)
    count = count_ref[0]

    def copy(i):
        cut = pl.ds(pl.multiple_of(tile_ref[i] * 128, 128), 128)
        return pltpu.make_async_copy(blocks.at[i, :, 0:FR, :], grid_ref.at[:, :, cut], sem.at[i])

    def start(i, carry):
        copy(i).start()
        return carry

    def wait(i, carry):
        copy(i).wait()
        return carry

    for clear in clears:
        clear.wait()
    lax.fori_loop(0, count, start, 0)
    lax.fori_loop(0, count, wait, 0)


def deposit(table, slots, grid):
    most = 2 * slots.shape[0] * slots.shape[1]
    return pl.pallas_call(
        deposit_kernel,
        out_shape=jax.ShapeDtypeStruct((2, FR, GY), F32),
        in_specs=[smem(), vmem(), hbm()],
        out_specs=hbm(),
        scratch_shapes=[
            pltpu.VMEM((FR, CLEAR), F32),
            pltpu.VMEM((most, 2, FR + 8, 128), F32),
            pltpu.SMEM((GY // 128,), jnp.int32),
            pltpu.SMEM((most,), jnp.int32),
            pltpu.SMEM((1,), jnp.int32),
            pltpu.SemaphoreType.DMA((most,)),
            pltpu.SemaphoreType.DMA((PIECES - EARLY,)),
        ],
        input_output_aliases={2: 0},
        compiler_params=pltpu.CompilerParams(vmem_limit_bytes=48 << 20),
        name="deposit",
    )(table, slots, grid)


def per_device(visibilities, anchor, drift, target, subgrid_w, facet_owner, row_offset, col_offset):
    nb, nf = lax.axis_size("base"), lax.axis_size("freq")
    target = target.reshape(1, -1)
    vr, vi, co, grid = prep(*[stay(x) for x in (target, visibilities, anchor, drift)])
    small = [stay(x.reshape(1, -1)) for x in (facet_owner, row_offset, col_offset, subgrid_w)]
    slots, table = main(*small, vr, vi, co, nb, nf)
    return deposit(table, slots, grid)


def solution(mesh):
    return jax.shard_map(
        per_device,
        mesh=mesh,
        in_specs=(
            P(None, "base", "freq"),
            P(None, "base"),
            P(None, "base"),
            P("base", None),
            P("base"),
            P("base", None),
            P("base"),
            P("base"),
        ),
        out_specs=P(None, "base", None),
        check_vma=False,
    )
```

```python
import functools
import math

import jax
import jax.numpy as jnp
import numpy as np
from jax import lax
from jax.experimental import pallas as pl
from jax.experimental.pallas import tpu as pltpu
from jax.sharding import PartitionSpec as P

G = 64
GY = 16384
CAP = 8
FCAP = 2
FR = 128
NT = (((1,), (1,)), ((), ()))
F32 = jnp.float32
BF16 = jnp.bfloat16
VMEM = pltpu.MemorySpace.VMEM
SMEM = pltpu.MemorySpace.SMEM


def vmem():
    return pl.BlockSpec(memory_space=VMEM)


def hbm():
    return pl.BlockSpec(memory_space=pltpu.MemorySpace.HBM)


def stay(x):
    return pltpu.with_memory_space_constraint(x, pltpu.MemorySpace.HBM)


def smem():
    return pl.BlockSpec(memory_space=SMEM)


CLEAR = 2048
PIECES = 2 * GY // CLEAR
EARLY = PIECES - 5


def clear_copy(zeros, grid_ref, sem, i, first):
    j = i % (GY // CLEAR)
    part = grid_ref.at[i // (GY // CLEAR), :, CLEAR * j : CLEAR * (j + 1)]
    return pltpu.make_async_copy(zeros, part, sem.at[i - first])


def prep_kernel(
    target_hbm, vis_hbm, anchor_hbm, drift_hbm, vr_ref, vi_ref, co_ref, grid_ref, target_ref, vis_ref, anchor_ref, drift_ref, pick_ref, zeros, sem, zsem
):
    pairs = [(target_hbm, target_ref), (vis_hbm, vis_ref), (anchor_hbm, anchor_ref), (drift_hbm, drift_ref)]
    loads = [pltpu.make_async_copy(src, dst, sem.at[i]) for i, (src, dst) in enumerate(pairs)]
    for load in loads:
        load.start()
    zeros[...] = jnp.zeros(zeros.shape, F32)
    clears = [clear_copy(zeros, grid_ref, zsem, i, 0) for i in range(EARLY)]
    for clear in clears:
        clear.start()
    loads[0].wait()
    blocks = target_ref.shape[1]
    groups = blocks // CAP
    width = 128
    rows = lax.broadcasted_iota(jnp.int32, (width, width), 0)
    lanes = lax.broadcasted_iota(jnp.int32, (width, width), 1)
    count = jnp.concatenate([(rows < lanes).astype(F32), jnp.ones((width, width), F32)], axis=1)
    ids = lax.broadcasted_iota(jnp.int32, (groups, width), 0)
    pieces = range(blocks // width)
    targets = [target_ref[:, width * i : width * (i + 1)] for i in pieces]
    hits = [(ids == target).astype(F32) for target in targets]
    counts = jnp.dot(
        jnp.concatenate(hits, axis=0).astype(BF16), count.astype(BF16), preferred_element_type=F32
    )
    seen = jnp.zeros((groups, width), F32)
    placed = []
    for i in pieces:
        inside = counts[groups * i : groups * (i + 1)]
        ranking = jnp.sum((inside[:, :width] + seen) * hits[i], axis=0, keepdims=True)
        placed.append(targets[i] * CAP + ranking.astype(jnp.int32))
        seen = seen + inside[:, width:]
    placed = jnp.concatenate(placed, axis=1)
    step = 128

    def choose(i, carry):
        start = pl.multiple_of(i * step, step)
        match = lax.broadcasted_iota(jnp.int32, (step, blocks), 0) + start == placed
        pick_ref[pl.ds(start, step), :] = match.astype(F32).astype(BF16)
        return carry

    lax.fori_loop(0, blocks // step, choose, 0)
    for load in loads[1:]:
        load.wait()
    pick = pick_ref[...]
    places = jnp.concatenate([anchor_ref[...].astype(F32), drift_ref[...].astype(F32)], axis=0).astype(BF16)
    co_ref[...] = lax.dot_general(pick, places, NT, preferred_element_type=F32)
    vr_ref[...] = jnp.dot(pick, vis_ref[0], preferred_element_type=F32)
    vi_ref[...] = jnp.dot(pick, vis_ref[1], preferred_element_type=F32)
    for clear in clears:
        clear.wait()


def prep(target, visibilities, anchor, drift):
    _, blocks, channels = visibilities.shape
    return pl.pallas_call(
        prep_kernel,
        out_shape=(
            jax.ShapeDtypeStruct((blocks, channels), F32),
            jax.ShapeDtypeStruct((blocks, channels), F32),
            jax.ShapeDtypeStruct((blocks, 4), F32),
            jax.ShapeDtypeStruct((2, FR, GY), F32),
        ),
        in_specs=[hbm()] * 4,
        out_specs=(vmem(), vmem(), vmem(), hbm()),
        scratch_shapes=[
            pltpu.VMEM((1, blocks), jnp.int32),
            pltpu.VMEM(visibilities.shape, BF16),
            pltpu.VMEM(anchor.shape, BF16),
            pltpu.VMEM(drift.shape, BF16),
            pltpu.VMEM((blocks, blocks), BF16),
            pltpu.VMEM((FR, CLEAR), F32),
            pltpu.SemaphoreType.DMA((4,)),
            pltpu.SemaphoreType.DMA((EARLY,)),
        ],
        compiler_params=pltpu.CompilerParams(vmem_limit_bytes=48 << 20),
        name="prep",
    )(target, visibilities, anchor, drift)


def trig(h):
    z = h * h
    s = 1 / 362880 + z * (-1 / 39916800)
    s = h * (1.0 + z * (-1 / 6 + z * (1 / 120 + z * (-1 / 5040 + z * s))))
    c = -1 / 3628800 + z * (1 / 479001600)
    c = 1.0 + z * (-0.5 + z * (1 / 24 + z * (-1 / 720 + z * (1 / 40320 + z * c))))
    return c, s


HALF = 152


def put(tab, row, v):
    tab[row : row + 8, :] = v[:, :128]
    tab[HALF + row : HALF + row + 8, :] = v[:, 128:]


def base_rows(h, tab):
    c0, s0 = trig(h)
    k1 = 4.0 * c0 * c0 - 2.0
    k2 = k1 * k1 - 2.0
    k4 = k2 * k2 - 2.0
    k8 = k4 * k4 - 2.0
    s8 = (2.0 * s0 * c0) * k1 * k2 * k4
    cp, cc = c0, (k1 - 1.0) * c0
    sp, sc = s0, (k1 + 1.0) * s0
    put(tab, 0, c0)
    put(tab, 64, s0)
    for p in range(1, 8):
        put(tab, 8 * p, cc)
        put(tab, 64 + 8 * p, sc)
        cp, cc = cc, k1 * cc - cp
        sp, sc = sc, k1 * sc - sp
    put(tab, 128, k8)
    put(tab, 136, 0.5 * k8)
    put(tab, 144, s8)
    return c0, s0


def expand(tab, s, h):
    o = HALF * h
    k8 = tab[o + 128 + s : o + 129 + s, :]
    c8 = tab[o + 136 + s : o + 137 + s, :]
    s8 = tab[o + 144 + s : o + 145 + s, :]
    a0 = tab[pl.ds(o + s, 8, stride=8), :]
    b0 = tab[pl.ds(o + 64 + s, 8, stride=8), :]
    a1 = c8 * a0 - s8 * b0
    b1 = c8 * b0 + s8 * a0
    a2 = k8 * a1 - a0
    b2 = k8 * b1 - b0
    a3 = k8 * a2 - a1
    b3 = k8 * b2 - b1
    return jnp.concatenate([a0, a1, a2, a3, b0, b1, b2, b3], axis=0)


def tables(g, chan, vr_ref, vi_ref, co_ref, tx, ty, tv):
    rows = pl.ds(pl.multiple_of(8 * g, 8), 8)
    co = co_ref[rows, :]
    hx = (co[:, 0:1] - 0.5 * G + chan * co[:, 2:3]) * (math.pi / G)
    hy = (co[:, 1:2] - 0.5 * G + chan * co[:, 3:4]) * (math.pi / G)
    cx, sx = base_rows(hx, tx)
    cy, sy = base_rows(hy, ty)
    er = cx * cy - sx * sy
    ei = cx * sy + sx * cy
    vr = vr_ref[rows, :]
    vi = vi_ref[rows, :]
    tv[0:8, :] = vr * er + vi * ei
    tv[8:16, :] = vi * er - vr * ei


def products(tx, ty, tv):
    acc = None
    for s in range(8):
        f = jnp.concatenate([expand(tx, s, h).astype(BF16) for h in (0, 1)], axis=1)
        parts = []
        for h in (0, 1):
            g0 = expand(ty, s, h)
            cut = slice(128 * h, 128 * h + 128)
            both = [g0 * tv[s : s + 1, cut], g0 * tv[8 + s : 9 + s, cut]]
            parts.append(jnp.concatenate(both, axis=0).astype(BF16))
        r = jnp.concatenate(parts, axis=1)
        d = lax.dot_general(f, r, NT, preferred_element_type=F32)
        acc = d if acc is None else acc + d
    return acc


def constants():
    l = np.arange(G) - G // 2 + 0.5
    p = np.arange(G // 2) + 0.5
    same = (np.abs(l)[:, None] == p[None, :]).astype(np.float64)
    a = np.concatenate([same, 0 * same], axis=1)
    b = np.concatenate([0 * same, same * np.sign(l)[:, None]], axis=1)
    turns = 2 * np.pi * ((np.arange(G)[:, None] * np.arange(G)[None, :]) % G) / G
    fr, fi = np.cos(turns), -np.sin(turns)
    left1 = np.concatenate([a, b], axis=0)
    right1 = np.block([[a.T, b.T], [-b.T, a.T]])
    left2 = np.concatenate([fr, fi], axis=0)
    right2 = np.block([[fr, fi], [-fi, fr]]) / G

    def split(x):
        high = x.astype(jnp.bfloat16)
        return high, (x - high.astype(np.float64)).astype(jnp.bfloat16)

    one_l, _ = split(left1)
    one_r, _ = split(right1)
    two_l, two_ll = split(left2)
    two_r, two_rl = split(right2)
    return [
        np.concatenate([one_l, one_l], axis=1),
        np.concatenate([one_r, one_r], axis=0),
        np.concatenate([two_l, two_l, two_ll, 0 * two_l], axis=1),
        np.concatenate([two_r, two_r, two_rl], axis=0),
    ]


def split_rows(x, times, axis):
    high = x.astype(BF16)
    low = (x - high.astype(F32)).astype(BF16)
    return jnp.concatenate(([high, low] + [high] * 2)[:times], axis=axis)


def dot16(a, b):
    return jnp.dot(a, b, preferred_element_type=F32)


def swap(x):
    return pltpu.roll(x, G, 1)


def screen(w):
    row = lax.broadcasted_iota(jnp.int32, (G, 2 * G), 0)
    lane = lax.broadcasted_iota(jnp.int32, (G, 2 * G), 1)
    xl = (row - G // 2).astype(F32) * (2.0 / G)
    xm = (jnp.where(lane < G, lane, lane - G) - G // 2).astype(F32) * (2.0 / G)
    c, s = trig((0.25 * math.pi) * w * (xl * xl + xm * xm))
    for _ in range(2):
        c, s = 2.0 * c * c - 1.0, 2.0 * c * s
    return c, jnp.where(lane < G, -s, s)


def make_patch(m, c, s, left1, right1, left2, right2):
    lane = lax.broadcasted_iota(jnp.int32, (G, 2 * G), 1)
    sign = jnp.where(lane < G, -1.0, 1.0).astype(F32)
    both = dot16(left1, split_rows(m, 2, 0))
    y = both[:G] + sign * swap(both[G:])
    z = dot16(split_rows(y, 2, 1), right1)
    k = z * c + swap(z) * s
    both = dot16(left2, split_rows(k, 4, 0))
    y = both[:G] + sign * swap(both[G:])
    return dot16(split_rows(y, 3, 1), right2)


MESH = pl.DeviceIdType.MESH


def main_kernel(
    nb,
    nf,
    owner_hbm,
    row_hbm,
    col_hbm,
    w_hbm,
    left1_hbm,
    right1_hbm,
    left2_hbm,
    right2_hbm,
    vr_ref,
    vi_ref,
    co_ref,
    slots,
    table,
    owner_ref,
    row_ref,
    col_ref,
    w_ref,
    left1,
    right1,
    left2,
    right2,
    spot_ref,
    tx0,
    ty0,
    tv0,
    tx1,
    ty1,
    tv1,
    cs,
    send,
    recv,
    total,
    csum,
    fsum,
    gath,
    outb,
    choice,
    load_sem,
    spot_s,
    spot_r,
    base_s,
    base_r,
    core_s,
    core_r,
    freq_s,
    freq_r,
    gath_s,
    gath_r,
    hand_s,
    hand_r,
    out_s,
    out_r,
    pair_s,
    pair_r,
):
    me_b = lax.axis_index("base")
    me_f = lax.axis_index("freq")
    own = nf
    core = me_f % 2
    place = me_f // 2
    even = (tx0, ty0, tv0)
    odd = (tx1, ty1, tv1)

    side = math.isqrt(nb)

    def peer(t, sign):
        z = (me_b // side + side + sign * (t % side)) % side
        y = (me_b % side + side + sign * ((t // side + t) % side)) % side
        return z * side + y

    def base_copy(src, dst, ss, rs, t):
        return pltpu.make_async_remote_copy(
            src_ref=src, dst_ref=dst, send_sem=ss, recv_sem=rs, device_id={"base": peer(t, 1)}, device_id_type=MESH
        )

    def freq_copy(src, dst, ss, rs, d):
        return pltpu.make_async_remote_copy(
            src_ref=src, dst_ref=dst, send_sem=ss, recv_sem=rs, device_id={"freq": (me_f + d) % nf}, device_id_type=MESH
        )

    def each(low, high, body):
        def step(i, carry):
            body(i)
            return carry

        lax.fori_loop(low, high, step, 0)

    barrier = pltpu.get_barrier_semaphore()
    each(1, nb, lambda t: pl.semaphore_signal(barrier, inc=1, device_id={"base": (me_b + t) % nb}, device_id_type=MESH))
    each(1, nf, lambda d: pl.semaphore_signal(barrier, inc=1, device_id={"freq": (me_f + d) % nf}, device_id_type=MESH))
    pairs = [
        (owner_hbm, owner_ref),
        (row_hbm, row_ref),
        (col_hbm, col_ref),
        (w_hbm, w_ref),
        (left1_hbm, left1),
        (right1_hbm, right1),
        (left2_hbm, left2),
        (right2_hbm, right2),
    ]
    loads = [pltpu.make_async_copy(src, dst, load_sem.at[i]) for i, (src, dst) in enumerate(pairs)]
    for load in loads:
        load.start()

    channels = vr_ref.shape[1]
    chan = (lax.broadcasted_iota(jnp.int32, (8, channels), 1) + me_f * channels).astype(F32)

    def subgrid(i):
        return peer(i // own + 1, 1) * own + i % own

    def prepare(i, tabs):
        tables(subgrid(i), chan, vr_ref, vi_ref, co_ref, *tabs)

    def spot_copy(t):
        return base_copy(spot_ref.at[pl.ds(peer(t, 1), 1)], table.at[pl.ds(me_b, 1)], spot_s.at[t - 1], spot_r.at[t - 1], t)

    def share_copy(t):
        return base_copy(send.at[t], recv.at[t], base_s.at[t], base_r.at[t], t + 1)

    prepare(0, even)
    lane = lax.broadcasted_iota(jnp.int32, (1, 128), 1)

    def choose(o):
        seen = jnp.int32(0)
        index = [jnp.int32(0)] * FCAP
        for s in range(own):
            hit = (owner_ref[0, s] == o).astype(jnp.int32)
            index = [index[r] + hit * (seen == r).astype(jnp.int32) * s for r in range(FCAP)]
            seen = seen + hit
        choice[o] = index[0] * (1 - core) + index[1] * core
        spot = jnp.zeros((1, 128), jnp.int32)
        for r in range(FCAP):
            fields = ((seen > r).astype(jnp.int32), row_ref[0, index[r]], col_ref[0, index[r]])
            for n, value in enumerate(fields):
                spot = jnp.where(lane == 3 * r + n, value, spot)
        spot_ref[pl.ds(o, 1), :] = spot

    def small_work():
        for load in loads:
            load.wait()
        c, s = screen(w_ref[0, me_f])
        cs[0] = c
        cs[1] = s
        each(0, nb, choose)
        table[pl.ds(me_b, 1), :] = spot_ref[pl.ds(me_b, 1), :]

    def group(t):
        def two(u):
            i = t * own + 2 * u
            prepare(i + 1, odd)
            send[t, 2 * u] = products(*even).astype(BF16)
            prepare(i + 2, even)
            send[t, 2 * u + 1] = products(*odd).astype(BF16)

        each(0, own // 2, two)

        @pl.when(t == 0)
        def _():
            pl.semaphore_wait(barrier, nb + nf - 2)

        @pl.when(t < nb - 1)
        def _():
            share_copy(t).start()

        @pl.when(t == 0)
        def _():
            small_work()
            each(1, nb, lambda t: spot_copy(t).start())

    each(0, nb, group)
    each(0, nb - 1, lambda t: share_copy(t).wait_recv())

    def sum_shares(j):
        m = send[nb - 1, j].astype(F32)
        for t in range(nb - 1):
            m = m + recv[t, j].astype(F32)
        return m

    chips = nf // 2
    turn = 1 - 2 * core + nf

    def core_copy(i):
        return freq_copy(total.at[1 - core, i], csum.at[i], core_s.at[i], core_r.at[i], turn)

    def sum_copy(d):
        return freq_copy(total.at[core, (place + d) % chips], fsum.at[d - 1], freq_s.at[d - 1], freq_r.at[d - 1], 2 * d)

    def offer(d):
        i = (place + d) % chips
        total[1 - core, i] = sum_shares(2 * i + 1 - core)
        core_copy(i).start()

    def join(i):
        m = sum_shares(2 * i + core)
        core_copy(i).wait_recv()
        return m + csum[i]

    def reduce(d):
        i = (place + d) % chips
        total[core, i] = join(i)
        sum_copy(d).start()

    each(1, chips + 1, offer)
    each(1, chips, reduce)
    m = join(place)
    each(1, chips, lambda d: sum_copy(d).wait_recv())
    for d in range(1, chips):
        m = m + fsum[d - 1]
    gath[me_f] = make_patch(m, cs[0], cs[1], left1[...], right1[...], left2[...], right2[...])

    def gath_copy(d):
        return freq_copy(gath.at[me_f], gath.at[me_f], gath_s.at[d - 1], gath_r.at[d - 1], 2 * d)

    def hand_copy(d):
        piece = gath.at[(me_f + nf - 2 * d) % nf]
        return freq_copy(piece, piece, hand_s.at[d], hand_r.at[d], turn)

    def hand_on(d):
        gath_copy(d).wait_recv()
        hand_copy(d).start()

    each(1, chips, lambda d: gath_copy(d).start())
    hand_copy(0).start()
    each(1, chips, hand_on)
    each(0, chips, lambda d: hand_copy(d).wait_recv())

    def out_copy(t):
        return base_copy(outb.at[peer(t, 1)], slots.at[core, me_b], out_s.at[t - 1], out_r.at[t - 1], t)

    def pick(o):
        return gath[choice[o]]

    def ship(t):
        o = peer(t, 1)
        outb[o] = pick(o)
        out_copy(t).start()

    each(1, nb, ship)
    slots[core, me_b] = pick(me_b)

    def pair_copy(t):
        source = peer(t, -1)
        part = slots.at[core, source]
        return pltpu.make_async_remote_copy(
            src_ref=part,
            dst_ref=part,
            send_sem=pair_s.at[t],
            recv_sem=pair_r.at[t],
            device_id={"freq": me_f + 1 - 2 * core},
            device_id_type=MESH,
        )

    pair_copy(0).start()

    def forward(t):
        out_copy(t).wait_recv()
        pair_copy(t).start()

    each(1, nb, forward)
    each(0, nb, lambda t: pair_copy(t).wait())
    each(1, nb, lambda t: out_copy(t).wait_send())
    each(1, chips, lambda d: gath_copy(d).wait_send())
    each(0, chips, lambda d: hand_copy(d).wait_send())
    each(1, chips, lambda d: sum_copy(d).wait_send())
    each(0, chips, lambda i: core_copy(i).wait_send())
    each(0, nb - 1, lambda t: share_copy(t).wait_send())
    each(1, nb, lambda t: spot_copy(t).wait())


def main(owner, row, col, w, vr, vi, co, nb, nf):
    own = w.shape[1]
    unit = (G, 2 * G)
    dma = pltpu.SemaphoreType.DMA
    consts = [stay(jnp.asarray(x)) for x in constants()]
    tabs = [pltpu.VMEM((2 * HALF, 128), F32), pltpu.VMEM((2 * HALF, 128), F32), pltpu.VMEM((16, 256), F32)]
    return pl.pallas_call(
        functools.partial(main_kernel, nb, nf),
        out_shape=(
            jax.ShapeDtypeStruct((FCAP, nb) + unit, F32),
            jax.ShapeDtypeStruct((nb, 128), jnp.int32),
        ),
        in_specs=[hbm()] * 8 + [vmem()] * 3,
        out_specs=(vmem(), vmem()),
        scratch_shapes=[
            pltpu.SMEM((1, own), jnp.int32),
            pltpu.SMEM((1, own), jnp.int32),
            pltpu.SMEM((1, own), jnp.int32),
            pltpu.SMEM((1, own), F32),
        ]
        + [pltpu.VMEM(x.shape, BF16) for x in consts]
        + [pltpu.VMEM((nb, 128), jnp.int32)]
        + tabs * 2
        + [
            pltpu.VMEM((2,) + unit, F32),
            pltpu.VMEM((nb, own) + unit, BF16),
            pltpu.VMEM((nb - 1, own) + unit, BF16),
            pltpu.VMEM((2, nf // 2) + unit, F32),
            pltpu.VMEM((nf // 2,) + unit, F32),
            pltpu.VMEM((nf // 2 - 1,) + unit, F32),
            pltpu.VMEM((nf,) + unit, F32),
            pltpu.VMEM((nb,) + unit, F32),
            pltpu.SMEM((nb,), jnp.int32),
            dma((8,)),
            dma((nb - 1,)),
            dma((nb - 1,)),
            dma((nb - 1,)),
            dma((nb - 1,)),
            dma((nf // 2,)),
            dma((nf // 2,)),
            dma((nf // 2 - 1,)),
            dma((nf // 2 - 1,)),
            dma((nf // 2 - 1,)),
            dma((nf // 2 - 1,)),
            dma((nf // 2,)),
            dma((nf // 2,)),
            dma((nb - 1,)),
            dma((nb - 1,)),
            dma((nb,)),
            dma((nb,)),
        ],
        compiler_params=pltpu.CompilerParams(
            vmem_limit_bytes=48 << 20, collective_id=0, has_side_effects=True
        ),
        name="main",
    )(owner, row, col, w, *consts, vr, vi, co)


def deposit_kernel(table_ref, slot_ref, grid_in, grid_ref, zeros, blocks, where_ref, tile_ref, count_ref, sem, zsem):
    del grid_in
    zeros[...] = jnp.zeros(zeros.shape, F32)
    clears = [clear_copy(zeros, grid_ref, zsem, i, EARLY) for i in range(EARLY, PIECES)]
    for clear in clears:
        clear.start()
    tiles = GY // 128

    def reset(i, carry):
        where_ref[i] = -1
        return carry

    lax.fori_loop(0, tiles, reset, 0)
    count_ref[0] = 0
    lane = lax.broadcasted_iota(jnp.int32, (G + 8, 128), 1)

    def block_of(tile):
        @pl.when(where_ref[tile] < 0)
        def _():
            count = count_ref[0]
            where_ref[tile] = count
            tile_ref[count] = tile
            count_ref[0] = count + 1
            blocks[count] = jnp.zeros(blocks.shape[1:], F32)

        return where_ref[tile]

    def place(b, rank):
        row = table_ref[b, 3 * rank + 1]
        r = pl.ds(pl.multiple_of(row // 8 * 8, 8), G + 8)
        col = table_ref[b, 3 * rank + 2]
        tile = col // 128
        c = col % 128
        patch = jnp.concatenate([slot_ref[rank, b], jnp.zeros((8, 2 * G), F32)], axis=0)
        patch = pltpu.roll(patch, row % 8, 0)
        real = pltpu.roll(jnp.where(lane < G, patch, 0.0), c, 1)
        imag = pltpu.roll(jnp.where(lane < G, 0.0, patch), c + G, 1)
        first = block_of(tile)
        blocks[first, 0, r, :] += jnp.where(lane >= c, real, 0.0)
        blocks[first, 1, r, :] += jnp.where(lane >= c, imag, 0.0)

        @pl.when(c > 128 - G)
        def _():
            second = block_of(tile + 1)
            blocks[second, 0, r, :] += jnp.where(lane < c, real, 0.0)
            blocks[second, 1, r, :] += jnp.where(lane < c, imag, 0.0)

    def source(b, carry):
        for rank in range(FCAP):

            @pl.when(table_ref[b, 3 * rank] > 0)
            def _():
                place(b, rank)

        return carry

    lax.fori_loop(0, table_ref.shape[0], source, 0)
    count = count_ref[0]

    def copy(i):
        cut = pl.ds(pl.multiple_of(tile_ref[i] * 128, 128), 128)
        return pltpu.make_async_copy(blocks.at[i, :, 0:FR, :], grid_ref.at[:, :, cut], sem.at[i])

    def start(i, carry):
        copy(i).start()
        return carry

    def wait(i, carry):
        copy(i).wait()
        return carry

    for clear in clears:
        clear.wait()
    lax.fori_loop(0, count, start, 0)
    lax.fori_loop(0, count, wait, 0)


def deposit(table, slots, grid):
    most = 2 * slots.shape[0] * slots.shape[1]
    return pl.pallas_call(
        deposit_kernel,
        out_shape=jax.ShapeDtypeStruct((2, FR, GY), F32),
        in_specs=[smem(), vmem(), hbm()],
        out_specs=hbm(),
        scratch_shapes=[
            pltpu.VMEM((FR, CLEAR), F32),
            pltpu.VMEM((most, 2, FR + 8, 128), F32),
            pltpu.SMEM((GY // 128,), jnp.int32),
            pltpu.SMEM((most,), jnp.int32),
            pltpu.SMEM((1,), jnp.int32),
            pltpu.SemaphoreType.DMA((most,)),
            pltpu.SemaphoreType.DMA((PIECES - EARLY,)),
        ],
        input_output_aliases={2: 0},
        compiler_params=pltpu.CompilerParams(vmem_limit_bytes=48 << 20),
        name="deposit",
    )(table, slots, grid)


def per_device(visibilities, anchor, drift, target, subgrid_w, facet_owner, row_offset, col_offset):
    nb, nf = lax.axis_size("base"), lax.axis_size("freq")
    target = target.reshape(1, -1)
    vr, vi, co, grid = prep(*[stay(x) for x in (target, visibilities, anchor, drift)])
    small = [stay(x.reshape(1, -1)) for x in (facet_owner, row_offset, col_offset, subgrid_w)]
    slots, table = main(*small, vr, vi, co, nb, nf)
    return deposit(table, slots, grid)


def solution(mesh):
    return jax.shard_map(
        per_device,
        mesh=mesh,
        in_specs=(
            P(None, "base", "freq"),
            P(None, "base"),
            P(None, "base"),
            P("base", None),
            P("base"),
            P("base", None),
            P("base"),
            P("base"),
        ),
        out_specs=P(None, "base", None),
        check_vma=False,
    )
```

```python
import functools
import math

import jax
import jax.numpy as jnp
import numpy as np
from jax import lax
from jax.experimental import pallas as pl
from jax.experimental.pallas import tpu as pltpu
from jax.sharding import PartitionSpec as P

G = 64
GY = 16384
CAP = 8
FCAP = 2
FR = 128
NT = (((1,), (1,)), ((), ()))
F32 = jnp.float32
BF16 = jnp.bfloat16
VMEM = pltpu.MemorySpace.VMEM
SMEM = pltpu.MemorySpace.SMEM


def vmem():
    return pl.BlockSpec(memory_space=VMEM)


def hbm():
    return pl.BlockSpec(memory_space=pltpu.MemorySpace.HBM)


def stay(x):
    return pltpu.with_memory_space_constraint(x, pltpu.MemorySpace.HBM)


def smem():
    return pl.BlockSpec(memory_space=SMEM)


CLEAR = 2048
PIECES = 2 * GY // CLEAR
EARLY = PIECES - 5


def clear_copy(zeros, grid_ref, sem, i, first):
    j = i % (GY // CLEAR)
    part = grid_ref.at[i // (GY // CLEAR), :, CLEAR * j : CLEAR * (j + 1)]
    return pltpu.make_async_copy(zeros, part, sem.at[i - first])


def prep_kernel(
    target_hbm, vis_hbm, anchor_hbm, drift_hbm, vr_ref, vi_ref, co_ref, grid_ref, target_ref, vis_ref, anchor_ref, drift_ref, pick_ref, zeros, sem, zsem
):
    pairs = [(target_hbm, target_ref), (vis_hbm, vis_ref), (anchor_hbm, anchor_ref), (drift_hbm, drift_ref)]
    loads = [pltpu.make_async_copy(src, dst, sem.at[i]) for i, (src, dst) in enumerate(pairs)]
    for load in loads:
        load.start()
    zeros[...] = jnp.zeros(zeros.shape, F32)
    clears = [clear_copy(zeros, grid_ref, zsem, i, 0) for i in range(EARLY)]
    for clear in clears:
        clear.start()
    loads[0].wait()
    blocks = target_ref.shape[1]
    groups = blocks // CAP
    width = 128
    rows = lax.broadcasted_iota(jnp.int32, (width, width), 0)
    lanes = lax.broadcasted_iota(jnp.int32, (width, width), 1)
    count = jnp.concatenate([(rows < lanes).astype(F32), jnp.ones((width, width), F32)], axis=1)
    ids = lax.broadcasted_iota(jnp.int32, (groups, width), 0)
    pieces = range(blocks // width)
    targets = [target_ref[:, width * i : width * (i + 1)] for i in pieces]
    hits = [(ids == target).astype(F32) for target in targets]
    counts = jnp.dot(
        jnp.concatenate(hits, axis=0).astype(BF16), count.astype(BF16), preferred_element_type=F32
    )
    seen = jnp.zeros((groups, width), F32)
    placed = []
    for i in pieces:
        inside = counts[groups * i : groups * (i + 1)]
        ranking = jnp.sum((inside[:, :width] + seen) * hits[i], axis=0, keepdims=True)
        placed.append(targets[i] * CAP + ranking.astype(jnp.int32))
        seen = seen + inside[:, width:]
    placed = jnp.concatenate(placed, axis=1)
    step = 128

    def choose(i, carry):
        start = pl.multiple_of(i * step, step)
        match = lax.broadcasted_iota(jnp.int32, (step, blocks), 0) + start == placed
        pick_ref[pl.ds(start, step), :] = match.astype(F32).astype(BF16)
        return carry

    lax.fori_loop(0, blocks // step, choose, 0)
    for load in loads[1:]:
        load.wait()
    pick = pick_ref[...]
    places = jnp.concatenate([anchor_ref[...].astype(F32), drift_ref[...].astype(F32)], axis=0).astype(BF16)
    co_ref[...] = lax.dot_general(pick, places, NT, preferred_element_type=F32)
    vr_ref[...] = jnp.dot(pick, vis_ref[0], preferred_element_type=F32)
    vi_ref[...] = jnp.dot(pick, vis_ref[1], preferred_element_type=F32)
    for clear in clears:
        clear.wait()


def prep(target, visibilities, anchor, drift):
    _, blocks, channels = visibilities.shape
    return pl.pallas_call(
        prep_kernel,
        out_shape=(
            jax.ShapeDtypeStruct((blocks, channels), F32),
            jax.ShapeDtypeStruct((blocks, channels), F32),
            jax.ShapeDtypeStruct((blocks, 4), F32),
            jax.ShapeDtypeStruct((2, FR, GY), F32),
        ),
        in_specs=[hbm()] * 4,
        out_specs=(vmem(), vmem(), vmem(), hbm()),
        scratch_shapes=[
            pltpu.VMEM((1, blocks), jnp.int32),
            pltpu.VMEM(visibilities.shape, BF16),
            pltpu.VMEM(anchor.shape, BF16),
            pltpu.VMEM(drift.shape, BF16),
            pltpu.VMEM((blocks, blocks), BF16),
            pltpu.VMEM((FR, CLEAR), F32),
            pltpu.SemaphoreType.DMA((4,)),
            pltpu.SemaphoreType.DMA((EARLY,)),
        ],
        compiler_params=pltpu.CompilerParams(vmem_limit_bytes=48 << 20),
        name="prep",
    )(target, visibilities, anchor, drift)


def trig(h):
    z = h * h
    s = 1 / 362880 + z * (-1 / 39916800)
    s = h * (1.0 + z * (-1 / 6 + z * (1 / 120 + z * (-1 / 5040 + z * s))))
    c = -1 / 3628800 + z * (1 / 479001600)
    c = 1.0 + z * (-0.5 + z * (1 / 24 + z * (-1 / 720 + z * (1 / 40320 + z * c))))
    return c, s


HALF = 152


def put(tab, row, v):
    tab[row : row + 8, :] = v[:, :128]
    tab[HALF + row : HALF + row + 8, :] = v[:, 128:]


def base_rows(h, tab):
    c0, s0 = trig(h)
    k1 = 4.0 * c0 * c0 - 2.0
    k2 = k1 * k1 - 2.0
    k4 = k2 * k2 - 2.0
    k8 = k4 * k4 - 2.0
    s8 = (2.0 * s0 * c0) * k1 * k2 * k4
    cp, cc = c0, (k1 - 1.0) * c0
    sp, sc = s0, (k1 + 1.0) * s0
    put(tab, 0, c0)
    put(tab, 64, s0)
    for p in range(1, 8):
        put(tab, 8 * p, cc)
        put(tab, 64 + 8 * p, sc)
        cp, cc = cc, k1 * cc - cp
        sp, sc = sc, k1 * sc - sp
    put(tab, 128, k8)
    put(tab, 136, 0.5 * k8)
    put(tab, 144, s8)
    return c0, s0


def expand(tab, s, h):
    o = HALF * h
    k8 = tab[o + 128 + s : o + 129 + s, :]
    c8 = tab[o + 136 + s : o + 137 + s, :]
    s8 = tab[o + 144 + s : o + 145 + s, :]
    a0 = tab[pl.ds(o + s, 8, stride=8), :]
    b0 = tab[pl.ds(o + 64 + s, 8, stride=8), :]
    a1 = c8 * a0 - s8 * b0
    b1 = c8 * b0 + s8 * a0
    a2 = k8 * a1 - a0
    b2 = k8 * b1 - b0
    a3 = k8 * a2 - a1
    b3 = k8 * b2 - b1
    return jnp.concatenate([a0, a1, a2, a3, b0, b1, b2, b3], axis=0)


def tables(g, chan, vr_ref, vi_ref, co_ref, tx, ty, tv):
    rows = pl.ds(pl.multiple_of(8 * g, 8), 8)
    co = co_ref[rows, :]
    hx = (co[:, 0:1] - 0.5 * G + chan * co[:, 2:3]) * (math.pi / G)
    hy = (co[:, 1:2] - 0.5 * G + chan * co[:, 3:4]) * (math.pi / G)
    cx, sx = base_rows(hx, tx)
    cy, sy = base_rows(hy, ty)
    er = cx * cy - sx * sy
    ei = cx * sy + sx * cy
    vr = vr_ref[rows, :]
    vi = vi_ref[rows, :]
    tv[0:8, :] = vr * er + vi * ei
    tv[8:16, :] = vi * er - vr * ei


def products(tx, ty, tv):
    acc = None
    for s in range(8):
        f = jnp.concatenate([expand(tx, s, h).astype(BF16) for h in (0, 1)], axis=1)
        parts = []
        for h in (0, 1):
            g0 = expand(ty, s, h)
            cut = slice(128 * h, 128 * h + 128)
            both = [g0 * tv[s : s + 1, cut], g0 * tv[8 + s : 9 + s, cut]]
            parts.append(jnp.concatenate(both, axis=0).astype(BF16))
        r = jnp.concatenate(parts, axis=1)
        d = lax.dot_general(f, r, NT, preferred_element_type=F32)
        acc = d if acc is None else acc + d
    return acc


def constants():
    l = np.arange(G) - G // 2 + 0.5
    p = np.arange(G // 2) + 0.5
    same = (np.abs(l)[:, None] == p[None, :]).astype(np.float64)
    a = np.concatenate([same, 0 * same], axis=1)
    b = np.concatenate([0 * same, same * np.sign(l)[:, None]], axis=1)
    turns = 2 * np.pi * ((np.arange(G)[:, None] * np.arange(G)[None, :]) % G) / G
    fr, fi = np.cos(turns), -np.sin(turns)
    left1 = np.concatenate([a, b], axis=0)
    right1 = np.block([[a.T, b.T], [-b.T, a.T]])
    left2 = np.concatenate([fr, fi], axis=0)
    right2 = np.block([[fr, fi], [-fi, fr]]) / G

    def split(x):
        high = x.astype(jnp.bfloat16)
        return high, (x - high.astype(np.float64)).astype(jnp.bfloat16)

    one_l, _ = split(left1)
    one_r, _ = split(right1)
    two_l, two_ll = split(left2)
    two_r, two_rl = split(right2)
    return [
        np.concatenate([one_l, one_l], axis=1),
        np.concatenate([one_r, one_r], axis=0),
        np.concatenate([two_l, two_l, two_ll, 0 * two_l], axis=1),
        np.concatenate([two_r, two_r, two_rl], axis=0),
    ]


def split_rows(x, times, axis):
    high = x.astype(BF16)
    low = (x - high.astype(F32)).astype(BF16)
    return jnp.concatenate(([high, low] + [high] * 2)[:times], axis=axis)


def dot16(a, b):
    return jnp.dot(a, b, preferred_element_type=F32)


def swap(x):
    return pltpu.roll(x, G, 1)


def screen(w):
    row = lax.broadcasted_iota(jnp.int32, (G, 2 * G), 0)
    lane = lax.broadcasted_iota(jnp.int32, (G, 2 * G), 1)
    xl = (row - G // 2).astype(F32) * (2.0 / G)
    xm = (jnp.where(lane < G, lane, lane - G) - G // 2).astype(F32) * (2.0 / G)
    c, s = trig((0.25 * math.pi) * w * (xl * xl + xm * xm))
    for _ in range(2):
        c, s = 2.0 * c * c - 1.0, 2.0 * c * s
    return c, jnp.where(lane < G, -s, s)


def make_patch(m, c, s, left1, right1, left2, right2):
    lane = lax.broadcasted_iota(jnp.int32, (G, 2 * G), 1)
    sign = jnp.where(lane < G, -1.0, 1.0).astype(F32)
    both = dot16(left1, split_rows(m, 2, 0))
    y = both[:G] + sign * swap(both[G:])
    z = dot16(split_rows(y, 2, 1), right1)
    k = z * c + swap(z) * s
    both = dot16(left2, split_rows(k, 4, 0))
    y = both[:G] + sign * swap(both[G:])
    return dot16(split_rows(y, 3, 1), right2)


MESH = pl.DeviceIdType.MESH


def main_kernel(
    nb,
    nf,
    owner_hbm,
    row_hbm,
    col_hbm,
    w_hbm,
    left1_hbm,
    right1_hbm,
    left2_hbm,
    right2_hbm,
    vr_ref,
    vi_ref,
    co_ref,
    slots,
    table,
    owner_ref,
    row_ref,
    col_ref,
    w_ref,
    left1,
    right1,
    left2,
    right2,
    spot_ref,
    tx0,
    ty0,
    tv0,
    tx1,
    ty1,
    tv1,
    cs,
    send,
    recv,
    total,
    fsum,
    gath,
    outb,
    choice,
    load_sem,
    spot_s,
    spot_r,
    base_s,
    base_r,
    freq_s,
    freq_r,
    gath_s,
    gath_r,
    hand_s,
    hand_r,
    out_s,
    out_r,
    pair_s,
    pair_r,
):
    me_b = lax.axis_index("base")
    me_f = lax.axis_index("freq")
    own = total.shape[0]
    core = me_f % 2
    even = (tx0, ty0, tv0)
    odd = (tx1, ty1, tv1)

    side = math.isqrt(nb)

    def peer(t, sign):
        z = (me_b // side + side + sign * (t % side)) % side
        y = (me_b % side + side + sign * ((t // side + t) % side)) % side
        return z * side + y

    def base_copy(src, dst, ss, rs, t):
        return pltpu.make_async_remote_copy(
            src_ref=src, dst_ref=dst, send_sem=ss, recv_sem=rs, device_id={"base": peer(t, 1)}, device_id_type=MESH
        )

    def freq_copy(src, dst, ss, rs, d):
        return pltpu.make_async_remote_copy(
            src_ref=src, dst_ref=dst, send_sem=ss, recv_sem=rs, device_id={"freq": (me_f + d) % nf}, device_id_type=MESH
        )

    def each(low, high, body):
        def step(i, carry):
            body(i)
            return carry

        lax.fori_loop(low, high, step, 0)

    barrier = pltpu.get_barrier_semaphore()
    each(1, nb, lambda t: pl.semaphore_signal(barrier, inc=1, device_id={"base": (me_b + t) % nb}, device_id_type=MESH))
    each(1, nf, lambda d: pl.semaphore_signal(barrier, inc=1, device_id={"freq": (me_f + d) % nf}, device_id_type=MESH))
    pairs = [
        (owner_hbm, owner_ref),
        (row_hbm, row_ref),
        (col_hbm, col_ref),
        (w_hbm, w_ref),
        (left1_hbm, left1),
        (right1_hbm, right1),
        (left2_hbm, left2),
        (right2_hbm, right2),
    ]
    loads = [pltpu.make_async_copy(src, dst, load_sem.at[i]) for i, (src, dst) in enumerate(pairs)]
    for load in loads:
        load.start()

    channels = vr_ref.shape[1]
    chan = (lax.broadcasted_iota(jnp.int32, (8, channels), 1) + me_f * channels).astype(F32)

    def subgrid(i):
        return peer(i // own + 1, 1) * own + i % own

    def prepare(i, tabs):
        tables(subgrid(i), chan, vr_ref, vi_ref, co_ref, *tabs)

    def spot_copy(t):
        return base_copy(spot_ref.at[pl.ds(peer(t, 1), 1)], table.at[pl.ds(me_b, 1)], spot_s.at[t - 1], spot_r.at[t - 1], t)

    def share_copy(t):
        return base_copy(send.at[t], recv.at[t], base_s.at[t], base_r.at[t], t + 1)

    prepare(0, even)
    lane = lax.broadcasted_iota(jnp.int32, (1, 128), 1)

    def choose(o):
        seen = jnp.int32(0)
        index = [jnp.int32(0)] * FCAP
        for s in range(own):
            hit = (owner_ref[0, s] == o).astype(jnp.int32)
            index = [index[r] + hit * (seen == r).astype(jnp.int32) * s for r in range(FCAP)]
            seen = seen + hit
        choice[o] = index[0] * (1 - core) + index[1] * core
        spot = jnp.zeros((1, 128), jnp.int32)
        for r in range(FCAP):
            fields = ((seen > r).astype(jnp.int32), row_ref[0, index[r]], col_ref[0, index[r]])
            for n, value in enumerate(fields):
                spot = jnp.where(lane == 3 * r + n, value, spot)
        spot_ref[pl.ds(o, 1), :] = spot

    def small_work():
        for load in loads:
            load.wait()
        c, s = screen(w_ref[0, me_f])
        cs[0] = c
        cs[1] = s
        each(0, nb, choose)
        table[pl.ds(me_b, 1), :] = spot_ref[pl.ds(me_b, 1), :]

    def group(t):
        def two(u):
            i = t * own + 2 * u
            prepare(i + 1, odd)
            send[t, 2 * u] = products(*even).astype(BF16)
            prepare(i + 2, even)
            send[t, 2 * u + 1] = products(*odd).astype(BF16)

        for u in range(own // 2):
            two(u)

        @pl.when(t == 0)
        def _():
            pl.semaphore_wait(barrier, nb + nf - 2)

        @pl.when(t < nb - 1)
        def _():
            share_copy(t).start()

        @pl.when(t == 0)
        def _():
            small_work()
            each(1, nb, lambda t: spot_copy(t).start())

    each(0, nb, group)
    each(0, nb - 1, lambda t: share_copy(t).wait_recv())

    def sum_shares(j):
        m = send[nb - 1, j].astype(F32)
        for t in range(nb - 1):
            m = m + recv[t, j].astype(F32)
        return m

    def sum_copy(d):
        return freq_copy(total.at[(me_f + d) % nf], fsum.at[d - 1], freq_s.at[d - 1], freq_r.at[d - 1], d)

    def reduce(d):
        j = (me_f + d) % nf
        total[j] = sum_shares(j)
        sum_copy(d).start()

    each(1, nf, reduce)
    m = sum_shares(me_f)
    each(1, nf, lambda d: sum_copy(d).wait_recv())
    for d in range(1, nf):
        m = m + fsum[d - 1]
    gath[me_f] = make_patch(m, cs[0], cs[1], left1[...], right1[...], left2[...], right2[...])

    chips = nf // 2
    turn = 1 - 2 * core + nf

    def gath_copy(d):
        return freq_copy(gath.at[me_f], gath.at[me_f], gath_s.at[d - 1], gath_r.at[d - 1], 2 * d)

    def hand_copy(d):
        piece = gath.at[(me_f + nf - 2 * d) % nf]
        return freq_copy(piece, piece, hand_s.at[d], hand_r.at[d], turn)

    def hand_on(d):
        gath_copy(d).wait_recv()
        hand_copy(d).start()

    each(1, chips, lambda d: gath_copy(d).start())
    hand_copy(0).start()
    each(1, chips, hand_on)
    each(0, chips, lambda d: hand_copy(d).wait_recv())

    def out_copy(t):
        return base_copy(outb.at[peer(t, 1)], slots.at[core, me_b], out_s.at[t - 1], out_r.at[t - 1], t)

    def pick(o):
        return gath[choice[o]]

    def ship(t):
        o = peer(t, 1)
        outb[o] = pick(o)
        out_copy(t).start()

    each(1, nb, ship)
    slots[core, me_b] = pick(me_b)

    def pair_copy(t):
        source = peer(t, -1)
        part = slots.at[core, source]
        return pltpu.make_async_remote_copy(
            src_ref=part,
            dst_ref=part,
            send_sem=pair_s.at[t],
            recv_sem=pair_r.at[t],
            device_id={"freq": me_f + 1 - 2 * core},
            device_id_type=MESH,
        )

    pair_copy(0).start()

    def forward(t):
        out_copy(t).wait_recv()
        pair_copy(t).start()

    each(1, nb, forward)
    each(0, nb, lambda t: pair_copy(t).wait())
    each(1, nb, lambda t: out_copy(t).wait_send())
    each(1, chips, lambda d: gath_copy(d).wait_send())
    each(0, chips, lambda d: hand_copy(d).wait_send())
    each(1, nf, lambda d: sum_copy(d).wait_send())
    each(0, nb - 1, lambda t: share_copy(t).wait_send())
    each(1, nb, lambda t: spot_copy(t).wait())


def main(owner, row, col, w, vr, vi, co, nb, nf):
    own = w.shape[1]
    unit = (G, 2 * G)
    dma = pltpu.SemaphoreType.DMA
    consts = [stay(jnp.asarray(x)) for x in constants()]
    tabs = [pltpu.VMEM((2 * HALF, 128), F32), pltpu.VMEM((2 * HALF, 128), F32), pltpu.VMEM((16, 256), F32)]
    return pl.pallas_call(
        functools.partial(main_kernel, nb, nf),
        out_shape=(
            jax.ShapeDtypeStruct((FCAP, nb) + unit, F32),
            jax.ShapeDtypeStruct((nb, 128), jnp.int32),
        ),
        in_specs=[hbm()] * 8 + [vmem()] * 3,
        out_specs=(vmem(), vmem()),
        scratch_shapes=[
            pltpu.SMEM((1, own), jnp.int32),
            pltpu.SMEM((1, own), jnp.int32),
            pltpu.SMEM((1, own), jnp.int32),
            pltpu.SMEM((1, own), F32),
        ]
        + [pltpu.VMEM(x.shape, BF16) for x in consts]
        + [pltpu.VMEM((nb, 128), jnp.int32)]
        + tabs * 2
        + [
            pltpu.VMEM((2,) + unit, F32),
            pltpu.VMEM((nb, own) + unit, BF16),
            pltpu.VMEM((nb - 1, own) + unit, BF16),
            pltpu.VMEM((own,) + unit, F32),
            pltpu.VMEM((nf - 1,) + unit, F32),
            pltpu.VMEM((nf,) + unit, F32),
            pltpu.VMEM((nb,) + unit, F32),
            pltpu.SMEM((nb,), jnp.int32),
            dma((8,)),
            dma((nb - 1,)),
            dma((nb - 1,)),
            dma((nb - 1,)),
            dma((nb - 1,)),
            dma((nf - 1,)),
            dma((nf - 1,)),
            dma((nf // 2 - 1,)),
            dma((nf // 2 - 1,)),
            dma((nf // 2,)),
            dma((nf // 2,)),
            dma((nb - 1,)),
            dma((nb - 1,)),
            dma((nb,)),
            dma((nb,)),
        ],
        compiler_params=pltpu.CompilerParams(
            vmem_limit_bytes=48 << 20, collective_id=0, has_side_effects=True
        ),
        name="main",
    )(owner, row, col, w, *consts, vr, vi, co)


def deposit_kernel(table_ref, slot_ref, grid_in, grid_ref, zeros, blocks, where_ref, tile_ref, count_ref, sem, zsem):
    del grid_in
    zeros[...] = jnp.zeros(zeros.shape, F32)
    clears = [clear_copy(zeros, grid_ref, zsem, i, EARLY) for i in range(EARLY, PIECES)]
    for clear in clears:
        clear.start()
    tiles = GY // 128

    def reset(i, carry):
        where_ref[i] = -1
        return carry

    lax.fori_loop(0, tiles, reset, 0)
    count_ref[0] = 0
    lane = lax.broadcasted_iota(jnp.int32, (G + 8, 128), 1)

    def block_of(tile):
        @pl.when(where_ref[tile] < 0)
        def _():
            count = count_ref[0]
            where_ref[tile] = count
            tile_ref[count] = tile
            count_ref[0] = count + 1
            blocks[count] = jnp.zeros(blocks.shape[1:], F32)

        return where_ref[tile]

    def place(b, rank):
        row = table_ref[b, 3 * rank + 1]
        r = pl.ds(pl.multiple_of(row // 8 * 8, 8), G + 8)
        col = table_ref[b, 3 * rank + 2]
        tile = col // 128
        c = col % 128
        patch = jnp.concatenate([slot_ref[rank, b], jnp.zeros((8, 2 * G), F32)], axis=0)
        patch = pltpu.roll(patch, row % 8, 0)
        real = pltpu.roll(jnp.where(lane < G, patch, 0.0), c, 1)
        imag = pltpu.roll(jnp.where(lane < G, 0.0, patch), c + G, 1)
        first = block_of(tile)
        blocks[first, 0, r, :] += jnp.where(lane >= c, real, 0.0)
        blocks[first, 1, r, :] += jnp.where(lane >= c, imag, 0.0)

        @pl.when(c > 128 - G)
        def _():
            second = block_of(tile + 1)
            blocks[second, 0, r, :] += jnp.where(lane < c, real, 0.0)
            blocks[second, 1, r, :] += jnp.where(lane < c, imag, 0.0)

    def source(b, carry):
        for rank in range(FCAP):

            @pl.when(table_ref[b, 3 * rank] > 0)
            def _():
                place(b, rank)

        return carry

    lax.fori_loop(0, table_ref.shape[0], source, 0)
    count = count_ref[0]

    def copy(i):
        cut = pl.ds(pl.multiple_of(tile_ref[i] * 128, 128), 128)
        return pltpu.make_async_copy(blocks.at[i, :, 0:FR, :], grid_ref.at[:, :, cut], sem.at[i])

    def start(i, carry):
        copy(i).start()
        return carry

    def wait(i, carry):
        copy(i).wait()
        return carry

    for clear in clears:
        clear.wait()
    lax.fori_loop(0, count, start, 0)
    lax.fori_loop(0, count, wait, 0)


def deposit(table, slots, grid):
    most = 2 * slots.shape[0] * slots.shape[1]
    return pl.pallas_call(
        deposit_kernel,
        out_shape=jax.ShapeDtypeStruct((2, FR, GY), F32),
        in_specs=[smem(), vmem(), hbm()],
        out_specs=hbm(),
        scratch_shapes=[
            pltpu.VMEM((FR, CLEAR), F32),
            pltpu.VMEM((most, 2, FR + 8, 128), F32),
            pltpu.SMEM((GY // 128,), jnp.int32),
            pltpu.SMEM((most,), jnp.int32),
            pltpu.SMEM((1,), jnp.int32),
            pltpu.SemaphoreType.DMA((most,)),
            pltpu.SemaphoreType.DMA((PIECES - EARLY,)),
        ],
        input_output_aliases={2: 0},
        compiler_params=pltpu.CompilerParams(vmem_limit_bytes=48 << 20),
        name="deposit",
    )(table, slots, grid)


def per_device(visibilities, anchor, drift, target, subgrid_w, facet_owner, row_offset, col_offset):
    nb, nf = lax.axis_size("base"), lax.axis_size("freq")
    target = target.reshape(1, -1)
    vr, vi, co, grid = prep(*[stay(x) for x in (target, visibilities, anchor, drift)])
    small = [stay(x.reshape(1, -1)) for x in (facet_owner, row_offset, col_offset, subgrid_w)]
    slots, table = main(*small, vr, vi, co, nb, nf)
    return deposit(table, slots, grid)


def solution(mesh):
    return jax.shard_map(
        per_device,
        mesh=mesh,
        in_specs=(
            P(None, "base", "freq"),
            P(None, "base"),
            P(None, "base"),
            P("base", None),
            P("base"),
            P("base", None),
            P("base"),
            P("base"),
        ),
        out_specs=P(None, "base", None),
        check_vma=False,
    )
```

```python
import functools
import math

import jax
import jax.numpy as jnp
import numpy as np
from jax import lax
from jax.experimental import pallas as pl
from jax.experimental.pallas import tpu as pltpu
from jax.sharding import PartitionSpec as P

G = 64
GY = 16384
CAP = 8
FCAP = 2
FR = 128
NT = (((1,), (1,)), ((), ()))
F32 = jnp.float32
BF16 = jnp.bfloat16
VMEM = pltpu.MemorySpace.VMEM
SMEM = pltpu.MemorySpace.SMEM


def vmem():
    return pl.BlockSpec(memory_space=VMEM)


def hbm():
    return pl.BlockSpec(memory_space=pltpu.MemorySpace.HBM)


def stay(x):
    return pltpu.with_memory_space_constraint(x, pltpu.MemorySpace.HBM)


def smem():
    return pl.BlockSpec(memory_space=SMEM)


CLEAR = 2048
PIECES = 2 * GY // CLEAR
EARLY = PIECES - 5


def clear_copy(zeros, grid_ref, sem, i, first):
    j = i % (GY // CLEAR)
    part = grid_ref.at[i // (GY // CLEAR), :, CLEAR * j : CLEAR * (j + 1)]
    return pltpu.make_async_copy(zeros, part, sem.at[i - first])


def prep_kernel(
    target_hbm, vis_hbm, anchor_hbm, drift_hbm, vr_ref, vi_ref, co_ref, grid_ref, target_ref, vis_ref, anchor_ref, drift_ref, pick_ref, zeros, sem, zsem
):
    pairs = [(target_hbm, target_ref), (vis_hbm, vis_ref), (anchor_hbm, anchor_ref), (drift_hbm, drift_ref)]
    loads = [pltpu.make_async_copy(src, dst, sem.at[i]) for i, (src, dst) in enumerate(pairs)]
    for load in loads:
        load.start()
    zeros[...] = jnp.zeros(zeros.shape, F32)
    clears = [clear_copy(zeros, grid_ref, zsem, i, 0) for i in range(EARLY)]
    for clear in clears:
        clear.start()
    loads[0].wait()
    blocks = target_ref.shape[1]
    groups = blocks // CAP
    width = 128
    rows = lax.broadcasted_iota(jnp.int32, (width, width), 0)
    lanes = lax.broadcasted_iota(jnp.int32, (width, width), 1)
    count = jnp.concatenate([(rows < lanes).astype(F32), jnp.ones((width, width), F32)], axis=1)
    ids = lax.broadcasted_iota(jnp.int32, (groups, width), 0)
    pieces = range(blocks // width)
    targets = [target_ref[:, width * i : width * (i + 1)] for i in pieces]
    hits = [(ids == target).astype(F32) for target in targets]
    counts = jnp.dot(
        jnp.concatenate(hits, axis=0).astype(BF16), count.astype(BF16), preferred_element_type=F32
    )
    seen = jnp.zeros((groups, width), F32)
    placed = []
    for i in pieces:
        inside = counts[groups * i : groups * (i + 1)]
        ranking = jnp.sum((inside[:, :width] + seen) * hits[i], axis=0, keepdims=True)
        placed.append(targets[i] * CAP + ranking.astype(jnp.int32))
        seen = seen + inside[:, width:]
    placed = jnp.concatenate(placed, axis=1)
    step = 128

    def choose(i, carry):
        start = pl.multiple_of(i * step, step)
        match = lax.broadcasted_iota(jnp.int32, (step, blocks), 0) + start == placed
        pick_ref[pl.ds(start, step), :] = match.astype(F32).astype(BF16)
        return carry

    lax.fori_loop(0, blocks // step, choose, 0)
    for load in loads[1:]:
        load.wait()
    pick = pick_ref[...]
    places = jnp.concatenate([anchor_ref[...].astype(F32), drift_ref[...].astype(F32)], axis=0).astype(BF16)
    co_ref[...] = lax.dot_general(pick, places, NT, preferred_element_type=F32)
    vr_ref[...] = jnp.dot(pick, vis_ref[0], preferred_element_type=F32)
    vi_ref[...] = jnp.dot(pick, vis_ref[1], preferred_element_type=F32)
    for clear in clears:
        clear.wait()


def prep(target, visibilities, anchor, drift):
    _, blocks, channels = visibilities.shape
    return pl.pallas_call(
        prep_kernel,
        out_shape=(
            jax.ShapeDtypeStruct((blocks, channels), F32),
            jax.ShapeDtypeStruct((blocks, channels), F32),
            jax.ShapeDtypeStruct((blocks, 4), F32),
            jax.ShapeDtypeStruct((2, FR, GY), F32),
        ),
        in_specs=[hbm()] * 4,
        out_specs=(vmem(), vmem(), vmem(), hbm()),
        scratch_shapes=[
            pltpu.VMEM((1, blocks), jnp.int32),
            pltpu.VMEM(visibilities.shape, BF16),
            pltpu.VMEM(anchor.shape, BF16),
            pltpu.VMEM(drift.shape, BF16),
            pltpu.VMEM((blocks, blocks), BF16),
            pltpu.VMEM((FR, CLEAR), F32),
            pltpu.SemaphoreType.DMA((4,)),
            pltpu.SemaphoreType.DMA((EARLY,)),
        ],
        compiler_params=pltpu.CompilerParams(vmem_limit_bytes=48 << 20),
        name="prep",
    )(target, visibilities, anchor, drift)


def trig(h):
    z = h * h
    s = 1 / 362880 + z * (-1 / 39916800)
    s = h * (1.0 + z * (-1 / 6 + z * (1 / 120 + z * (-1 / 5040 + z * s))))
    c = -1 / 3628800 + z * (1 / 479001600)
    c = 1.0 + z * (-0.5 + z * (1 / 24 + z * (-1 / 720 + z * (1 / 40320 + z * c))))
    return c, s


HALF = 152


def put(tab, row, v):
    tab[row : row + 8, :] = v[:, :128]
    tab[HALF + row : HALF + row + 8, :] = v[:, 128:]


def base_rows(h, tab):
    c0, s0 = trig(h)
    k1 = 4.0 * c0 * c0 - 2.0
    k2 = k1 * k1 - 2.0
    k4 = k2 * k2 - 2.0
    k8 = k4 * k4 - 2.0
    s8 = (2.0 * s0 * c0) * k1 * k2 * k4
    cp, cc = c0, (k1 - 1.0) * c0
    sp, sc = s0, (k1 + 1.0) * s0
    put(tab, 0, c0)
    put(tab, 64, s0)
    for p in range(1, 8):
        put(tab, 8 * p, cc)
        put(tab, 64 + 8 * p, sc)
        cp, cc = cc, k1 * cc - cp
        sp, sc = sc, k1 * sc - sp
    put(tab, 128, k8)
    put(tab, 136, 0.5 * k8)
    put(tab, 144, s8)
    return c0, s0


def expand(tab, s, h):
    o = HALF * h
    k8 = tab[o + 128 + s : o + 129 + s, :]
    c8 = tab[o + 136 + s : o + 137 + s, :]
    s8 = tab[o + 144 + s : o + 145 + s, :]
    a0 = tab[pl.ds(o + s, 8, stride=8), :]
    b0 = tab[pl.ds(o + 64 + s, 8, stride=8), :]
    a1 = c8 * a0 - s8 * b0
    b1 = c8 * b0 + s8 * a0
    a2 = k8 * a1 - a0
    b2 = k8 * b1 - b0
    a3 = k8 * a2 - a1
    b3 = k8 * b2 - b1
    return jnp.concatenate([a0, a1, a2, a3, b0, b1, b2, b3], axis=0)


def tables(g, chan, vr_ref, vi_ref, co_ref, tx, ty, tv):
    rows = pl.ds(pl.multiple_of(8 * g, 8), 8)
    co = co_ref[rows, :]
    hx = (co[:, 0:1] - 0.5 * G + chan * co[:, 2:3]) * (math.pi / G)
    hy = (co[:, 1:2] - 0.5 * G + chan * co[:, 3:4]) * (math.pi / G)
    cx, sx = base_rows(hx, tx)
    cy, sy = base_rows(hy, ty)
    er = cx * cy - sx * sy
    ei = cx * sy + sx * cy
    vr = vr_ref[rows, :]
    vi = vi_ref[rows, :]
    tv[0:8, :] = vr * er + vi * ei
    tv[8:16, :] = vi * er - vr * ei


def products(tx, ty, tv):
    acc = None
    for s in range(8):
        f = jnp.concatenate([expand(tx, s, h).astype(BF16) for h in (0, 1)], axis=1)
        parts = []
        for h in (0, 1):
            g0 = expand(ty, s, h)
            cut = slice(128 * h, 128 * h + 128)
            both = [g0 * tv[s : s + 1, cut], g0 * tv[8 + s : 9 + s, cut]]
            parts.append(jnp.concatenate(both, axis=0).astype(BF16))
        r = jnp.concatenate(parts, axis=1)
        d = lax.dot_general(f, r, NT, preferred_element_type=F32)
        acc = d if acc is None else acc + d
    return acc


def constants():
    l = np.arange(G) - G // 2 + 0.5
    p = np.arange(G // 2) + 0.5
    same = (np.abs(l)[:, None] == p[None, :]).astype(np.float64)
    a = np.concatenate([same, 0 * same], axis=1)
    b = np.concatenate([0 * same, same * np.sign(l)[:, None]], axis=1)
    turns = 2 * np.pi * ((np.arange(G)[:, None] * np.arange(G)[None, :]) % G) / G
    fr, fi = np.cos(turns), -np.sin(turns)
    left1 = np.concatenate([a, b], axis=0)
    right1 = np.block([[a.T, b.T], [-b.T, a.T]])
    left2 = np.concatenate([fr, fi], axis=0)
    right2 = np.block([[fr, fi], [-fi, fr]]) / G

    def split(x):
        high = x.astype(jnp.bfloat16)
        return high, (x - high.astype(np.float64)).astype(jnp.bfloat16)

    one_l, _ = split(left1)
    one_r, _ = split(right1)
    two_l, two_ll = split(left2)
    two_r, two_rl = split(right2)
    return [
        np.concatenate([one_l, one_l], axis=1),
        np.concatenate([one_r, one_r], axis=0),
        np.concatenate([two_l, two_l, two_ll, 0 * two_l], axis=1),
        np.concatenate([two_r, two_r, two_rl], axis=0),
    ]


def split_rows(x, times, axis):
    high = x.astype(BF16)
    low = (x - high.astype(F32)).astype(BF16)
    return jnp.concatenate(([high, low] + [high] * 2)[:times], axis=axis)


def dot16(a, b):
    return jnp.dot(a, b, preferred_element_type=F32)


def swap(x):
    return pltpu.roll(x, G, 1)


def screen(w):
    row = lax.broadcasted_iota(jnp.int32, (G, 2 * G), 0)
    lane = lax.broadcasted_iota(jnp.int32, (G, 2 * G), 1)
    xl = (row - G // 2).astype(F32) * (2.0 / G)
    xm = (jnp.where(lane < G, lane, lane - G) - G // 2).astype(F32) * (2.0 / G)
    c, s = trig((0.25 * math.pi) * w * (xl * xl + xm * xm))
    for _ in range(2):
        c, s = 2.0 * c * c - 1.0, 2.0 * c * s
    return c, jnp.where(lane < G, -s, s)


def make_patch(m, c, s, left1, right1, left2, right2):
    lane = lax.broadcasted_iota(jnp.int32, (G, 2 * G), 1)
    sign = jnp.where(lane < G, -1.0, 1.0).astype(F32)
    both = dot16(left1, split_rows(m, 2, 0))
    y = both[:G] + sign * swap(both[G:])
    z = dot16(split_rows(y, 2, 1), right1)
    k = z * c + swap(z) * s
    both = dot16(left2, split_rows(k, 4, 0))
    y = both[:G] + sign * swap(both[G:])
    return dot16(split_rows(y, 3, 1), right2)


MESH = pl.DeviceIdType.MESH


def main_kernel(
    nb,
    nf,
    owner_hbm,
    row_hbm,
    col_hbm,
    w_hbm,
    left1_hbm,
    right1_hbm,
    left2_hbm,
    right2_hbm,
    vr_ref,
    vi_ref,
    co_ref,
    slots,
    table,
    owner_ref,
    row_ref,
    col_ref,
    w_ref,
    left1,
    right1,
    left2,
    right2,
    spot_ref,
    tx0,
    ty0,
    tv0,
    tx1,
    ty1,
    tv1,
    cs,
    send,
    recv,
    total,
    fsum,
    gath,
    outb,
    choice,
    load_sem,
    spot_s,
    spot_r,
    base_s,
    base_r,
    freq_s,
    freq_r,
    gath_s,
    gath_r,
    hand_s,
    hand_r,
    out_s,
    out_r,
    pair_s,
    pair_r,
):
    me_b = lax.axis_index("base")
    me_f = lax.axis_index("freq")
    own = total.shape[0]
    core = me_f % 2
    even = (tx0, ty0, tv0)
    odd = (tx1, ty1, tv1)

    side = math.isqrt(nb)

    def peer(t, sign):
        z = (me_b // side + side + sign * (t % side)) % side
        y = (me_b % side + side + sign * ((t // side + t) % side)) % side
        return z * side + y

    def base_copy(src, dst, ss, rs, t):
        return pltpu.make_async_remote_copy(
            src_ref=src, dst_ref=dst, send_sem=ss, recv_sem=rs, device_id={"base": peer(t, 1)}, device_id_type=MESH
        )

    def freq_copy(src, dst, ss, rs, d):
        return pltpu.make_async_remote_copy(
            src_ref=src, dst_ref=dst, send_sem=ss, recv_sem=rs, device_id={"freq": (me_f + d) % nf}, device_id_type=MESH
        )

    def each(low, high, body):
        def step(i, carry):
            body(i)
            return carry

        lax.fori_loop(low, high, step, 0)

    barrier = pltpu.get_barrier_semaphore()
    each(1, nb, lambda t: pl.semaphore_signal(barrier, inc=1, device_id={"base": (me_b + t) % nb}, device_id_type=MESH))
    each(1, nf, lambda d: pl.semaphore_signal(barrier, inc=1, device_id={"freq": (me_f + d) % nf}, device_id_type=MESH))
    pairs = [
        (owner_hbm, owner_ref),
        (row_hbm, row_ref),
        (col_hbm, col_ref),
        (w_hbm, w_ref),
        (left1_hbm, left1),
        (right1_hbm, right1),
        (left2_hbm, left2),
        (right2_hbm, right2),
    ]
    loads = [pltpu.make_async_copy(src, dst, load_sem.at[i]) for i, (src, dst) in enumerate(pairs)]
    for load in loads:
        load.start()

    channels = vr_ref.shape[1]
    chan = (lax.broadcasted_iota(jnp.int32, (8, channels), 1) + me_f * channels).astype(F32)

    def subgrid(i):
        return peer(i // own + 1, 1) * own + i % own

    def prepare(i, tabs):
        tables(subgrid(i), chan, vr_ref, vi_ref, co_ref, *tabs)

    def spot_copy(t):
        return base_copy(spot_ref.at[pl.ds(peer(t, 1), 1)], table.at[pl.ds(me_b, 1)], spot_s.at[t - 1], spot_r.at[t - 1], t)

    def share_copy(t):
        return base_copy(send.at[t], recv.at[t], base_s.at[t], base_r.at[t], t + 1)

    prepare(0, even)
    lane = lax.broadcasted_iota(jnp.int32, (1, 128), 1)

    def choose(o):
        seen = jnp.int32(0)
        index = [jnp.int32(0)] * FCAP
        for s in range(own):
            hit = (owner_ref[0, s] == o).astype(jnp.int32)
            index = [index[r] + hit * (seen == r).astype(jnp.int32) * s for r in range(FCAP)]
            seen = seen + hit
        choice[o] = index[0] * (1 - core) + index[1] * core
        spot = jnp.zeros((1, 128), jnp.int32)
        for r in range(FCAP):
            fields = ((seen > r).astype(jnp.int32), row_ref[0, index[r]], col_ref[0, index[r]])
            for n, value in enumerate(fields):
                spot = jnp.where(lane == 3 * r + n, value, spot)
        spot_ref[pl.ds(o, 1), :] = spot

    def small_work():
        for load in loads:
            load.wait()
        c, s = screen(w_ref[0, me_f])
        cs[0] = c
        cs[1] = s
        each(0, nb, choose)
        table[pl.ds(me_b, 1), :] = spot_ref[pl.ds(me_b, 1), :]

    def group(t):
        def two(u):
            i = t * own + 2 * u
            prepare(i + 1, odd)
            send[t, 2 * u] = products(*even).astype(BF16)
            prepare(i + 2, even)
            send[t, 2 * u + 1] = products(*odd).astype(BF16)

        for u in range(own // 2):
            two(u)

        @pl.when(t == 0)
        def _():
            pl.semaphore_wait(barrier, nb + nf - 2)

        @pl.when(t < nb - 1)
        def _():
            share_copy(t).start()

        @pl.when(t == 0)
        def _():
            small_work()
            each(1, nb, lambda t: spot_copy(t).start())

    each(0, nb, group)
    each(0, nb - 1, lambda t: share_copy(t).wait_recv())

    def sum_shares(j):
        m = send[nb - 1, j].astype(F32)
        for t in range(nb - 1):
            m = m + recv[t, j].astype(F32)
        return m

    def sum_copy(d):
        return freq_copy(total.at[(me_f + d) % nf], fsum.at[d - 1], freq_s.at[d - 1], freq_r.at[d - 1], d)

    def reduce(d):
        j = (me_f + d) % nf
        total[j] = sum_shares(j)
        sum_copy(d).start()

    for d in range(1, nf):
        reduce(d)
    m = sum_shares(me_f)
    each(1, nf, lambda d: sum_copy(d).wait_recv())
    for d in range(1, nf):
        m = m + fsum[d - 1]
    gath[me_f] = make_patch(m, cs[0], cs[1], left1[...], right1[...], left2[...], right2[...])

    chips = nf // 2
    turn = 1 - 2 * core + nf

    def gath_copy(d):
        return freq_copy(gath.at[me_f], gath.at[me_f], gath_s.at[d - 1], gath_r.at[d - 1], 2 * d)

    def hand_copy(d):
        piece = gath.at[(me_f + nf - 2 * d) % nf]
        return freq_copy(piece, piece, hand_s.at[d], hand_r.at[d], turn)

    def hand_on(d):
        gath_copy(d).wait_recv()
        hand_copy(d).start()

    each(1, chips, lambda d: gath_copy(d).start())
    hand_copy(0).start()
    each(1, chips, hand_on)
    each(0, chips, lambda d: hand_copy(d).wait_recv())

    def out_copy(t):
        return base_copy(outb.at[peer(t, 1)], slots.at[core, me_b], out_s.at[t - 1], out_r.at[t - 1], t)

    def pick(o):
        return gath[choice[o]]

    def ship(t):
        o = peer(t, 1)
        outb[o] = pick(o)
        out_copy(t).start()

    for t in range(1, nb):
        ship(t)
    slots[core, me_b] = pick(me_b)

    def pair_copy(t):
        source = peer(t, -1)
        part = slots.at[core, source]
        return pltpu.make_async_remote_copy(
            src_ref=part,
            dst_ref=part,
            send_sem=pair_s.at[t],
            recv_sem=pair_r.at[t],
            device_id={"freq": me_f + 1 - 2 * core},
            device_id_type=MESH,
        )

    pair_copy(0).start()

    def forward(t):
        out_copy(t).wait_recv()
        pair_copy(t).start()

    each(1, nb, forward)
    each(0, nb, lambda t: pair_copy(t).wait())
    each(1, nb, lambda t: out_copy(t).wait_send())
    each(1, chips, lambda d: gath_copy(d).wait_send())
    each(0, chips, lambda d: hand_copy(d).wait_send())
    each(1, nf, lambda d: sum_copy(d).wait_send())
    each(0, nb - 1, lambda t: share_copy(t).wait_send())
    each(1, nb, lambda t: spot_copy(t).wait())


def main(owner, row, col, w, vr, vi, co, nb, nf):
    own = w.shape[1]
    unit = (G, 2 * G)
    dma = pltpu.SemaphoreType.DMA
    consts = [stay(jnp.asarray(x)) for x in constants()]
    tabs = [pltpu.VMEM((2 * HALF, 128), F32), pltpu.VMEM((2 * HALF, 128), F32), pltpu.VMEM((16, 256), F32)]
    return pl.pallas_call(
        functools.partial(main_kernel, nb, nf),
        out_shape=(
            jax.ShapeDtypeStruct((FCAP, nb) + unit, F32),
            jax.ShapeDtypeStruct((nb, 128), jnp.int32),
        ),
        in_specs=[hbm()] * 8 + [vmem()] * 3,
        out_specs=(vmem(), vmem()),
        scratch_shapes=[
            pltpu.SMEM((1, own), jnp.int32),
            pltpu.SMEM((1, own), jnp.int32),
            pltpu.SMEM((1, own), jnp.int32),
            pltpu.SMEM((1, own), F32),
        ]
        + [pltpu.VMEM(x.shape, BF16) for x in consts]
        + [pltpu.VMEM((nb, 128), jnp.int32)]
        + tabs * 2
        + [
            pltpu.VMEM((2,) + unit, F32),
            pltpu.VMEM((nb, own) + unit, BF16),
            pltpu.VMEM((nb - 1, own) + unit, BF16),
            pltpu.VMEM((own,) + unit, F32),
            pltpu.VMEM((nf - 1,) + unit, F32),
            pltpu.VMEM((nf,) + unit, F32),
            pltpu.VMEM((nb,) + unit, F32),
            pltpu.SMEM((nb,), jnp.int32),
            dma((8,)),
            dma((nb - 1,)),
            dma((nb - 1,)),
            dma((nb - 1,)),
            dma((nb - 1,)),
            dma((nf - 1,)),
            dma((nf - 1,)),
            dma((nf // 2 - 1,)),
            dma((nf // 2 - 1,)),
            dma((nf // 2,)),
            dma((nf // 2,)),
            dma((nb - 1,)),
            dma((nb - 1,)),
            dma((nb,)),
            dma((nb,)),
        ],
        compiler_params=pltpu.CompilerParams(
            vmem_limit_bytes=48 << 20, collective_id=0, has_side_effects=True
        ),
        name="main",
    )(owner, row, col, w, *consts, vr, vi, co)


def deposit_kernel(table_ref, slot_ref, grid_in, grid_ref, zeros, blocks, where_ref, tile_ref, count_ref, sem, zsem):
    del grid_in
    zeros[...] = jnp.zeros(zeros.shape, F32)
    clears = [clear_copy(zeros, grid_ref, zsem, i, EARLY) for i in range(EARLY, PIECES)]
    for clear in clears:
        clear.start()
    tiles = GY // 128

    def reset(i, carry):
        where_ref[i] = -1
        return carry

    lax.fori_loop(0, tiles, reset, 0)
    count_ref[0] = 0
    lane = lax.broadcasted_iota(jnp.int32, (G + 8, 128), 1)

    def block_of(tile):
        @pl.when(where_ref[tile] < 0)
        def _():
            count = count_ref[0]
            where_ref[tile] = count
            tile_ref[count] = tile
            count_ref[0] = count + 1
            blocks[count] = jnp.zeros(blocks.shape[1:], F32)

        return where_ref[tile]

    def place(b, rank):
        row = table_ref[b, 3 * rank + 1]
        r = pl.ds(pl.multiple_of(row // 8 * 8, 8), G + 8)
        col = table_ref[b, 3 * rank + 2]
        tile = col // 128
        c = col % 128
        patch = jnp.concatenate([slot_ref[rank, b], jnp.zeros((8, 2 * G), F32)], axis=0)
        patch = pltpu.roll(patch, row % 8, 0)
        real = pltpu.roll(jnp.where(lane < G, patch, 0.0), c, 1)
        imag = pltpu.roll(jnp.where(lane < G, 0.0, patch), c + G, 1)
        first = block_of(tile)
        blocks[first, 0, r, :] += jnp.where(lane >= c, real, 0.0)
        blocks[first, 1, r, :] += jnp.where(lane >= c, imag, 0.0)

        @pl.when(c > 128 - G)
        def _():
            second = block_of(tile + 1)
            blocks[second, 0, r, :] += jnp.where(lane < c, real, 0.0)
            blocks[second, 1, r, :] += jnp.where(lane < c, imag, 0.0)

    def source(b, carry):
        for rank in range(FCAP):

            @pl.when(table_ref[b, 3 * rank] > 0)
            def _():
                place(b, rank)

        return carry

    lax.fori_loop(0, table_ref.shape[0], source, 0)
    count = count_ref[0]

    def copy(i):
        cut = pl.ds(pl.multiple_of(tile_ref[i] * 128, 128), 128)
        return pltpu.make_async_copy(blocks.at[i, :, 0:FR, :], grid_ref.at[:, :, cut], sem.at[i])

    def start(i, carry):
        copy(i).start()
        return carry

    def wait(i, carry):
        copy(i).wait()
        return carry

    for clear in clears:
        clear.wait()
    lax.fori_loop(0, count, start, 0)
    lax.fori_loop(0, count, wait, 0)


def deposit(table, slots, grid):
    most = 2 * slots.shape[0] * slots.shape[1]
    return pl.pallas_call(
        deposit_kernel,
        out_shape=jax.ShapeDtypeStruct((2, FR, GY), F32),
        in_specs=[smem(), vmem(), hbm()],
        out_specs=hbm(),
        scratch_shapes=[
            pltpu.VMEM((FR, CLEAR), F32),
            pltpu.VMEM((most, 2, FR + 8, 128), F32),
            pltpu.SMEM((GY // 128,), jnp.int32),
            pltpu.SMEM((most,), jnp.int32),
            pltpu.SMEM((1,), jnp.int32),
            pltpu.SemaphoreType.DMA((most,)),
            pltpu.SemaphoreType.DMA((PIECES - EARLY,)),
        ],
        input_output_aliases={2: 0},
        compiler_params=pltpu.CompilerParams(vmem_limit_bytes=48 << 20),
        name="deposit",
    )(table, slots, grid)


def per_device(visibilities, anchor, drift, target, subgrid_w, facet_owner, row_offset, col_offset):
    nb, nf = lax.axis_size("base"), lax.axis_size("freq")
    target = target.reshape(1, -1)
    vr, vi, co, grid = prep(*[stay(x) for x in (target, visibilities, anchor, drift)])
    small = [stay(x.reshape(1, -1)) for x in (facet_owner, row_offset, col_offset, subgrid_w)]
    slots, table = main(*small, vr, vi, co, nb, nf)
    return deposit(table, slots, grid)


def solution(mesh):
    return jax.shard_map(
        per_device,
        mesh=mesh,
        in_specs=(
            P(None, "base", "freq"),
            P(None, "base"),
            P(None, "base"),
            P("base", None),
            P("base"),
            P("base", None),
            P("base"),
            P("base"),
        ),
        out_specs=P(None, "base", None),
        check_vma=False,
    )
```
